32 devices in a mesh: dp: 8 (over y, x, core), fsdp: 4 (over z).
Axes of the slice: x: 2, y: 2, z: 4, core: 2. Of those that a mesh axis runs over, the one named last changes fastest.
Arguments:
- patches: bfloat16 [8192, 1152], P(('dp', 'fsdp')), may hold values from -6 to 6
- conditions: bfloat16 [128, 1152], P(('dp', 'fsdp')), may hold values from -6 to 6
- segment_ids: int32 [8192], P(('dp', 'fsdp')), may hold values from 0 to 3, as said below
- grid_coords: int32 [2, 8192], P(None, ('dp', 'fsdp')), may hold values from 0 to 15, as said below
- mod_weight: bfloat16 [1152, 6912], P('dp', 'fsdp'), may hold values from -0.1875 to 0.1875
- mod_bias: bfloat16 [6912], P('fsdp'), may hold values from -3 to 3
- qkv_weight: bfloat16 [1152, 3456], P('dp', 'fsdp'), may hold values from -0.1875 to 0.1875
- qkv_bias: bfloat16 [3456], P('fsdp'), may hold values from -3 to 3
- qk_gains: bfloat16 [2, 72], P(None, 'fsdp'), may hold values from 0.25 to 1.75
- proj_weight: bfloat16 [1152, 1152], P('dp', 'fsdp'), may hold values from -2 to 2
- proj_bias: bfloat16 [1152], P('fsdp'), may hold values from -3 to 3
- up_weight: bfloat16 [1152, 6144], P('dp', 'fsdp'), may hold values from -0.1875 to 0.1875
- up_bias: bfloat16 [6144], P('fsdp'), may hold values from -3 to 3
- down_weight: bfloat16 [3072, 1152], P('dp', 'fsdp'), may hold values from -0.109375 to 0.109375
- down_bias: bfloat16 [1152], P('fsdp'), may hold values from -3 to 3
- out_cotangent: bfloat16 [8192, 1152], P(('dp', 'fsdp')), may hold values from -6 to 6
Outputs:
- block_out: bfloat16 [8192, 1152], P(('dp', 'fsdp'))
- patch_grad: bfloat16 [8192, 1152], P(('dp', 'fsdp'))
- cond_grad: bfloat16 [128, 1152], P(('dp', 'fsdp'))
- mod_weight_grad: float32 [1152, 6912], P('dp', 'fsdp')
- mod_bias_grad: float32 [6912], P('fsdp')
- qkv_weight_grad: float32 [1152, 3456], P('dp', 'fsdp')
- qkv_bias_grad: float32 [3456], P('fsdp')
- qk_gains_grad: float32 [2, 72], P(None, 'fsdp')
- proj_weight_grad: float32 [1152, 1152], P('dp', 'fsdp')
- proj_bias_grad: float32 [1152], P('fsdp')
- up_weight_grad: float32 [1152, 6144], P('dp', 'fsdp')
- up_bias_grad: float32 [6144], P('fsdp')
- down_weight_grad: float32 [3072, 1152], P('dp', 'fsdp')
- down_bias_grad: float32 [1152], P('fsdp')
The draws below stay inside these ranges and needn't reach their ends.
Inputs may be any that keep to these rules, and one draw needn't show every extreme that they name: `segment_ids`: the 256 rows r with the same r // 256 hold either one image (all ids 0) or four images of 64 rows in order with ids 0, 1, 2, 3; both kinds occur in every draw. `grid_coords`: row and column of each patch on its image's grid in row-major order: 16 x 16 for an image of 256 rows, 8 on each side for one of 64 rows.
All inputs are finite; a program needn't handle non-finite values.
Results may differ from the reference program's by a relative error of at most 0.017.
Values may be sent and summed in bfloat16 or wider, within the bound.
A program may use at most 256 MiB of HBM per device.

```python
import jax
import jax.numpy as jnp
from jax import lax

D = 1152
HEADS = 16
HEAD = 72
FF = 3072
SIDE = 16
SLOTS = 4
TOK_DEV = 256
TOKENS = 8192
ITEMS = 128


def patch_layout(key):
    device_count = TOKENS // TOK_DEV
    layouts = jax.random.randint(jax.random.fold_in(key, 11), (device_count,), 0, 2)
    layouts = layouts.at[0].set(1).at[1].set(0)
    position = jnp.arange(TOK_DEV, dtype=jnp.int32)
    small_rows = TOK_DEV // 4
    small_side = SIDE // 2
    local_pos = position % small_rows
    small_ids = position // small_rows
    single = layouts[:, None] == 1
    item_ids = jnp.where(single, jnp.zeros_like(small_ids)[None, :], small_ids[None, :])
    row_grid = jnp.where(single, (position // SIDE)[None, :], (local_pos // small_side)[None, :])
    col_grid = jnp.where(single, (position % SIDE)[None, :], (local_pos % small_side)[None, :])
    coords = jnp.stack([row_grid.reshape(TOKENS), col_grid.reshape(TOKENS)])
    return (item_ids.reshape(TOKENS).astype(jnp.int32), coords.astype(jnp.int32))


def draw_segment_ids(key, part):
    return patch_layout(key)[0]


def draw_grid_coords(key, part):
    return patch_layout(key)[1]


def steps_of(rng, dims, split, least, top_value):
    factor_of = 1.0
    for dim, parts in split:
        steps = jax.random.uniform(jax.random.fold_in(jax.random.fold_in(rng, 6), dim), (parts,), jnp.float32, least / len(split), top_value / len(split))
        factor_of = factor_of * jnp.repeat(jnp.exp(steps), dims[dim] // parts).reshape((-1,) + (1,) * (len(dims) - 1 - dim))
    return factor_of


def centred(key, extent, spread, reach, shards=(), held_as=jnp.bfloat16):
    values = spread * jax.random.normal(key, extent, jnp.float32)
    if shards:
        values = values * steps_of(key, extent, shards, -0.22, 0.18)
    return jnp.clip(values, -reach, reach).astype(held_as)


def setup_inputs(seed: int = 0) -> dict:
    key_of = jax.random.split(jax.random.key(seed), 17)
    return {
        "patches": centred(key_of[0], (TOKENS, D), 1.0, 6.0, ((0, 32),)),
        "conditions": centred(key_of[1], (ITEMS, D), 1.0, 6.0, ((0, 32),)),
        "segment_ids": draw_segment_ids(jax.random.fold_in(key_of[16], 71), 0),
        "grid_coords": draw_grid_coords(jax.random.fold_in(key_of[16], 71), 0),
        "mod_weight": centred(key_of[4], (D, 6 * D), D ** -0.5, 0.1875, ((0, 8), (1, 4))),
        "mod_bias": centred(key_of[5], (6 * D,), 0.5, 3.0, ((0, 4),)),
        "qkv_weight": centred(key_of[6], (D, 3 * D), D ** -0.5, 0.1875, ((0, 8), (1, 4))),
        "qkv_bias": centred(key_of[7], (3 * D,), 0.5, 3.0, ((0, 4),)),
        "qk_gains": jnp.clip(1.0 + 0.15 * jax.random.normal(key_of[8], (2, HEAD), jnp.float32), 0.25, 1.75).astype(jnp.bfloat16),
        "proj_weight": centred(key_of[9], (D, D), (max(D // 128, 4)) ** -0.5, 2.0, ((0, 8), (1, 4))),
        "proj_bias": centred(key_of[10], (D,), 0.5, 3.0, ((0, 4),)),
        "up_weight": centred(key_of[11], (D, 2 * FF), D ** -0.5, 0.1875, ((0, 8), (1, 4))),
        "up_bias": centred(key_of[12], (2 * FF,), 0.5, 3.0, ((0, 4),)),
        "down_weight": centred(key_of[13], (FF, D), FF ** -0.5, 0.109375, ((0, 8), (1, 4))),
        "down_bias": centred(key_of[14], (D,), 0.5, 3.0, ((0, 4),)),
        "out_cotangent": centred(key_of[15], (TOKENS, D), 1.0, 6.0, ((0, 32),)),
    }


epsilon = 1e-06
highest = lax.Precision.HIGHEST

@jax.custom_vjp
def low(v):
    return lax.optimization_barrier(v.astype(jnp.bfloat16)).astype(jnp.float32)

@jax.custom_vjp
def low_back(v):
    return v

def low_keep(v):
    return (low(v), None)

def low_pass(kept, grad):
    return (grad,)

def back_keep(v):
    return (v, None)

def back_low(kept, grad):
    return (low(grad),)
low.defvjp(low_keep, low_pass)
low_back.defvjp(back_keep, back_low)

def matmul(left, right):
    return jnp.dot(left, right, precision=highest, preferred_element_type=jnp.float32)

def rms_scale(values):
    return lax.rsqrt(lax.optimization_barrier(jnp.mean(values * values, axis=-1, keepdims=True)) + epsilon)

def rotary_tables(coord_rows, quarter):
    frequencies = 10000.0 ** (-jnp.arange(quarter, dtype=jnp.float32) / quarter)
    row_angle = coord_rows[0].astype(jnp.float32)[:, None, None] * frequencies
    col_angle = coord_rows[1].astype(jnp.float32)[:, None, None] * frequencies
    return (jnp.cos(row_angle), jnp.sin(row_angle), jnp.cos(col_angle), jnp.sin(col_angle))

def rotate(values, tables, direction):
    half_size = values.shape[-1] // 2
    quarter = half_size // 2
    pieces_out = []
    for which_half in range(2):
        cosine = tables[2 * which_half]
        sine_tab = direction * tables[2 * which_half + 1]
        start_col = which_half * half_size
        first_part = values[..., start_col:start_col + quarter]
        second = values[..., start_col + quarter:start_col + half_size]
        pieces_out.append(first_part * cosine - second * sine_tab)
        pieces_out.append(second * cosine + first_part * sine_tab)
    return jnp.concatenate(pieces_out, axis=-1)

def attend_device(inputs):
    queries, key_rows, value_rows, seg_rows = inputs
    scores = low_back(jnp.einsum('qhd,khd->hqk', queries, key_rows, precision=highest) * HEAD ** (-0.5))
    same_item = seg_rows[:, None] == seg_rows[None, :]
    scores = jnp.where(same_item[None], scores, -1e+30)
    row_max = lax.optimization_barrier(jnp.max(scores, axis=-1, keepdims=True))
    exponentials = jnp.exp(scores - row_max)
    denominator = lax.optimization_barrier(jnp.sum(exponentials, axis=-1, keepdims=True))
    probs = low(exponentials / denominator)
    return jnp.einsum('hqk,khd->qhd', probs, value_rows, precision=highest)

def reference(patches, conditions, segment_ids, grid_coords, mod_weight, mod_bias, qkv_weight, qkv_bias, qk_gains, proj_weight, proj_bias, up_weight, up_bias, down_weight, down_bias, out_cotangent):
    device_count = TOKENS // TOK_DEV
    groups = device_count // 4
    group_rows = 4 * TOK_DEV
    seg_groups = segment_ids.reshape(groups, group_rows)
    coord_groups = grid_coords.reshape(2, groups, group_rows).transpose(1, 0, 2)
    floats = [array.astype(jnp.float32) for array in (patches, conditions, mod_weight, mod_bias, qkv_weight, qkv_bias, qk_gains, proj_weight, proj_bias, up_weight, up_bias, down_weight, down_bias)]

    def forward(patch_all, cond_all, mod_weight, mod_bias, qkv_weight, qkv_bias, qk_gains, proj_weight, proj_bias, up_weight, up_bias, down_weight, down_bias):
        silu_cond = low(jax.nn.silu(cond_all))
        modulation = low_back(matmul(silu_cond, mod_weight) + mod_bias)

        def block_rows(inputs):
            patch_rows, mod_rows, seg_rows, coord_rows = inputs
            group_size = patch_rows.shape[0]
            item_rows = jnp.arange(group_size, dtype=jnp.int32) // TOK_DEV * SLOTS + seg_rows
            per_token = mod_rows[item_rows]
            shift_attn = per_token[:, 0:D]
            scale_attn = per_token[:, D:2 * D]
            gate_attn = per_token[:, 2 * D:3 * D]
            shift_ffn = per_token[:, 3 * D:4 * D]
            scale_ffn = per_token[:, 4 * D:5 * D]
            gate_ffn = per_token[:, 5 * D:6 * D]
            normed_one = patch_rows * rms_scale(patch_rows)
            hidden_one = low(normed_one * (1.0 + scale_attn) + shift_attn)
            qkv_rows = low_back(matmul(hidden_one, qkv_weight) + qkv_bias)
            tables = rotary_tables(coord_rows, HEAD // 4)
            query_raw = qkv_rows[:, 0:D].reshape(group_size, HEADS, HEAD)
            key_raw = qkv_rows[:, D:2 * D].reshape(group_size, HEADS, HEAD)
            queries = low(rotate(query_raw * rms_scale(query_raw) * qk_gains[0], tables, 1.0))
            key_rows = low(rotate(key_raw * rms_scale(key_raw) * qk_gains[1], tables, 1.0))
            value_rows = low(qkv_rows[:, 2 * D:3 * D].reshape(group_size, HEADS, HEAD))
            device_shape = (group_size // TOK_DEV, TOK_DEV, HEADS, HEAD)
            attended = lax.map(jax.checkpoint(attend_device), (queries.reshape(device_shape), key_rows.reshape(device_shape), value_rows.reshape(device_shape), seg_rows.reshape(group_size // TOK_DEV, TOK_DEV)))
            attended = low_back(low(attended.reshape(group_size, D)))
            branch_attn = low_back(matmul(attended, proj_weight) + proj_bias)
            middle = patch_rows + gate_attn * branch_attn
            normed_two = middle * rms_scale(middle)
            hidden_two = low(normed_two * (1.0 + scale_ffn) + shift_ffn)
            gate_up = low_back(matmul(hidden_two, up_weight) + up_bias)
            gated = low(jax.nn.silu(gate_up[:, :FF]) * gate_up[:, FF:])
            branch_ffn = low_back(matmul(gated, down_weight) + down_bias)
            return middle + gate_ffn * branch_ffn
        outputs = lax.map(jax.checkpoint(block_rows), (patch_all.reshape(groups, group_rows, D), modulation.reshape(groups, 4 * SLOTS, 6 * D), seg_groups, coord_groups))
        return outputs.reshape(TOKENS, D)
    result, pullback = jax.vjp(forward, *floats)
    gradients = pullback(out_cotangent.astype(jnp.float32))
    return (result.astype(jnp.bfloat16), gradients[0].astype(jnp.bfloat16), gradients[1].astype(jnp.bfloat16), gradients[2], gradients[3], gradients[4], gradients[5], gradients[6], gradients[7], gradients[8], gradients[9], gradients[10], gradients[11], gradients[12])
```

```python
import jax
import jax.numpy as jnp
from jax import lax
from jax.sharding import PartitionSpec as P

HEADS = 16
SPAN = 64

epsilon = 1e-06
low = jnp.bfloat16
full = jnp.float32


def rms_scale(values):
    return lax.rsqrt(jnp.mean(values * values, axis=-1, keepdims=True) + epsilon)


def norm_backward(grad_normed, normed, factor):
    return factor * (grad_normed - normed * jnp.mean(grad_normed * normed, axis=-1, keepdims=True))


def rotary_tables(coord_rows, quarter):
    frequencies = 10000.0 ** (-jnp.arange(quarter, dtype=full) / quarter)
    row_angle = coord_rows[0].astype(full)[:, None, None] * frequencies
    col_angle = coord_rows[1].astype(full)[:, None, None] * frequencies
    return (jnp.cos(row_angle), jnp.sin(row_angle), jnp.cos(col_angle), jnp.sin(col_angle))


def rotate(values, tables, direction):
    half_size = values.shape[-1] // 2
    quarter = half_size // 2
    pieces_out = []
    for which_half in range(2):
        cosine = tables[2 * which_half]
        sine_tab = direction * tables[2 * which_half + 1]
        start_col = which_half * half_size
        first_part = values[..., start_col : start_col + quarter]
        second = values[..., start_col + quarter : start_col + half_size]
        pieces_out.append(first_part * cosine - second * sine_tab)
        pieces_out.append(second * cosine + first_part * sine_tab)
    return jnp.concatenate(pieces_out, axis=-1)


def dot(left, right):
    return jnp.dot(left, right, preferred_element_type=full)


def dot_t(left, right):
    return lax.dot_general(left, right, (((1,), (1,)), ((), ())), preferred_element_type=full)


def outer_grad(left, right):
    return lax.dot_general(left, right, (((0,), (0,)), ((), ())), preferred_element_type=full)


def silu_slope(values):
    sigmoid_gate = jax.nn.sigmoid(values)
    return sigmoid_gate * (1.0 + values * (1.0 - sigmoid_gate))


def swap(values, axis, size, bit):
    return lax.ppermute(values, axis, [(k, k ^ bit) for k in range(size)])


def bits_of(size):
    return [1 << b for b in range(size.bit_length() - 1)]


def gather_small(values, axis, size):
    index = lax.axis_index(axis)
    for bit in bits_of(size):
        other = swap(values, axis, size, bit)
        upper = (index & bit) != 0
        values = jnp.concatenate(
            [jnp.where(upper, other, values), jnp.where(upper, values, other)], axis=0
        )
    return values


def scatter_sum_small(values, axis, size):
    index = lax.axis_index(axis)
    for bit in reversed(bits_of(size)):
        half = values.shape[0] // 2
        upper = (index & bit) != 0
        first, second = values[:half], values[half:]
        values = jnp.where(upper, second, first) + swap(
            jnp.where(upper, first, second), axis, size, bit
        )
    return values


def sum_small(values, axis, size):
    for bit in bits_of(size):
        values = values + swap(values, axis, size, bit)
    return values


def xor_order(values, index, size):
    tail = values.shape[1:]
    for bit in bits_of(size):
        paired = values.reshape((size // (2 * bit), 2, bit) + tail)
        values = jnp.where((index & bit) != 0, jnp.flip(paired, axis=1), paired)
        values = values.reshape((size,) + tail)
    return values


def exchange_small(values, axis, size):
    index = lax.axis_index(axis)
    tail = values.shape[1:]
    values = xor_order(values, index, size)
    for bit in bits_of(size):
        paired = values.reshape((size // (2 * bit), 2, bit) + tail)
        moved = swap(paired[:, 1], axis, size, bit)
        values = jnp.stack([paired[:, 0], moved], axis=1).reshape((size,) + tail)
    return xor_order(values, index, size)


def gather_weight(weight, dp_size, fsdp_size):
    rows, cols = weight.shape
    whole = lax.all_gather(weight, ("dp", "fsdp"), axis=0, tiled=False)
    whole = whole.reshape(dp_size, fsdp_size, rows, cols).transpose(1, 0, 2, 3)
    return whole.reshape(fsdp_size, dp_size * rows, cols)


def scatter_grad(blocks, dp_size):
    rows, cols = blocks[0].shape
    parts = jnp.stack([b.reshape(dp_size, rows // dp_size, cols) for b in blocks], axis=1)
    parts = lax.psum_scatter(parts, "dp", scatter_dimension=0, tiled=False)
    return lax.psum_scatter(parts, "fsdp", scatter_dimension=0, tiled=False).astype(full)


def masked_scores(query_low, key_low, same_item, score_scale):
    scores = jnp.einsum("qhd,khd->hqk", query_low, key_low, preferred_element_type=full)
    return jnp.where(same_item, scores * score_scale, -1e30)


def make_per_device(dp_size, fsdp_size):
    def per_device(
        patches,
        conditions,
        segment_ids,
        grid_coords,
        mod_weight,
        mod_bias,
        qkv_weight,
        qkv_bias,
        qk_gains,
        proj_weight,
        proj_bias,
        up_weight,
        up_bias,
        down_weight,
        down_bias,
        out_cotangent,
    ):
        row_count, model_width = patches.shape
        slots = conditions.shape[0]
        spans = row_count // SPAN
        head_size = model_width // HEADS
        score_scale = head_size ** (-0.5)
        head_shape = (row_count, HEADS, head_size)
        dp_index = lax.axis_index("dp")
        mod_rows, mod_cols = mod_weight.shape

        qkv_full = gather_weight(qkv_weight, dp_size, fsdp_size)
        proj_full = gather_weight(proj_weight, dp_size, fsdp_size)
        up_full = gather_weight(up_weight, dp_size, fsdp_size)
        down_full = gather_weight(down_weight, dp_size, fsdp_size)

        gain_cols = qk_gains.shape[1]
        sizes = [qkv_bias.shape[0], proj_bias.shape[0], up_bias.shape[0], down_bias.shape[0]]
        vector = jnp.concatenate(
            [qkv_bias, proj_bias, up_bias, down_bias, qk_gains[0], qk_gains[1]]
        )
        vectors = gather_small(vector[None], "fsdp", fsdp_size).astype(full)
        bounds = [0]
        for size in sizes + [gain_cols, gain_cols]:
            bounds.append(bounds[-1] + size)
        pieces = [vectors[:, bounds[k] : bounds[k + 1]] for k in range(6)]
        qkv_vector, proj_vector, up_vector, down_vector, gain_q, gain_k = [
            p.reshape(-1) for p in pieces
        ]

        cond_full = conditions.astype(full)
        silu_low = jax.nn.silu(cond_full).astype(low)
        silu_all = gather_small(
            gather_small(silu_low[None], "fsdp", fsdp_size)[None], "dp", dp_size
        ).reshape(dp_size * fsdp_size * slots, model_width)
        silu_cols = lax.dynamic_slice_in_dim(silu_all, dp_index * mod_rows, mod_rows, axis=1)
        mod_part = dot(silu_cols, mod_weight).reshape(dp_size, fsdp_size, slots, mod_cols)
        mod_sum = scatter_sum_small(mod_part, "dp", dp_size)[0] + mod_bias.astype(full)
        modulation = exchange_small(mod_sum, "fsdp", fsdp_size)
        modulation = modulation.transpose(1, 0, 2).reshape(slots, fsdp_size * mod_cols)
        span_ids = segment_ids.reshape(spans, SPAN)[:, 0]
        span_hot = (span_ids[:, None] == jnp.arange(slots, dtype=jnp.int32)[None, :]).astype(full)
        span_mod = jnp.sum(span_hot[:, :, None] * modulation[None], axis=1)

        def per_row(k):
            part = span_mod[:, k * model_width : (k + 1) * model_width]
            return jnp.broadcast_to(part[:, None, :], (spans, SPAN, model_width)).reshape(
                row_count, model_width
            )

        shift_attn, scale_attn, gate_attn, shift_ffn, scale_ffn, gate_ffn = map(per_row, range(6))

        def cols_of(blocks):
            return jnp.concatenate(blocks, axis=1)

        def forward_dot(rows_low, weight_full):
            return cols_of([dot(rows_low, weight_full[j]) for j in range(fsdp_size)])

        def split(values):
            width = values.shape[1] // fsdp_size
            return [values[:, j * width : (j + 1) * width] for j in range(fsdp_size)]

        def backward_dot(grad_low, weight_full):
            parts = split(grad_low)
            total = dot_t(parts[0], weight_full[0])
            for j in range(1, fsdp_size):
                total = total + dot_t(parts[j], weight_full[j])
            return total

        def weight_grad(rows_low, grad_low):
            return scatter_grad(
                [outer_grad(rows_low, part).astype(low) for part in split(grad_low)], dp_size
            )

        tables = rotary_tables(grid_coords, head_size // 4)
        patch_full = patches.astype(full)
        scale_one = rms_scale(patch_full)
        normed_one = patch_full * scale_one
        hidden_one = (normed_one * (1.0 + scale_attn) + shift_attn).astype(low)
        qkv_rows = forward_dot(hidden_one, qkv_full) + qkv_vector
        query_raw = qkv_rows[:, 0:model_width].reshape(head_shape)
        key_raw = qkv_rows[:, model_width : 2 * model_width].reshape(head_shape)
        value_low = qkv_rows[:, 2 * model_width :].reshape(head_shape).astype(low)
        query_scale = rms_scale(query_raw)
        query_unit = query_raw * query_scale
        key_scale = rms_scale(key_raw)
        key_unit = key_raw * key_scale
        query_low = rotate(query_unit * gain_q, tables, 1.0).astype(low)
        key_low = rotate(key_unit * gain_k, tables, 1.0).astype(low)
        same_item = (segment_ids[:, None] == segment_ids[None, :])[None]
        scores = masked_scores(query_low, key_low, same_item, score_scale)
        exponentials = jnp.exp(scores - jnp.max(scores, axis=-1, keepdims=True))
        probs = exponentials / jnp.sum(exponentials, axis=-1, keepdims=True)
        probs_low = probs.astype(low)
        attended_low = (
            jnp.einsum("hqk,khd->qhd", probs_low, value_low, preferred_element_type=full)
            .reshape(row_count, model_width)
            .astype(low)
        )
        branch_attn = forward_dot(attended_low, proj_full) + proj_vector
        middle = patch_full + gate_attn * branch_attn
        scale_two = rms_scale(middle)
        normed_two = middle * scale_two
        hidden_two = (normed_two * (1.0 + scale_ffn) + shift_ffn).astype(low)
        gate_up = forward_dot(hidden_two, up_full) + up_vector
        hidden_units = gate_up.shape[1] // 2
        gate_part = gate_up[:, :hidden_units]
        up_part = gate_up[:, hidden_units:]
        gated_low = (jax.nn.silu(gate_part) * up_part).astype(low)
        branch_ffn = forward_dot(gated_low, down_full) + down_vector
        block_out = (middle + gate_ffn * branch_ffn).astype(low)

        grad_out = out_cotangent.astype(full)
        grad_gate_ffn = grad_out * branch_ffn
        grad_branch_ffn = (grad_out * gate_ffn).astype(low)
        down_bias_grad = jnp.sum(grad_branch_ffn.astype(full), axis=0)
        grad_gated = backward_dot(grad_branch_ffn, down_full)
        down_grad = weight_grad(gated_low, grad_branch_ffn)
        grad_gate_up = jnp.concatenate(
            [grad_gated * up_part * silu_slope(gate_part), grad_gated * jax.nn.silu(gate_part)],
            axis=1,
        ).astype(low)
        up_bias_grad = jnp.sum(grad_gate_up.astype(full), axis=0)
        grad_hidden_two = backward_dot(grad_gate_up, up_full)
        up_grad = weight_grad(hidden_two, grad_gate_up)
        grad_middle = grad_out + norm_backward(
            grad_hidden_two * (1.0 + scale_ffn), normed_two, scale_two
        )
        grad_gate_attn = grad_middle * branch_attn
        grad_branch_attn = (grad_middle * gate_attn).astype(low)
        proj_bias_grad = jnp.sum(grad_branch_attn.astype(full), axis=0)
        grad_attended = backward_dot(grad_branch_attn, proj_full).astype(low).reshape(head_shape)
        proj_grad = weight_grad(attended_low, grad_branch_attn)
        grad_probs = jnp.einsum(
            "qhd,khd->hqk", grad_attended, value_low, preferred_element_type=full
        )
        row_dot = jnp.sum(probs * grad_probs, axis=-1, keepdims=True)
        grad_scores = (probs * (grad_probs - row_dot)).astype(low)
        grad_values = jnp.einsum(
            "hqk,qhd->khd", probs_low, grad_attended, preferred_element_type=full
        )
        grad_query_rot = score_scale * jnp.einsum(
            "hqk,khd->qhd", grad_scores, key_low, preferred_element_type=full
        )
        grad_key_rot = score_scale * jnp.einsum(
            "hqk,qhd->khd", grad_scores, query_low, preferred_element_type=full
        )
        back_query = rotate(grad_query_rot, tables, -1.0)
        back_key = rotate(grad_key_rot, tables, -1.0)
        gain_q_grad = jnp.sum(back_query * query_unit, axis=(0, 1))
        gain_k_grad = jnp.sum(back_key * key_unit, axis=(0, 1))
        grad_query_raw = norm_backward(back_query * gain_q, query_unit, query_scale)
        grad_key_raw = norm_backward(back_key * gain_k, key_unit, key_scale)
        grad_qkv = jnp.concatenate(
            [
                grad_query_raw.reshape(row_count, model_width),
                grad_key_raw.reshape(row_count, model_width),
                grad_values.reshape(row_count, model_width),
            ],
            axis=1,
        ).astype(low)
        qkv_grad = weight_grad(hidden_one, grad_qkv)
        qkv_bias_grad = jnp.sum(grad_qkv.astype(full), axis=0)
        grad_hidden_one = backward_dot(grad_qkv, qkv_full)
        patch_grad = (
            grad_middle + norm_backward(grad_hidden_one * (1.0 + scale_attn), normed_one, scale_one)
        ).astype(low)

        def span_sum(values):
            return jnp.sum(values.reshape(spans, SPAN, model_width), axis=1)

        grad_spans = jnp.concatenate(
            [
                span_sum(grad_hidden_one),
                span_sum(grad_hidden_one * normed_one),
                span_sum(grad_gate_attn),
                span_sum(grad_hidden_two),
                span_sum(grad_hidden_two * normed_two),
                span_sum(grad_gate_ffn),
            ],
            axis=1,
        )
        grad_modulation = jnp.sum(span_hot[:, :, None] * grad_spans[:, None, :], axis=0).astype(low)
        grad_mod = grad_modulation.reshape(slots, fsdp_size, mod_cols).transpose(1, 0, 2)
        grad_mod = exchange_small(grad_mod, "fsdp", fsdp_size)
        grad_mod = gather_small(grad_mod[None], "dp", dp_size).reshape(-1, mod_cols)
        mod_bias_grad = jnp.sum(grad_mod.astype(full), axis=0)
        mod_grad = outer_grad(silu_cols, grad_mod)
        cond_part = dot_t(grad_mod, mod_weight).reshape(dp_size, fsdp_size, slots, mod_rows)
        cond_part = scatter_sum_small(cond_part.transpose(1, 0, 2, 3), "fsdp", fsdp_size)[0]
        cond_part = exchange_small(cond_part, "dp", dp_size)
        cond_grad = (
            cond_part.transpose(1, 0, 2).reshape(slots, model_width) * silu_slope(cond_full)
        ).astype(low)

        rows = [qkv_bias_grad, proj_bias_grad, up_bias_grad, down_bias_grad, gain_q_grad, gain_k_grad]
        vector_grad = jnp.concatenate([r.reshape(fsdp_size, -1) for r in rows], axis=1)
        vector_grad = scatter_sum_small(vector_grad, "fsdp", fsdp_size)
        vector_grad = sum_small(vector_grad, "dp", dp_size)[0]
        out = [vector_grad[bounds[k] : bounds[k + 1]] for k in range(6)]
        return (
            block_out,
            patch_grad,
            cond_grad,
            mod_grad,
            mod_bias_grad,
            qkv_grad,
            out[0],
            jnp.stack([out[4], out[5]]),
            proj_grad,
            out[1],
            up_grad,
            out[2],
            down_grad,
            out[3],
        )

    return per_device


def solution(mesh):
    rows = P(("dp", "fsdp"), None)
    matrix = P("dp", "fsdp")
    vector = P("fsdp")
    gains = P(None, "fsdp")
    return jax.shard_map(
        make_per_device(mesh.shape["dp"], mesh.shape["fsdp"]),
        mesh=mesh,
        in_specs=(
            rows,
            rows,
            P(("dp", "fsdp")),
            P(None, ("dp", "fsdp")),
            matrix,
            vector,
            matrix,
            vector,
            gains,
            matrix,
            vector,
            matrix,
            vector,
            matrix,
            vector,
            rows,
        ),
        out_specs=(
            rows,
            rows,
            rows,
            matrix,
            vector,
            matrix,
            vector,
            gains,
            matrix,
            vector,
            matrix,
            vector,
            matrix,
            vector,
        ),
        check_vma=False,
    )
```

```python
import jax
import jax.numpy as jnp
from jax import lax
from jax.experimental import pallas as pl
from jax.experimental.pallas import tpu as pltpu
from jax.sharding import PartitionSpec as P

HEADS = 16
SPAN = 64

epsilon = 1e-06
low = jnp.bfloat16
full = jnp.float32


def rms_scale(values):
    return lax.rsqrt(jnp.mean(values * values, axis=-1, keepdims=True) + epsilon)


def norm_backward(grad_normed, normed, factor):
    return factor * (grad_normed - normed * jnp.mean(grad_normed * normed, axis=-1, keepdims=True))


def rotary_tables(coord_rows, quarter):
    frequencies = 10000.0 ** (-jnp.arange(quarter, dtype=full) / quarter)
    row_angle = coord_rows[0].astype(full)[:, None, None] * frequencies
    col_angle = coord_rows[1].astype(full)[:, None, None] * frequencies
    return (jnp.cos(row_angle), jnp.sin(row_angle), jnp.cos(col_angle), jnp.sin(col_angle))


def rotate(values, tables, direction):
    half_size = values.shape[-1] // 2
    quarter = half_size // 2
    pieces_out = []
    for which_half in range(2):
        cosine = tables[2 * which_half]
        sine_tab = direction * tables[2 * which_half + 1]
        start_col = which_half * half_size
        first_part = values[..., start_col : start_col + quarter]
        second = values[..., start_col + quarter : start_col + half_size]
        pieces_out.append(first_part * cosine - second * sine_tab)
        pieces_out.append(second * cosine + first_part * sine_tab)
    return jnp.concatenate(pieces_out, axis=-1)


def dot(left, right):
    return jnp.dot(left, right, preferred_element_type=full)


def dot_t(left, right):
    return lax.dot_general(left, right, (((1,), (1,)), ((), ())), preferred_element_type=full)


def outer_grad(left, right):
    return lax.dot_general(left, right, (((0,), (0,)), ((), ())), preferred_element_type=full)


def silu_slope(values):
    sigmoid_gate = jax.nn.sigmoid(values)
    return sigmoid_gate * (1.0 + values * (1.0 - sigmoid_gate))


def swap(values, axis, size, bit):
    return lax.ppermute(values, axis, [(k, k ^ bit) for k in range(size)])


def bits_of(size):
    return [1 << b for b in range(size.bit_length() - 1)]


def gather_small(values, axis, size):
    index = lax.axis_index(axis)
    for bit in bits_of(size):
        other = swap(values, axis, size, bit)
        upper = (index & bit) != 0
        values = jnp.concatenate(
            [jnp.where(upper, other, values), jnp.where(upper, values, other)], axis=0
        )
    return values


def scatter_sum_small(values, axis, size):
    index = lax.axis_index(axis)
    for bit in reversed(bits_of(size)):
        half = values.shape[0] // 2
        upper = (index & bit) != 0
        first, second = values[:half], values[half:]
        values = jnp.where(upper, second, first) + swap(
            jnp.where(upper, first, second), axis, size, bit
        )
    return values


def sum_small(values, axis, size):
    for bit in bits_of(size):
        values = values + swap(values, axis, size, bit)
    return values


def xor_order(values, index, size):
    tail = values.shape[1:]
    for bit in bits_of(size):
        paired = values.reshape((size // (2 * bit), 2, bit) + tail)
        values = jnp.where((index & bit) != 0, jnp.flip(paired, axis=1), paired)
        values = values.reshape((size,) + tail)
    return values


def exchange_small(values, axis, size):
    index = lax.axis_index(axis)
    tail = values.shape[1:]
    values = xor_order(values, index, size)
    for bit in bits_of(size):
        paired = values.reshape((size // (2 * bit), 2, bit) + tail)
        moved = swap(paired[:, 1], axis, size, bit)
        values = jnp.stack([paired[:, 0], moved], axis=1).reshape((size,) + tail)
    return xor_order(values, index, size)


def gather_weight(weight, dp_size, fsdp_size):
    rows, cols = weight.shape
    whole = lax.all_gather(weight, ("dp", "fsdp"), axis=0, tiled=False)
    whole = whole.reshape(dp_size, fsdp_size, rows, cols).transpose(1, 0, 2, 3)
    return whole.reshape(fsdp_size, dp_size * rows, cols)


def scatter_grad(blocks, dp_size):
    rows, cols = blocks[0].shape
    parts = jnp.stack([b.reshape(dp_size, rows // dp_size, cols) for b in blocks], axis=1)
    parts = lax.psum_scatter(parts, "dp", scatter_dimension=0, tiled=False)
    return lax.psum_scatter(parts, "fsdp", scatter_dimension=0, tiled=False).astype(full)


def masked_scores(query_low, key_low, same_item, score_scale):
    scores = jnp.einsum("qhd,khd->hqk", query_low, key_low, preferred_element_type=full)
    return jnp.where(same_item, scores * score_scale, -1e30)


def make_plain(dp_size, fsdp_size):
    def per_device(
        patches,
        conditions,
        segment_ids,
        grid_coords,
        mod_weight,
        mod_bias,
        qkv_weight,
        qkv_bias,
        qk_gains,
        proj_weight,
        proj_bias,
        up_weight,
        up_bias,
        down_weight,
        down_bias,
        out_cotangent,
    ):
        row_count, model_width = patches.shape
        slots = conditions.shape[0]
        spans = row_count // SPAN
        head_size = model_width // HEADS
        score_scale = head_size ** (-0.5)
        head_shape = (row_count, HEADS, head_size)
        dp_index = lax.axis_index("dp")
        mod_rows, mod_cols = mod_weight.shape

        qkv_full = gather_weight(qkv_weight, dp_size, fsdp_size)
        proj_full = gather_weight(proj_weight, dp_size, fsdp_size)
        up_full = gather_weight(up_weight, dp_size, fsdp_size)
        down_full = gather_weight(down_weight, dp_size, fsdp_size)

        gain_cols = qk_gains.shape[1]
        sizes = [qkv_bias.shape[0], proj_bias.shape[0], up_bias.shape[0], down_bias.shape[0]]
        vector = jnp.concatenate(
            [qkv_bias, proj_bias, up_bias, down_bias, qk_gains[0], qk_gains[1]]
        )
        vectors = gather_small(vector[None], "fsdp", fsdp_size).astype(full)
        bounds = [0]
        for size in sizes + [gain_cols, gain_cols]:
            bounds.append(bounds[-1] + size)
        pieces = [vectors[:, bounds[k] : bounds[k + 1]] for k in range(6)]
        qkv_vector, proj_vector, up_vector, down_vector, gain_q, gain_k = [
            p.reshape(-1) for p in pieces
        ]

        cond_full = conditions.astype(full)
        silu_low = jax.nn.silu(cond_full).astype(low)
        silu_all = gather_small(
            gather_small(silu_low[None], "fsdp", fsdp_size)[None], "dp", dp_size
        ).reshape(dp_size * fsdp_size * slots, model_width)
        silu_cols = lax.dynamic_slice_in_dim(silu_all, dp_index * mod_rows, mod_rows, axis=1)
        mod_part = dot(silu_cols, mod_weight).reshape(dp_size, fsdp_size, slots, mod_cols)
        mod_sum = scatter_sum_small(mod_part, "dp", dp_size)[0] + mod_bias.astype(full)
        modulation = exchange_small(mod_sum, "fsdp", fsdp_size)
        modulation = modulation.transpose(1, 0, 2).reshape(slots, fsdp_size * mod_cols)
        span_ids = segment_ids.reshape(spans, SPAN)[:, 0]
        span_hot = (span_ids[:, None] == jnp.arange(slots, dtype=jnp.int32)[None, :]).astype(full)
        span_mod = jnp.sum(span_hot[:, :, None] * modulation[None], axis=1)

        def per_row(k):
            part = span_mod[:, k * model_width : (k + 1) * model_width]
            return jnp.broadcast_to(part[:, None, :], (spans, SPAN, model_width)).reshape(
                row_count, model_width
            )

        shift_attn, scale_attn, gate_attn, shift_ffn, scale_ffn, gate_ffn = map(per_row, range(6))

        def cols_of(blocks):
            return jnp.concatenate(blocks, axis=1)

        def forward_dot(rows_low, weight_full):
            return cols_of([dot(rows_low, weight_full[j]) for j in range(fsdp_size)])

        def split(values):
            width = values.shape[1] // fsdp_size
            return [values[:, j * width : (j + 1) * width] for j in range(fsdp_size)]

        def backward_dot(grad_low, weight_full):
            parts = split(grad_low)
            total = dot_t(parts[0], weight_full[0])
            for j in range(1, fsdp_size):
                total = total + dot_t(parts[j], weight_full[j])
            return total

        def weight_grad(rows_low, grad_low):
            return scatter_grad(
                [outer_grad(rows_low, part).astype(low) for part in split(grad_low)], dp_size
            )

        tables = rotary_tables(grid_coords, head_size // 4)
        patch_full = patches.astype(full)
        scale_one = rms_scale(patch_full)
        normed_one = patch_full * scale_one
        hidden_one = (normed_one * (1.0 + scale_attn) + shift_attn).astype(low)
        qkv_rows = forward_dot(hidden_one, qkv_full) + qkv_vector
        query_raw = qkv_rows[:, 0:model_width].reshape(head_shape)
        key_raw = qkv_rows[:, model_width : 2 * model_width].reshape(head_shape)
        value_low = qkv_rows[:, 2 * model_width :].reshape(head_shape).astype(low)
        query_scale = rms_scale(query_raw)
        query_unit = query_raw * query_scale
        key_scale = rms_scale(key_raw)
        key_unit = key_raw * key_scale
        query_low = rotate(query_unit * gain_q, tables, 1.0).astype(low)
        key_low = rotate(key_unit * gain_k, tables, 1.0).astype(low)
        same_item = (segment_ids[:, None] == segment_ids[None, :])[None]
        scores = masked_scores(query_low, key_low, same_item, score_scale)
        exponentials = jnp.exp(scores - jnp.max(scores, axis=-1, keepdims=True))
        probs = exponentials / jnp.sum(exponentials, axis=-1, keepdims=True)
        probs_low = probs.astype(low)
        attended_low = (
            jnp.einsum("hqk,khd->qhd", probs_low, value_low, preferred_element_type=full)
            .reshape(row_count, model_width)
            .astype(low)
        )
        branch_attn = forward_dot(attended_low, proj_full) + proj_vector
        middle = patch_full + gate_attn * branch_attn
        scale_two = rms_scale(middle)
        normed_two = middle * scale_two
        hidden_two = (normed_two * (1.0 + scale_ffn) + shift_ffn).astype(low)
        gate_up = forward_dot(hidden_two, up_full) + up_vector
        hidden_units = gate_up.shape[1] // 2
        gate_part = gate_up[:, :hidden_units]
        up_part = gate_up[:, hidden_units:]
        gated_low = (jax.nn.silu(gate_part) * up_part).astype(low)
        branch_ffn = forward_dot(gated_low, down_full) + down_vector
        block_out = (middle + gate_ffn * branch_ffn).astype(low)

        grad_out = out_cotangent.astype(full)
        grad_gate_ffn = grad_out * branch_ffn
        grad_branch_ffn = (grad_out * gate_ffn).astype(low)
        down_bias_grad = jnp.sum(grad_branch_ffn.astype(full), axis=0)
        grad_gated = backward_dot(grad_branch_ffn, down_full)
        down_grad = weight_grad(gated_low, grad_branch_ffn)
        grad_gate_up = jnp.concatenate(
            [grad_gated * up_part * silu_slope(gate_part), grad_gated * jax.nn.silu(gate_part)],
            axis=1,
        ).astype(low)
        up_bias_grad = jnp.sum(grad_gate_up.astype(full), axis=0)
        grad_hidden_two = backward_dot(grad_gate_up, up_full)
        up_grad = weight_grad(hidden_two, grad_gate_up)
        grad_middle = grad_out + norm_backward(
            grad_hidden_two * (1.0 + scale_ffn), normed_two, scale_two
        )
        grad_gate_attn = grad_middle * branch_attn
        grad_branch_attn = (grad_middle * gate_attn).astype(low)
        proj_bias_grad = jnp.sum(grad_branch_attn.astype(full), axis=0)
        grad_attended = backward_dot(grad_branch_attn, proj_full).astype(low).reshape(head_shape)
        proj_grad = weight_grad(attended_low, grad_branch_attn)
        grad_probs = jnp.einsum(
            "qhd,khd->hqk", grad_attended, value_low, preferred_element_type=full
        )
        row_dot = jnp.sum(probs * grad_probs, axis=-1, keepdims=True)
        grad_scores = (probs * (grad_probs - row_dot)).astype(low)
        grad_values = jnp.einsum(
            "hqk,qhd->khd", probs_low, grad_attended, preferred_element_type=full
        )
        grad_query_rot = score_scale * jnp.einsum(
            "hqk,khd->qhd", grad_scores, key_low, preferred_element_type=full
        )
        grad_key_rot = score_scale * jnp.einsum(
            "hqk,qhd->khd", grad_scores, query_low, preferred_element_type=full
        )
        back_query = rotate(grad_query_rot, tables, -1.0)
        back_key = rotate(grad_key_rot, tables, -1.0)
        gain_q_grad = jnp.sum(back_query * query_unit, axis=(0, 1))
        gain_k_grad = jnp.sum(back_key * key_unit, axis=(0, 1))
        grad_query_raw = norm_backward(back_query * gain_q, query_unit, query_scale)
        grad_key_raw = norm_backward(back_key * gain_k, key_unit, key_scale)
        grad_qkv = jnp.concatenate(
            [
                grad_query_raw.reshape(row_count, model_width),
                grad_key_raw.reshape(row_count, model_width),
                grad_values.reshape(row_count, model_width),
            ],
            axis=1,
        ).astype(low)
        qkv_grad = weight_grad(hidden_one, grad_qkv)
        qkv_bias_grad = jnp.sum(grad_qkv.astype(full), axis=0)
        grad_hidden_one = backward_dot(grad_qkv, qkv_full)
        patch_grad = (
            grad_middle + norm_backward(grad_hidden_one * (1.0 + scale_attn), normed_one, scale_one)
        ).astype(low)

        def span_sum(values):
            return jnp.sum(values.reshape(spans, SPAN, model_width), axis=1)

        grad_spans = jnp.concatenate(
            [
                span_sum(grad_hidden_one),
                span_sum(grad_hidden_one * normed_one),
                span_sum(grad_gate_attn),
                span_sum(grad_hidden_two),
                span_sum(grad_hidden_two * normed_two),
                span_sum(grad_gate_ffn),
            ],
            axis=1,
        )
        grad_modulation = jnp.sum(span_hot[:, :, None] * grad_spans[:, None, :], axis=0).astype(low)
        grad_mod = grad_modulation.reshape(slots, fsdp_size, mod_cols).transpose(1, 0, 2)
        grad_mod = exchange_small(grad_mod, "fsdp", fsdp_size)
        grad_mod = gather_small(grad_mod[None], "dp", dp_size).reshape(-1, mod_cols)
        mod_bias_grad = jnp.sum(grad_mod.astype(full), axis=0)
        mod_grad = outer_grad(silu_cols, grad_mod)
        cond_part = dot_t(grad_mod, mod_weight).reshape(dp_size, fsdp_size, slots, mod_rows)
        cond_part = scatter_sum_small(cond_part.transpose(1, 0, 2, 3), "fsdp", fsdp_size)[0]
        cond_part = exchange_small(cond_part, "dp", dp_size)
        cond_grad = (
            cond_part.transpose(1, 0, 2).reshape(slots, model_width) * silu_slope(cond_full)
        ).astype(low)

        rows = [qkv_bias_grad, proj_bias_grad, up_bias_grad, down_bias_grad, gain_q_grad, gain_k_grad]
        vector_grad = jnp.concatenate([r.reshape(fsdp_size, -1) for r in rows], axis=1)
        vector_grad = scatter_sum_small(vector_grad, "fsdp", fsdp_size)
        vector_grad = sum_small(vector_grad, "dp", dp_size)[0]
        out = [vector_grad[bounds[k] : bounds[k + 1]] for k in range(6)]
        return (
            block_out,
            patch_grad,
            cond_grad,
            mod_grad,
            mod_bias_grad,
            qkv_grad,
            out[0],
            jnp.stack([out[4], out[5]]),
            proj_grad,
            out[1],
            up_grad,
            out[2],
            down_grad,
            out[3],
        )

    return per_device


PLANE = 4


def cross(values, hop):
    return lax.ppermute(values, "dp", [(k, k ^ (2 * hop)) for k in range(2 * PLANE)])


def partner(values):
    return lax.ppermute(values, "dp", [(k, k ^ 1) for k in range(2 * PLANE)])


def along(values, hop, size):
    return lax.ppermute(values, "fsdp", [(k, k ^ hop) for k in range(size)])


def plane_blocks(values):
    return [values] + [cross(values, hop) for hop in range(1, PLANE)]


def plane_sum(blocks):
    total = blocks[0]
    for hop in range(1, PLANE):
        total = total + cross(blocks[hop].astype(low), hop).astype(full)
    return total


def z_blocks(values, index, size):
    blocks = jnp.stack([values] + [along(values, hop, size) for hop in range(1, size)])
    return xor_order(blocks, index, size)


def z_exchange(values, index, size):
    values = xor_order(values, index, size)
    moved = jnp.stack([values[0]] + [along(values[hop], hop, size) for hop in range(1, size)])
    return xor_order(moved, index, size)


def z_sum_own(values, index, size):
    values = xor_order(values, index, size)
    total = values[0].astype(full)
    for hop in range(1, size):
        total = total + along(values[hop], hop, size).astype(full)
    return total


class Place:
    def __init__(self, y, x, core, z):
        self.y, self.x, self.core, self.z = y, x, core, z
        self.chip = 2 * y + x
        self.dp = 2 * self.chip + core

    def hop(self, dy, dx, dc, dz):
        low_z, high_z = self.z % 2, self.z // 2
        low_z = 1 - low_z if dz & 1 else low_z
        high_z = 1 - high_z if dz & 2 else high_z
        return Place(
            1 - self.y if dy else self.y,
            1 - self.x if dx else self.x,
            1 - self.core if dc else self.core,
            2 * high_z + low_z,
        )


SELF = (0, 0, 0, 0)
PLANE_HOPS = [(0, 1, 0, 0), (1, 0, 0, 0), (1, 1, 0, 0)]
Z_HOPS = [(0, 0, 0, 1), (0, 0, 0, 2), (0, 0, 0, 3)]
CORE_HOP = (0, 0, 1, 0)
DP_HOPS = [(dy, dx, dc, 0) for dy in (0, 1) for dx in (0, 1) for dc in (0, 1)]
ALL_HOPS = [(dy, dx, dc, dz) for dz in range(4) for dy, dx, dc, _ in DP_HOPS]
GROUP_HOPS = [(dy, dx, 0, dz) for dz in range(4) for dy in (0, 1) for dx in (0, 1)]


def exchange(identity, inputs, out_shapes, plan):
    hops = []
    for move in plan:
        if move[0] != SELF and move[0] not in hops:
            hops.append(move[0])

    def kernel(*refs):
        ins, outs = refs[: len(inputs)], refs[len(inputs) : len(inputs) + len(out_shapes)]
        send, recv = refs[-2:]
        dp_index = lax.axis_index("dp")
        me = Place(dp_index // 4, (dp_index // 2) % 2, dp_index % 2, lax.axis_index("fsdp"))

        def target(hop):
            peer = me.hop(*hop)
            return peer, {"dp": peer.dp, "fsdp": peer.z}

        barrier = pltpu.get_barrier_semaphore()
        for hop in hops:
            pl.semaphore_signal(
                barrier, 1, device_id=target(hop)[1], device_id_type=pl.DeviceIdType.MESH
            )
        pl.semaphore_wait(barrier, len(hops))
        copies = []
        forwarded = set()
        for number, (hop, source, source_at, out, out_at, after) in enumerate(plan):
            peer, device = target(hop)
            src = (ins if after is None else outs)[source]
            src = src if source_at is None else src.at[source_at(me, peer)]
            dst = outs[out]
            dst = dst if out_at is None else dst.at[out_at(me, peer)]
            for earlier in after or ():
                if earlier not in forwarded:
                    if plan[earlier][0] == SELF:
                        copies[earlier].wait()
                    else:
                        copies[earlier].wait_recv()
                    forwarded.add(earlier)
            if hop == SELF:
                copy = pltpu.make_async_copy(src, dst, send.at[number])
            else:
                copy = pltpu.make_async_remote_copy(
                    src_ref=src,
                    dst_ref=dst,
                    send_sem=send.at[number],
                    recv_sem=recv.at[number],
                    device_id=device,
                    device_id_type=pl.DeviceIdType.MESH,
                )
            copy.start()
            copies.append(copy)
        for number, copy in enumerate(copies):
            if plan[number][0] == SELF:
                if number not in forwarded:
                    copy.wait()
                continue
            copy.wait_send()
            if number not in forwarded:
                copy.wait_recv()

    anywhere = pl.BlockSpec(memory_space=pl.ANY)
    return pl.pallas_call(
        kernel,
        out_shape=[jax.ShapeDtypeStruct(shape, dtype) for shape, dtype in out_shapes],
        in_specs=[anywhere] * len(inputs),
        out_specs=[anywhere] * len(out_shapes),
        scratch_shapes=[
            pltpu.SemaphoreType.DMA((len(plan),)),
            pltpu.SemaphoreType.DMA((len(plan),)),
        ],
        compiler_params=pltpu.CompilerParams(collective_id=identity, has_side_effects=True),
    )(*inputs)


def gather_moves(hops, source, out, out_at):
    return [(hop, source, None, out, out_at, None) for hop in hops]


def by_chip(me, peer):
    return (me.chip,)


def by_dp(me, peer):
    return (me.dp,)


def by_z(me, peer):
    return (me.z,)


def by_core(me, peer):
    return (me.core,)


def tie(first, second):
    return lax.optimization_barrier((first, second))


def put(values, own, *at):
    start = tuple(at) + (0,) * (values.ndim - len(at))
    return lax.dynamic_update_slice(values, own.reshape((1,) * len(at) + own.shape), start)


def slotted(hops, source, source_at, out):
    return [
        (hop, source, source_at, out, lambda me, peer, n=n: (n,), None)
        for n, hop in enumerate(hops)
    ]


def to_chip(me, peer):
    return (peer.chip,)


def to_z(me, peer):
    return (peer.z,)


def make_plane(z_size):
    def per_device(
        patches,
        conditions,
        segment_ids,
        grid_coords,
        mod_weight,
        mod_bias,
        qkv_weight,
        qkv_bias,
        qk_gains,
        proj_weight,
        proj_bias,
        up_weight,
        up_bias,
        down_weight,
        down_bias,
        out_cotangent,
    ):
        row_count, width = patches.shape
        slots = conditions.shape[0]
        spans = row_count // SPAN
        head_size = width // HEADS
        heads = HEADS // PLANE
        part_cols = width // PLANE
        score_scale = head_size ** (-0.5)
        dp_index = lax.axis_index("dp")
        z_index = lax.axis_index("fsdp")
        chip = dp_index >> 1
        core = dp_index & 1
        upper = core == 1
        mod_rows, mod_cols = mod_weight.shape
        rows_all = PLANE * row_count
        shard = qkv_weight.shape[0]

        def core_order(mine, other):
            return jnp.where(upper, other, mine), jnp.where(upper, mine, other)

        def both_cores(first, second):
            return jnp.concatenate(
                [jnp.concatenate([first[j], second[j]], axis=0) for j in range(z_size)], axis=1
            )

        def scatter_columns(pieces):
            ordered = xor_order(jnp.stack(pieces), chip, PLANE)
            mine = jnp.stack(
                [ordered[0]] + [cross(ordered[hop], hop) for hop in range(1, PLANE)]
            )
            first, second = core_order(mine, partner(mine))
            both = xor_order(jnp.stack([first, second], axis=1), chip, PLANE)
            return both.reshape(2 * PLANE * both.shape[2], both.shape[3])

        cond_full = conditions.astype(full)
        silu_low = jax.nn.silu(cond_full).astype(low)
        vector = jnp.concatenate(
            [qkv_bias, proj_bias, up_bias, down_bias, qk_gains[0], qk_gains[1]]
        )[None]
        meta = jnp.concatenate([segment_ids[None], grid_coords], axis=0)
        cols_qkv = qkv_weight.shape[1]
        cols_proj = proj_weight.shape[1]
        plan = gather_moves(Z_HOPS + [SELF], 0, 0, lambda me, peer: (me.dp, me.z))
        plan += gather_moves(Z_HOPS, 1, 1, by_z)
        plan += gather_moves(Z_HOPS, 3, 3, by_z)
        plan += gather_moves(Z_HOPS + [SELF], 4, 4, by_z)
        plan += gather_moves(PLANE_HOPS + [SELF], 5, 5, by_chip)
        plan += [(hop, 0, by_dp, 0, by_dp, (0, 1, 2, 3)) for hop in DP_HOPS if hop != SELF]
        plan += gather_moves(PLANE_HOPS, 2, 2, by_chip)
        silu_all, qkv_z, patch_all, proj_z, vectors, meta_all = exchange(
            1,
            [silu_low, qkv_weight, patches, proj_weight, vector, meta],
            [
                ((2 * PLANE, z_size, slots, width), low),
                ((z_size, shard, cols_qkv), low),
                ((PLANE, row_count, width), low),
                ((z_size, shard, cols_proj), low),
                ((z_size,) + vector.shape, low),
                ((PLANE,) + meta.shape, jnp.int32),
            ],
            plan,
        )

        qkv_z, up_later = tie(qkv_z, up_weight)
        up_z = lax.all_gather(up_later, "fsdp", axis=0, tiled=False)
        qkv_z = put(qkv_z, qkv_weight, z_index)
        proj_z = put(proj_z, proj_weight, z_index)
        patch_all = put(patch_all, patches, chip)

        silu_all = silu_all.reshape(-1, width)
        silu_cols = lax.dynamic_slice_in_dim(silu_all, dp_index * mod_rows, mod_rows, axis=1)
        mod_part = dot(silu_cols, mod_weight).reshape(2 * PLANE, z_size * slots, mod_cols)
        qkv_wide = jnp.concatenate([qkv_z[j] for j in range(z_size)], axis=1)
        qkv_pieces = jnp.stack(
            [
                jnp.concatenate(
                    [
                        qkv_wide[:, t * width + p * part_cols : t * width + (p + 1) * part_cols]
                        for t in range(3)
                    ],
                    axis=1,
                )
                for p in range(PLANE)
            ]
        )
        plan = [
            (hop, 0, to_chip, 0, by_dp, None) for hop in PLANE_HOPS
        ]
        plan += [
            (hop, 1, lambda me, peer: (peer.dp,), 1, lambda me, peer: (me.dp,), None)
            for hop in DP_HOPS
            if hop != SELF
        ]
        plan.append((CORE_HOP, 2, None, 2, None, None))
        for number, (dy, dx, dc, dz) in enumerate(PLANE_HOPS):
            from_hop = lambda me, peer, dy=dy, dx=dx: (me.hop(dy, dx, 0, 0).dp,)
            plan.append((CORE_HOP, 0, from_hop, 0, from_hop, (number,)))
        plan.append((CORE_HOP, 0, by_chip, 0, by_dp, None))
        qkv_slice, mod_parts, proj_other = exchange(
            2,
            [qkv_pieces, mod_part, proj_z],
            [
                ((2 * PLANE, shard, 3 * part_cols), low),
                (mod_part.shape, full),
                (proj_z.shape, low),
            ],
            plan,
        )
        qkv_slice = put(
            qkv_slice, lax.dynamic_index_in_dim(qkv_pieces, chip, 0, keepdims=False), dp_index
        )
        mod_parts = put(
            mod_parts, lax.dynamic_index_in_dim(mod_part, dp_index, 0, keepdims=False), dp_index
        )
        qkv_slice = qkv_slice.reshape(-1, 3 * part_cols)
        proj_slice = both_cores(*core_order(proj_z, proj_other))
        mod_sum = (jnp.sum(mod_parts, axis=0) + mod_bias.astype(full)).reshape(
            z_size, slots, mod_cols
        )
        plan = [
            (hop, 0, to_z, 0, lambda me, peer: (me.chip, me.z), None) for hop in Z_HOPS + [SELF]
        ]
        plan += [(hop, 0, by_chip, 0, by_chip, (0, 1, 2, 3)) for hop in PLANE_HOPS]
        (group_mod,) = exchange(
            3, [mod_sum], [((PLANE, z_size, slots, mod_cols), full)], plan
        )
        group_mod = group_mod.transpose(0, 2, 1, 3).reshape(PLANE, slots, z_size * mod_cols)
        modulation = lax.dynamic_index_in_dim(group_mod, chip, 0, keepdims=False)

        group_mod, (cot_later, up_z) = tie(group_mod, (out_cotangent, up_z))
        cot_all = xor_order(jnp.stack(plane_blocks(cot_later)), chip, PLANE)
        cot_all = cot_all.reshape(rows_all, width)
        half = up_weight.shape[1] * z_size // 2
        part_units = half // PLANE
        up_wide = jnp.concatenate([up_z[j] for j in range(z_size)], axis=1)
        up_slice = scatter_columns(
            [
                jnp.concatenate(
                    [
                        up_wide[:, t * half + p * part_units : t * half + (p + 1) * part_units]
                        for t in range(2)
                    ],
                    axis=1,
                )
                for p in range(PLANE)
            ]
        )
        segments = meta_all[:, 0].reshape(-1)
        tables = rotary_tables(meta_all[:, 1:].transpose(1, 0, 2).reshape(2, -1), head_size // 4)

        gain_cols = qk_gains.shape[1]
        sizes = [qkv_bias.shape[0], proj_bias.shape[0], up_bias.shape[0], down_bias.shape[0]]
        vectors = vectors[:, 0].astype(full)
        bounds = [0]
        for size in sizes + [gain_cols, gain_cols]:
            bounds.append(bounds[-1] + size)
        pieces = [vectors[:, bounds[k] : bounds[k + 1]] for k in range(6)]
        qkv_vector, proj_vector, up_vector, down_vector, gain_q, gain_k = [
            p.reshape(-1) for p in pieces
        ]

        def own_columns(flat, groups):
            parts = flat.reshape(groups, PLANE, -1)
            return lax.dynamic_slice_in_dim(parts, chip, 1, axis=1).reshape(-1)

        seg_spans = segments.reshape(PLANE, spans, SPAN)[:, :, 0]
        hot = (seg_spans[:, :, None] == jnp.arange(slots, dtype=jnp.int32)).astype(full)
        group_spans = jnp.sum(hot[:, :, :, None] * group_mod[:, None], axis=2)
        own_spans_ids = segment_ids.reshape(spans, SPAN)[:, 0]
        own_hot = (own_spans_ids[:, None] == jnp.arange(slots, dtype=jnp.int32)).astype(full)
        own_spans = jnp.sum(own_hot[:, :, None] * modulation[None], axis=1)

        def spread(values):
            count = values.shape[0]
            return jnp.broadcast_to(values[:, None, :], (count, SPAN, width)).reshape(
                count * SPAN, width
            )

        def per_row(k):
            return spread(own_spans[:, k * width : (k + 1) * width])

        def per_row_all(k):
            return spread(
                group_spans[:, :, k * width : (k + 1) * width].reshape(PLANE * spans, width)
            )

        patch_all = patch_all.reshape(rows_all, width).astype(full)
        hidden_one = (
            patch_all * rms_scale(patch_all) * (1.0 + per_row_all(1)) + per_row_all(0)
        ).astype(low)

        def core_swap(source, out, count):
            return [
                (
                    CORE_HOP,
                    source,
                    lambda me, peer, k=k: (k, peer.core),
                    out,
                    lambda me, peer, k=k: (k,),
                    None,
                )
                for k in range(count)
            ]

        def half_of(parts):
            return ((parts.shape[0],) + parts.shape[2:], low)

        def sum_cores(parts, other):
            mine = jnp.where(upper, parts[:, 1], parts[:, 0])
            return (mine.astype(full) + other.astype(full)).astype(low)

        def row_parts(left, right):
            cols = right.shape[1] // z_size
            parts = jnp.stack(
                [
                    outer_grad(left, right[:, j * cols : (j + 1) * cols]).astype(low)
                    for j in range(z_size)
                ]
            )
            return parts.reshape(z_size, 2, -1, cols)

        def widen(moved, groups):
            moved = moved.reshape(PLANE, shard, groups, -1)
            wide = jnp.concatenate(
                [moved[p, :, t] for t in range(groups) for p in range(PLANE)], axis=1
            )
            cols = wide.shape[1] // z_size
            return jnp.stack([wide[:, j * cols : (j + 1) * cols] for j in range(z_size)])

        def own_of(values, index):
            return lax.dynamic_index_in_dim(values, index, 0, keepdims=False)

        def z_sum_of(blocks, sent):
            return block_sum(blocks, own_of(sent, z_index))

        def plane_gather(identity, values, *more):
            (out,) = exchange(
                identity,
                [values],
                [((PLANE,) + values.shape, low)],
                gather_moves(PLANE_HOPS, 0, 0, by_chip),
            )
            return put(out, values, chip).reshape(rows_all, width)

        scatter_plan = slotted(PLANE_HOPS, 0, to_chip, 0)
        others = (PLANE - 1, row_count, width)

        def plane_scatter(values):
            return values.astype(low).reshape(PLANE, row_count, width)

        def block_sum(blocks, own):
            return own.astype(full) + jnp.sum(blocks.astype(full), axis=0)

        def plane_sum_of(blocks, sent):
            return block_sum(blocks, lax.dynamic_index_in_dim(sent, chip, 0, keepdims=False))

        head_shape = (rows_all, heads, head_size)
        block_shape = (PLANE, row_count, heads, head_size)
        qkv_rows = dot(hidden_one, qkv_slice) + own_columns(qkv_vector, 3)
        query_raw = qkv_rows[:, 0:part_cols].reshape(head_shape)
        key_raw = qkv_rows[:, part_cols : 2 * part_cols].reshape(head_shape)
        value_low = qkv_rows[:, 2 * part_cols :].astype(low).reshape(block_shape)
        query_scale = rms_scale(query_raw)
        query_unit = query_raw * query_scale
        key_scale = rms_scale(key_raw)
        key_unit = key_raw * key_scale
        query_low = rotate(query_unit * gain_q, tables, 1.0).astype(low).reshape(block_shape)
        key_low = rotate(key_unit * gain_k, tables, 1.0).astype(low).reshape(block_shape)
        seg_blocks = segments.reshape(PLANE, row_count)
        same_item = (seg_blocks[:, :, None] == seg_blocks[:, None, :])[:, None]
        scores = jnp.einsum("bqhd,bkhd->bhqk", query_low, key_low, preferred_element_type=full)
        scores = jnp.where(same_item, scores * score_scale, -1e30)
        exponentials = jnp.exp(scores - jnp.max(scores, axis=-1, keepdims=True))
        probs = exponentials / jnp.sum(exponentials, axis=-1, keepdims=True)
        probs_low = probs.astype(low)
        attended_low = (
            jnp.einsum("bhqk,bkhd->bqhd", probs_low, value_low, preferred_element_type=full)
            .astype(low)
            .reshape(rows_all, part_cols)
        )
        attn_terms = plane_scatter(dot(attended_low, proj_slice))
        attn_terms, (cot_all, up_slice) = tie(attn_terms, (cot_all, up_slice))
        cot_all = cot_all.astype(full)
        branch_blocks, down_z = exchange(
            4,
            [attn_terms, down_weight],
            [
                (others, low),
                ((z_size,) + down_weight.shape, low),
            ],
            scatter_plan + gather_moves(Z_HOPS, 1, 1, by_z),
        )
        down_z = put(down_z, down_weight, z_index)
        branch_attn = plane_sum_of(branch_blocks, attn_terms) + proj_vector

        patch_full = patches.astype(full)
        scale_one = rms_scale(patch_full)
        normed_one = patch_full * scale_one
        middle = patch_full + per_row(2) * branch_attn
        scale_two = rms_scale(middle)
        normed_two = middle * scale_two
        hidden_two = (normed_two * (1.0 + per_row(4)) + per_row(3)).astype(low)

        hidden_all, down_other = exchange(
            5,
            [hidden_two, down_z],
            [((PLANE, row_count, width), low), (down_z.shape, low)],
            gather_moves(PLANE_HOPS, 0, 0, by_chip) + [(CORE_HOP, 1, None, 1, None, None)],
        )
        hidden_all = put(hidden_all, hidden_two, chip).reshape(rows_all, width)
        down_slice = both_cores(*core_order(down_z, down_other))
        grad_branch_ffn = (cot_all * per_row_all(5)).astype(low)
        grad_gated = dot_t(grad_branch_ffn, down_slice)
        gate_up = dot(hidden_all, up_slice) + own_columns(up_vector, 2)
        gate_part = gate_up[:, :part_units]
        up_part = gate_up[:, part_units:]
        gated_low = (jax.nn.silu(gate_part) * up_part).astype(low)
        grad_gate_up = jnp.concatenate(
            [grad_gated * up_part * silu_slope(gate_part), grad_gated * jax.nn.silu(gate_part)],
            axis=1,
        ).astype(low)
        hidden_two_terms = plane_scatter(dot_t(grad_gate_up, up_slice))
        down_parts = row_parts(gated_low, grad_branch_ffn)
        up_parts = outer_grad(hidden_all, grad_gate_up).astype(low).reshape(PLANE, 2, shard, -1)
        hidden_two_blocks, down_other, up_other = exchange(
            6,
            [hidden_two_terms, down_parts, up_parts],
            [(others, low), half_of(down_parts), half_of(up_parts)],
            scatter_plan + core_swap(1, 1, z_size) + core_swap(2, 2, PLANE),
        )
        grad_hidden_two = plane_sum_of(hidden_two_blocks, hidden_two_terms)
        down_mine = sum_cores(down_parts, down_other)
        up_mine = sum_cores(up_parts, up_other)
        ffn_terms = plane_scatter(dot(gated_low, down_slice))

        grad_out = out_cotangent.astype(full)
        own_gbf = (grad_out * per_row(5)).astype(low).astype(full)
        down_bias_grad = jnp.sum(own_gbf, axis=0)
        up_bias_cols = jnp.sum(grad_gate_up.astype(full), axis=0)
        grad_middle = grad_out + norm_backward(
            grad_hidden_two * (1.0 + per_row(4)), normed_two, scale_two
        )
        grad_gate_attn = grad_middle * branch_attn
        grad_branch_attn = (grad_middle * per_row(2)).astype(low)
        proj_bias_grad = jnp.sum(grad_branch_attn.astype(full), axis=0)
        grad_branch_all, down_blocks = exchange(
            7,
            [grad_branch_attn, down_mine],
            [
                ((PLANE, row_count, width), low),
                ((z_size - 1,) + down_mine.shape[1:], low),
            ],
            gather_moves(PLANE_HOPS, 0, 0, by_chip) + slotted(Z_HOPS, 1, to_z, 1),
        )
        grad_branch_all = put(grad_branch_all, grad_branch_attn, chip).reshape(rows_all, width)
        down_grad = z_sum_of(down_blocks, down_mine)

        grad_branch_all, (ffn_terms, up_mine) = tie(grad_branch_all, (ffn_terms, up_mine))
        ffn_terms = xor_order(ffn_terms, chip, PLANE)
        branch_ffn = ffn_terms[0].astype(full)
        for hop in range(1, PLANE):
            branch_ffn = branch_ffn + cross(ffn_terms[hop], hop).astype(full)
        branch_ffn = branch_ffn + down_vector
        block_out = (middle + per_row(5) * branch_ffn).astype(low)
        grad_gate_ffn = grad_out * branch_ffn
        up_mine = xor_order(up_mine, chip, PLANE)
        up_moved = jnp.stack([up_mine[0]] + [cross(up_mine[hop], hop) for hop in range(1, PLANE)])
        up_wide = widen(xor_order(up_moved, chip, PLANE), 2)

        grad_attended = dot_t(grad_branch_all, proj_slice).astype(low).reshape(block_shape)
        proj_parts = row_parts(attended_low, grad_branch_all)
        grad_probs = jnp.einsum(
            "bqhd,bkhd->bhqk", grad_attended, value_low, preferred_element_type=full
        )
        row_dot = jnp.sum(probs * grad_probs, axis=-1, keepdims=True)
        grad_scores = (probs * (grad_probs - row_dot)).astype(low)
        grad_values = jnp.einsum(
            "bhqk,bqhd->bkhd", probs_low, grad_attended, preferred_element_type=full
        )
        grad_query_rot = score_scale * jnp.einsum(
            "bhqk,bkhd->bqhd", grad_scores, key_low, preferred_element_type=full
        )
        grad_key_rot = score_scale * jnp.einsum(
            "bhqk,bqhd->bkhd", grad_scores, query_low, preferred_element_type=full
        )
        back_query = rotate(grad_query_rot.reshape(head_shape), tables, -1.0)
        back_key = rotate(grad_key_rot.reshape(head_shape), tables, -1.0)
        gain_q_grad = jnp.sum(back_query * query_unit, axis=(0, 1))
        gain_k_grad = jnp.sum(back_key * key_unit, axis=(0, 1))
        grad_query_raw = norm_backward(back_query * gain_q, query_unit, query_scale)
        grad_key_raw = norm_backward(back_key * gain_k, key_unit, key_scale)
        grad_qkv = jnp.concatenate(
            [
                grad_query_raw.reshape(rows_all, part_cols),
                grad_key_raw.reshape(rows_all, part_cols),
                grad_values.reshape(rows_all, part_cols),
            ],
            axis=1,
        ).astype(low)
        qkv_bias_cols = jnp.sum(grad_qkv.astype(full), axis=0)
        qkv_parts = outer_grad(hidden_one, grad_qkv).astype(low).reshape(PLANE, 2, shard, -1)
        hidden_one_terms = plane_scatter(dot_t(grad_qkv, qkv_slice))
        hidden_one_terms, (block_out, grad_gate_ffn, up_wide) = tie(
            hidden_one_terms, (block_out, grad_gate_ffn, up_wide)
        )
        up_grad = lax.psum_scatter(up_wide, "fsdp", scatter_dimension=0, tiled=False).astype(full)
        hidden_one_blocks, qkv_other, proj_other = exchange(
            8,
            [hidden_one_terms, qkv_parts, proj_parts],
            [(others, low), half_of(qkv_parts), half_of(proj_parts)],
            scatter_plan + core_swap(1, 1, PLANE) + core_swap(2, 2, z_size),
        )
        grad_hidden_one = plane_sum_of(hidden_one_blocks, hidden_one_terms)
        qkv_mine = sum_cores(qkv_parts, qkv_other)
        proj_mine = sum_cores(proj_parts, proj_other)
        patch_grad = (
            grad_middle + norm_backward(grad_hidden_one * (1.0 + per_row(1)), normed_one, scale_one)
        ).astype(low)

        def span_sum(values):
            return jnp.sum(values.reshape(spans, SPAN, width), axis=1)

        grad_spans = jnp.concatenate(
            [
                span_sum(grad_hidden_one),
                span_sum(grad_hidden_one * normed_one),
                span_sum(grad_gate_attn),
                span_sum(grad_hidden_two),
                span_sum(grad_hidden_two * normed_two),
                span_sum(grad_gate_ffn),
            ],
            axis=1,
        )
        grad_modulation = jnp.sum(own_hot[:, :, None] * grad_spans[:, None, :], axis=0).astype(low)
        grad_mod = grad_modulation.reshape(slots, z_size, mod_cols).transpose(1, 0, 2)

        def place(flat, groups):
            spot = (jnp.arange(PLANE) == chip).astype(full)
            return (flat.reshape(groups, 1, -1) * spot[None, :, None]).reshape(-1)

        rows = [
            place(qkv_bias_cols, 3),
            proj_bias_grad,
            place(up_bias_cols, 2),
            down_bias_grad,
            gain_q_grad,
            gain_k_grad,
        ]
        vector_grad = jnp.concatenate([r.reshape(z_size, 1, -1) for r in rows], axis=2)
        plan = [
            (hop, 1, to_z, 1, lambda me, peer: (me.dp, me.z), None) for hop in Z_HOPS + [SELF]
        ]
        plan += [(hop, 2, to_z, 2, by_z, None) for hop in Z_HOPS + [SELF]]
        plan += [(hop, 0, to_chip, 0, by_chip, None) for hop in PLANE_HOPS]
        plan += [(hop, 1, by_dp, 1, by_dp, (0, 1, 2, 3)) for hop in DP_HOPS if hop != SELF]
        plan += slotted(Z_HOPS, 3, to_z, 3)
        qkv_moved, grad_mod, vector_parts, proj_blocks = exchange(
            9,
            [qkv_mine, grad_mod, vector_grad, proj_mine],
            [
                (qkv_mine.shape, low),
                ((2 * PLANE, z_size, slots, mod_cols), low),
                (vector_grad.shape, full),
                ((z_size - 1,) + proj_mine.shape[1:], low),
            ],
            plan,
        )
        proj_grad = z_sum_of(proj_blocks, proj_mine)
        qkv_wide = widen(put(qkv_moved, own_of(qkv_mine, chip), chip), 3)
        grad_mod = grad_mod.reshape(-1, mod_cols)
        vector_sum = jnp.sum(vector_parts, axis=0)
        cond_part = dot_t(grad_mod, mod_weight).reshape(2 * PLANE, z_size, slots, mod_rows)
        plan = slotted(Z_HOPS, 0, to_z, 0)
        plan += [
            (
                hop,
                1,
                lambda me, peer: (peer.dp, peer.z),
                1,
                lambda me, peer: (me.dp, me.z),
                None,
            )
            for hop in ALL_HOPS
        ]
        plan += gather_moves(DP_HOPS, 2, 2, by_dp)
        qkv_blocks, cond_parts, vector_parts = exchange(
            10,
            [qkv_wide, cond_part, vector_sum],
            [
                ((z_size - 1,) + qkv_wide.shape[1:], low),
                (cond_part.shape, full),
                ((2 * PLANE,) + vector_sum.shape, full),
            ],
            plan,
        )
        qkv_grad = z_sum_of(qkv_blocks, qkv_wide)
        mod_bias_grad = jnp.sum(grad_mod.astype(full), axis=0)
        mod_grad = outer_grad(silu_cols, grad_mod)
        cond_part = jnp.sum(cond_parts, axis=1)
        cond_grad = (
            cond_part.transpose(1, 0, 2).reshape(slots, width) * silu_slope(cond_full)
        ).astype(low)
        vector_grad = jnp.sum(vector_parts, axis=0)[0]
        out = [vector_grad[bounds[k] : bounds[k + 1]] for k in range(6)]
        return (
            block_out,
            patch_grad,
            cond_grad,
            mod_grad,
            mod_bias_grad,
            qkv_grad,
            out[0],
            jnp.stack([out[4], out[5]]),
            proj_grad,
            out[1],
            up_grad,
            out[2],
            down_grad,
            out[3],
        )

    return per_device


def solution(mesh):
    if mesh.shape["dp"] == 2 * PLANE and mesh.shape["fsdp"] == 4:
        body = make_plane(mesh.shape["fsdp"])
    else:
        body = make_plain(mesh.shape["dp"], mesh.shape["fsdp"])
    rows = P(("dp", "fsdp"), None)
    matrix = P("dp", "fsdp")
    vector = P("fsdp")
    gains = P(None, "fsdp")
    return jax.shard_map(
        body,
        mesh=mesh,
        in_specs=(
            rows,
            rows,
            P(("dp", "fsdp")),
            P(None, ("dp", "fsdp")),
            matrix,
            vector,
            matrix,
            vector,
            gains,
            matrix,
            vector,
            matrix,
            vector,
            matrix,
            vector,
            rows,
        ),
        out_specs=(
            rows,
            rows,
            rows,
            matrix,
            vector,
            matrix,
            vector,
            gains,
            matrix,
            vector,
            matrix,
            vector,
            matrix,
            vector,
        ),
        check_vma=False,
    )
```

```python
import functools

import jax
import jax.numpy as jnp
import numpy as np
from jax import lax
from jax.experimental import pallas as pl
from jax.experimental.pallas import tpu as pltpu
from jax.sharding import PartitionSpec as P

HEADS = 16
SPAN = 64
SIDE = 16

epsilon = 1e-06
low = jnp.bfloat16
full = jnp.float32


def rms_scale(values):
    return lax.rsqrt(jnp.mean(values * values, axis=-1, keepdims=True) + epsilon)


def norm_backward(grad_normed, normed, factor):
    return factor * (grad_normed - normed * jnp.mean(grad_normed * normed, axis=-1, keepdims=True))


def rotary_tables(coord_rows, quarter):
    frequencies = 10000.0 ** (-jnp.arange(quarter, dtype=full) / quarter)
    row_angle = coord_rows[0].astype(full)[:, None, None] * frequencies
    col_angle = coord_rows[1].astype(full)[:, None, None] * frequencies
    return (jnp.cos(row_angle), jnp.sin(row_angle), jnp.cos(col_angle), jnp.sin(col_angle))


def rotate(values, tables, direction):
    half_size = values.shape[-1] // 2
    quarter = half_size // 2
    pieces_out = []
    for which_half in range(2):
        cosine = tables[2 * which_half]
        sine_tab = direction * tables[2 * which_half + 1]
        start_col = which_half * half_size
        first_part = values[..., start_col : start_col + quarter]
        second = values[..., start_col + quarter : start_col + half_size]
        pieces_out.append(first_part * cosine - second * sine_tab)
        pieces_out.append(second * cosine + first_part * sine_tab)
    return jnp.concatenate(pieces_out, axis=-1)


def dot(left, right):
    return jnp.dot(left, right, preferred_element_type=full)


def dot_t(left, right):
    return lax.dot_general(left, right, (((1,), (1,)), ((), ())), preferred_element_type=full)


def outer_grad(left, right):
    return lax.dot_general(left, right, (((0,), (0,)), ((), ())), preferred_element_type=full)


def silu_slope(values):
    sigmoid_gate = jax.nn.sigmoid(values)
    return sigmoid_gate * (1.0 + values * (1.0 - sigmoid_gate))


def swap(values, axis, size, bit):
    return lax.ppermute(values, axis, [(k, k ^ bit) for k in range(size)])


def bits_of(size):
    return [1 << b for b in range(size.bit_length() - 1)]


def gather_small(values, axis, size):
    index = lax.axis_index(axis)
    for bit in bits_of(size):
        other = swap(values, axis, size, bit)
        upper = (index & bit) != 0
        values = jnp.concatenate(
            [jnp.where(upper, other, values), jnp.where(upper, values, other)], axis=0
        )
    return values


def scatter_sum_small(values, axis, size):
    index = lax.axis_index(axis)
    for bit in reversed(bits_of(size)):
        half = values.shape[0] // 2
        upper = (index & bit) != 0
        first, second = values[:half], values[half:]
        values = jnp.where(upper, second, first) + swap(
            jnp.where(upper, first, second), axis, size, bit
        )
    return values


def sum_small(values, axis, size):
    for bit in bits_of(size):
        values = values + swap(values, axis, size, bit)
    return values


def xor_order(values, index, size):
    tail = values.shape[1:]
    for bit in bits_of(size):
        paired = values.reshape((size // (2 * bit), 2, bit) + tail)
        values = jnp.where((index & bit) != 0, jnp.flip(paired, axis=1), paired)
        values = values.reshape((size,) + tail)
    return values


def exchange_small(values, axis, size):
    index = lax.axis_index(axis)
    tail = values.shape[1:]
    values = xor_order(values, index, size)
    for bit in bits_of(size):
        paired = values.reshape((size // (2 * bit), 2, bit) + tail)
        moved = swap(paired[:, 1], axis, size, bit)
        values = jnp.stack([paired[:, 0], moved], axis=1).reshape((size,) + tail)
    return xor_order(values, index, size)


def gather_weight(weight, dp_size, fsdp_size):
    rows, cols = weight.shape
    whole = lax.all_gather(weight, ("dp", "fsdp"), axis=0, tiled=False)
    whole = whole.reshape(dp_size, fsdp_size, rows, cols).transpose(1, 0, 2, 3)
    return whole.reshape(fsdp_size, dp_size * rows, cols)


def scatter_grad(blocks, dp_size):
    rows, cols = blocks[0].shape
    parts = jnp.stack([b.reshape(dp_size, rows // dp_size, cols) for b in blocks], axis=1)
    parts = lax.psum_scatter(parts, "dp", scatter_dimension=0, tiled=False)
    return lax.psum_scatter(parts, "fsdp", scatter_dimension=0, tiled=False).astype(full)


def masked_scores(query_low, key_low, same_item, score_scale):
    scores = jnp.einsum("qhd,khd->hqk", query_low, key_low, preferred_element_type=full)
    return jnp.where(same_item, scores * score_scale, -1e30)


def make_plain(dp_size, fsdp_size):
    def per_device(
        patches,
        conditions,
        segment_ids,
        grid_coords,
        mod_weight,
        mod_bias,
        qkv_weight,
        qkv_bias,
        qk_gains,
        proj_weight,
        proj_bias,
        up_weight,
        up_bias,
        down_weight,
        down_bias,
        out_cotangent,
    ):
        row_count, model_width = patches.shape
        slots = conditions.shape[0]
        spans = row_count // SPAN
        head_size = model_width // HEADS
        score_scale = head_size ** (-0.5)
        head_shape = (row_count, HEADS, head_size)
        dp_index = lax.axis_index("dp")
        mod_rows, mod_cols = mod_weight.shape

        qkv_full = gather_weight(qkv_weight, dp_size, fsdp_size)
        proj_full = gather_weight(proj_weight, dp_size, fsdp_size)
        up_full = gather_weight(up_weight, dp_size, fsdp_size)
        down_full = gather_weight(down_weight, dp_size, fsdp_size)

        gain_cols = qk_gains.shape[1]
        sizes = [qkv_bias.shape[0], proj_bias.shape[0], up_bias.shape[0], down_bias.shape[0]]
        vector = jnp.concatenate(
            [qkv_bias, proj_bias, up_bias, down_bias, qk_gains[0], qk_gains[1]]
        )
        vectors = gather_small(vector[None], "fsdp", fsdp_size).astype(full)
        bounds = [0]
        for size in sizes + [gain_cols, gain_cols]:
            bounds.append(bounds[-1] + size)
        pieces = [vectors[:, bounds[k] : bounds[k + 1]] for k in range(6)]
        qkv_vector, proj_vector, up_vector, down_vector, gain_q, gain_k = [
            p.reshape(-1) for p in pieces
        ]

        cond_full = conditions.astype(full)
        silu_low = jax.nn.silu(cond_full).astype(low)
        silu_all = gather_small(
            gather_small(silu_low[None], "fsdp", fsdp_size)[None], "dp", dp_size
        ).reshape(dp_size * fsdp_size * slots, model_width)
        silu_cols = lax.dynamic_slice_in_dim(silu_all, dp_index * mod_rows, mod_rows, axis=1)
        mod_part = dot(silu_cols, mod_weight).reshape(dp_size, fsdp_size, slots, mod_cols)
        mod_sum = scatter_sum_small(mod_part, "dp", dp_size)[0] + mod_bias.astype(full)
        modulation = exchange_small(mod_sum, "fsdp", fsdp_size)
        modulation = modulation.transpose(1, 0, 2).reshape(slots, fsdp_size * mod_cols)
        span_ids = segment_ids.reshape(spans, SPAN)[:, 0]
        span_hot = (span_ids[:, None] == jnp.arange(slots, dtype=jnp.int32)[None, :]).astype(full)
        span_mod = jnp.sum(span_hot[:, :, None] * modulation[None], axis=1)

        def per_row(k):
            part = span_mod[:, k * model_width : (k + 1) * model_width]
            return jnp.broadcast_to(part[:, None, :], (spans, SPAN, model_width)).reshape(
                row_count, model_width
            )

        shift_attn, scale_attn, gate_attn, shift_ffn, scale_ffn, gate_ffn = map(per_row, range(6))

        def cols_of(blocks):
            return jnp.concatenate(blocks, axis=1)

        def forward_dot(rows_low, weight_full):
            return cols_of([dot(rows_low, weight_full[j]) for j in range(fsdp_size)])

        def split(values):
            width = values.shape[1] // fsdp_size
            return [values[:, j * width : (j + 1) * width] for j in range(fsdp_size)]

        def backward_dot(grad_low, weight_full):
            parts = split(grad_low)
            total = dot_t(parts[0], weight_full[0])
            for j in range(1, fsdp_size):
                total = total + dot_t(parts[j], weight_full[j])
            return total

        def weight_grad(rows_low, grad_low):
            return scatter_grad(
                [outer_grad(rows_low, part).astype(low) for part in split(grad_low)], dp_size
            )

        tables = rotary_tables(grid_coords, head_size // 4)
        patch_full = patches.astype(full)
        scale_one = rms_scale(patch_full)
        normed_one = patch_full * scale_one
        hidden_one = (normed_one * (1.0 + scale_attn) + shift_attn).astype(low)
        qkv_rows = forward_dot(hidden_one, qkv_full) + qkv_vector
        query_raw = qkv_rows[:, 0:model_width].reshape(head_shape)
        key_raw = qkv_rows[:, model_width : 2 * model_width].reshape(head_shape)
        value_low = qkv_rows[:, 2 * model_width :].reshape(head_shape).astype(low)
        query_scale = rms_scale(query_raw)
        query_unit = query_raw * query_scale
        key_scale = rms_scale(key_raw)
        key_unit = key_raw * key_scale
        query_low = rotate(query_unit * gain_q, tables, 1.0).astype(low)
        key_low = rotate(key_unit * gain_k, tables, 1.0).astype(low)
        same_item = (segment_ids[:, None] == segment_ids[None, :])[None]
        scores = masked_scores(query_low, key_low, same_item, score_scale)
        exponentials = jnp.exp(scores - jnp.max(scores, axis=-1, keepdims=True))
        probs = exponentials / jnp.sum(exponentials, axis=-1, keepdims=True)
        probs_low = probs.astype(low)
        attended_low = (
            jnp.einsum("hqk,khd->qhd", probs_low, value_low, preferred_element_type=full)
            .reshape(row_count, model_width)
            .astype(low)
        )
        branch_attn = forward_dot(attended_low, proj_full) + proj_vector
        middle = patch_full + gate_attn * branch_attn
        scale_two = rms_scale(middle)
        normed_two = middle * scale_two
        hidden_two = (normed_two * (1.0 + scale_ffn) + shift_ffn).astype(low)
        gate_up = forward_dot(hidden_two, up_full) + up_vector
        hidden_units = gate_up.shape[1] // 2
        gate_part = gate_up[:, :hidden_units]
        up_part = gate_up[:, hidden_units:]
        gated_low = (jax.nn.silu(gate_part) * up_part).astype(low)
        branch_ffn = forward_dot(gated_low, down_full) + down_vector
        block_out = (middle + gate_ffn * branch_ffn).astype(low)

        grad_out = out_cotangent.astype(full)
        grad_gate_ffn = grad_out * branch_ffn
        grad_branch_ffn = (grad_out * gate_ffn).astype(low)
        down_bias_grad = jnp.sum(grad_branch_ffn.astype(full), axis=0)
        grad_gated = backward_dot(grad_branch_ffn, down_full)
        down_grad = weight_grad(gated_low, grad_branch_ffn)
        grad_gate_up = jnp.concatenate(
            [grad_gated * up_part * silu_slope(gate_part), grad_gated * jax.nn.silu(gate_part)],
            axis=1,
        ).astype(low)
        up_bias_grad = jnp.sum(grad_gate_up.astype(full), axis=0)
        grad_hidden_two = backward_dot(grad_gate_up, up_full)
        up_grad = weight_grad(hidden_two, grad_gate_up)
        grad_middle = grad_out + norm_backward(
            grad_hidden_two * (1.0 + scale_ffn), normed_two, scale_two
        )
        grad_gate_attn = grad_middle * branch_attn
        grad_branch_attn = (grad_middle * gate_attn).astype(low)
        proj_bias_grad = jnp.sum(grad_branch_attn.astype(full), axis=0)
        grad_attended = backward_dot(grad_branch_attn, proj_full).astype(low).reshape(head_shape)
        proj_grad = weight_grad(attended_low, grad_branch_attn)
        grad_probs = jnp.einsum(
            "qhd,khd->hqk", grad_attended, value_low, preferred_element_type=full
        )
        row_dot = jnp.sum(probs * grad_probs, axis=-1, keepdims=True)
        grad_scores = (probs * (grad_probs - row_dot)).astype(low)
        grad_values = jnp.einsum(
            "hqk,qhd->khd", probs_low, grad_attended, preferred_element_type=full
        )
        grad_query_rot = score_scale * jnp.einsum(
            "hqk,khd->qhd", grad_scores, key_low, preferred_element_type=full
        )
        grad_key_rot = score_scale * jnp.einsum(
            "hqk,qhd->khd", grad_scores, query_low, preferred_element_type=full
        )
        back_query = rotate(grad_query_rot, tables, -1.0)
        back_key = rotate(grad_key_rot, tables, -1.0)
        gain_q_grad = jnp.sum(back_query * query_unit, axis=(0, 1))
        gain_k_grad = jnp.sum(back_key * key_unit, axis=(0, 1))
        grad_query_raw = norm_backward(back_query * gain_q, query_unit, query_scale)
        grad_key_raw = norm_backward(back_key * gain_k, key_unit, key_scale)
        grad_qkv = jnp.concatenate(
            [
                grad_query_raw.reshape(row_count, model_width),
                grad_key_raw.reshape(row_count, model_width),
                grad_values.reshape(row_count, model_width),
            ],
            axis=1,
        ).astype(low)
        qkv_grad = weight_grad(hidden_one, grad_qkv)
        qkv_bias_grad = jnp.sum(grad_qkv.astype(full), axis=0)
        grad_hidden_one = backward_dot(grad_qkv, qkv_full)
        patch_grad = (
            grad_middle + norm_backward(grad_hidden_one * (1.0 + scale_attn), normed_one, scale_one)
        ).astype(low)

        def span_sum(values):
            return jnp.sum(values.reshape(spans, SPAN, model_width), axis=1)

        grad_spans = jnp.concatenate(
            [
                span_sum(grad_hidden_one),
                span_sum(grad_hidden_one * normed_one),
                span_sum(grad_gate_attn),
                span_sum(grad_hidden_two),
                span_sum(grad_hidden_two * normed_two),
                span_sum(grad_gate_ffn),
            ],
            axis=1,
        )
        grad_modulation = jnp.sum(span_hot[:, :, None] * grad_spans[:, None, :], axis=0).astype(low)
        grad_mod = grad_modulation.reshape(slots, fsdp_size, mod_cols).transpose(1, 0, 2)
        grad_mod = exchange_small(grad_mod, "fsdp", fsdp_size)
        grad_mod = gather_small(grad_mod[None], "dp", dp_size).reshape(-1, mod_cols)
        mod_bias_grad = jnp.sum(grad_mod.astype(full), axis=0)
        mod_grad = outer_grad(silu_cols, grad_mod)
        cond_part = dot_t(grad_mod, mod_weight).reshape(dp_size, fsdp_size, slots, mod_rows)
        cond_part = scatter_sum_small(cond_part.transpose(1, 0, 2, 3), "fsdp", fsdp_size)[0]
        cond_part = exchange_small(cond_part, "dp", dp_size)
        cond_grad = (
            cond_part.transpose(1, 0, 2).reshape(slots, model_width) * silu_slope(cond_full)
        ).astype(low)

        rows = [qkv_bias_grad, proj_bias_grad, up_bias_grad, down_bias_grad, gain_q_grad, gain_k_grad]
        vector_grad = jnp.concatenate([r.reshape(fsdp_size, -1) for r in rows], axis=1)
        vector_grad = scatter_sum_small(vector_grad, "fsdp", fsdp_size)
        vector_grad = sum_small(vector_grad, "dp", dp_size)[0]
        out = [vector_grad[bounds[k] : bounds[k + 1]] for k in range(6)]
        return (
            block_out,
            patch_grad,
            cond_grad,
            mod_grad,
            mod_bias_grad,
            qkv_grad,
            out[0],
            jnp.stack([out[4], out[5]]),
            proj_grad,
            out[1],
            up_grad,
            out[2],
            down_grad,
            out[3],
        )

    return per_device


PLANE = 4


def cross(values, hop):
    return lax.ppermute(values, "dp", [(k, k ^ (2 * hop)) for k in range(2 * PLANE)])


def partner(values):
    return lax.ppermute(values, "dp", [(k, k ^ 1) for k in range(2 * PLANE)])


def along(values, hop, size):
    return lax.ppermute(values, "fsdp", [(k, k ^ hop) for k in range(size)])


def plane_blocks(values):
    return [values] + [cross(values, hop) for hop in range(1, PLANE)]


def plane_sum(blocks):
    total = blocks[0]
    for hop in range(1, PLANE):
        total = total + cross(blocks[hop].astype(low), hop).astype(full)
    return total


def z_blocks(values, index, size):
    blocks = jnp.stack([values] + [along(values, hop, size) for hop in range(1, size)])
    return xor_order(blocks, index, size)


def z_exchange(values, index, size):
    values = xor_order(values, index, size)
    moved = jnp.stack([values[0]] + [along(values[hop], hop, size) for hop in range(1, size)])
    return xor_order(moved, index, size)


def z_sum_own(values, index, size):
    values = xor_order(values, index, size)
    total = values[0].astype(full)
    for hop in range(1, size):
        total = total + along(values[hop], hop, size).astype(full)
    return total


class Place:
    def __init__(self, y, x, core, z):
        self.y, self.x, self.core, self.z = y, x, core, z
        self.chip = 2 * y + x
        self.dp = 2 * self.chip + core

    def hop(self, dy, dx, dc, dz):
        low_z, high_z = self.z % 2, self.z // 2
        low_z = 1 - low_z if dz & 1 else low_z
        high_z = 1 - high_z if dz & 2 else high_z
        return Place(
            1 - self.y if dy else self.y,
            1 - self.x if dx else self.x,
            1 - self.core if dc else self.core,
            2 * high_z + low_z,
        )


SELF = (0, 0, 0, 0)
PLANE_HOPS = [(0, 1, 0, 0), (1, 0, 0, 0), (1, 1, 0, 0)]
Z_HOPS = [(0, 0, 0, 1), (0, 0, 0, 2), (0, 0, 0, 3)]
CORE_HOP = (0, 0, 1, 0)
DP_HOPS = [(dy, dx, dc, 0) for dy in (0, 1) for dx in (0, 1) for dc in (0, 1)]
ALL_HOPS = [(dy, dx, dc, dz) for dz in range(4) for dy, dx, dc, _ in DP_HOPS]
GROUP_HOPS = [(dy, dx, 0, dz) for dz in range(4) for dy in (0, 1) for dx in (0, 1)]


def exchange(identity, inputs, out_shapes, plan):
    hops = []
    for move in plan:
        if move[0] != SELF and move[0] not in hops:
            hops.append(move[0])

    def kernel(*refs):
        ins, outs = refs[: len(inputs)], refs[len(inputs) : len(inputs) + len(out_shapes)]
        send, recv = refs[-2:]
        dp_index = lax.axis_index("dp")
        me = Place(dp_index // 4, (dp_index // 2) % 2, dp_index % 2, lax.axis_index("fsdp"))

        def target(hop):
            peer = me.hop(*hop)
            return peer, {"dp": peer.dp, "fsdp": peer.z}

        barrier = pltpu.get_barrier_semaphore()
        for hop in hops:
            pl.semaphore_signal(
                barrier, 1, device_id=target(hop)[1], device_id_type=pl.DeviceIdType.MESH
            )
        pl.semaphore_wait(barrier, len(hops))
        copies = []
        forwarded = set()
        for number, (hop, source, source_at, out, out_at, after) in enumerate(plan):
            peer, device = target(hop)
            src = (ins if after is None else outs)[source]
            src = src if source_at is None else src.at[source_at(me, peer)]
            dst = outs[out]
            dst = dst if out_at is None else dst.at[out_at(me, peer)]
            for earlier in after or ():
                if earlier not in forwarded:
                    if plan[earlier][0] == SELF:
                        copies[earlier].wait()
                    else:
                        copies[earlier].wait_recv()
                    forwarded.add(earlier)
            if hop == SELF:
                copy = pltpu.make_async_copy(src, dst, send.at[number])
            else:
                copy = pltpu.make_async_remote_copy(
                    src_ref=src,
                    dst_ref=dst,
                    send_sem=send.at[number],
                    recv_sem=recv.at[number],
                    device_id=device,
                    device_id_type=pl.DeviceIdType.MESH,
                )
            copy.start()
            copies.append(copy)
        for number, copy in enumerate(copies):
            if plan[number][0] == SELF:
                if number not in forwarded:
                    copy.wait()
                continue
            copy.wait_send()
            if number not in forwarded:
                copy.wait_recv()

    anywhere = pl.BlockSpec(memory_space=pl.ANY)
    return pl.pallas_call(
        kernel,
        out_shape=[jax.ShapeDtypeStruct(shape, dtype) for shape, dtype in out_shapes],
        in_specs=[anywhere] * len(inputs),
        out_specs=[anywhere] * len(out_shapes),
        scratch_shapes=[
            pltpu.SemaphoreType.DMA((len(plan),)),
            pltpu.SemaphoreType.DMA((len(plan),)),
        ],
        compiler_params=pltpu.CompilerParams(collective_id=identity, has_side_effects=True),
    )(*inputs)


def gather_moves(hops, source, out, out_at):
    return [(hop, source, None, out, out_at, None) for hop in hops]


def by_chip(me, peer):
    return (me.chip,)


def by_dp(me, peer):
    return (me.dp,)


def by_z(me, peer):
    return (me.z,)


def by_core(me, peer):
    return (me.core,)


def tie(first, second):
    return lax.optimization_barrier((first, second))


def put(values, own, *at):
    start = tuple(at) + (0,) * (values.ndim - len(at))
    return lax.dynamic_update_slice(values, own.reshape((1,) * len(at) + own.shape), start)


HOP_X, HOP_Y = PLANE_HOPS[0], PLANE_HOPS[1]


def relayed(source, out, place, first):
    def at(hop, half):
        return lambda me, peer: (place(me, hop), half)

    def onto(hop, half):
        return lambda me, peer: (place(peer, hop), half)

    def part(half):
        return lambda me, peer: (half,)

    diagonal = PLANE_HOPS[2]
    return [
        (HOP_X, source, part(0), out, onto(HOP_X, 0), None),
        (HOP_Y, source, part(1), out, onto(HOP_Y, 1), None),
        (HOP_X, source, part(1), out, onto(HOP_X, 1), None),
        (HOP_Y, source, part(0), out, onto(HOP_Y, 0), None),
        (HOP_Y, out, at(HOP_X, 0), out, onto(diagonal, 0), (first,)),
        (HOP_X, out, at(HOP_Y, 1), out, onto(diagonal, 1), (first + 1,)),
    ]


def chip_place(me, hop):
    return me.hop(*hop).chip


def hop_place(me, hop):
    return PLANE_HOPS.index(hop)


def slotted(hops, source, source_at, out):
    return [
        (hop, source, source_at, out, lambda me, peer, n=n: (n,), None)
        for n, hop in enumerate(hops)
    ]


def to_chip(me, peer):
    return (peer.chip,)


def to_z(me, peer):
    return (peer.z,)


LANES = 128


def head_of(values, number, head_size):
    part = values[:, number * head_size : (number + 1) * head_size]
    pad = jnp.zeros((values.shape[0], LANES - head_size), values.dtype)
    return jnp.concatenate([part, pad], axis=1)


def pair_of(values, head_size):
    quarter = head_size // 4
    lane = lax.broadcasted_iota(jnp.int32, values.shape, 1)
    second = (lane // quarter) % 2 == 1
    return jnp.where(
        second, pltpu.roll(values, quarter, 1), pltpu.roll(values, LANES - quarter, 1)
    )


def unit_of(raw, head_size):
    factor = lax.rsqrt(jnp.sum(raw * raw, axis=1, keepdims=True) * (1.0 / head_size) + epsilon)
    return raw * factor, factor


def head_probs(query, key, same, score_scale):
    scores = jnp.where(same, dot_t(query, key) * score_scale, -1e30)
    exponentials = jnp.exp(scores - jnp.max(scores, axis=1, keepdims=True))
    return exponentials * (1.0 / jnp.sum(exponentials, axis=1, keepdims=True))


def rotary_rows(head_size):
    quarter = head_size // 4
    frequencies = np.float32(10000.0) ** (-np.arange(quarter, dtype=np.float32) / quarter)
    angles = np.arange(SIDE, dtype=np.float32)[:, None] * frequencies.astype(np.float32)
    cosine = np.zeros((2, SIDE, LANES), np.float32)
    sine = np.zeros((2, SIDE, LANES), np.float32)
    for k in range(2):
        first = 2 * quarter * k
        cosine[k, :, first : first + 2 * quarter] = np.tile(np.cos(angles), (1, 2))
        sine[k, :, first : first + quarter] = -np.sin(angles)
        sine[k, :, first + quarter : first + 2 * quarter] = np.sin(angles)
    return jnp.asarray(cosine.reshape(-1, LANES)), jnp.asarray(sine.reshape(-1, LANES))


def rotary_of(meta, cosine_rows, sine_rows):
    place = lax.broadcasted_iota(jnp.int32, (meta.shape[0], 2 * SIDE), 1)
    hot = (meta[:, 1:2] == place) | (meta[:, 2:3] + SIDE == place)
    hot = hot.astype(full)
    take = functools.partial(jnp.dot, preferred_element_type=full, precision=lax.Precision.HIGHEST)
    return take(hot, cosine_rows), take(hot, sine_rows)


def attention_block(head_size, heads, refs):
    (rows, gains, cosine, sine, seg_row, seg_col) = refs
    same = seg_row == seg_col
    gain_q, gain_k = gains[0:1], gains[1:2]
    for h in range(heads):
        query_unit, query_factor = unit_of(head_of(rows, h, head_size), head_size)
        key_unit, key_factor = unit_of(head_of(rows, heads + h, head_size), head_size)
        query = query_unit * gain_q
        key = key_unit * gain_k
        query = (query * cosine + pair_of(query, head_size) * sine).astype(low)
        key = (key * cosine + pair_of(key, head_size) * sine).astype(low)
        value = head_of(rows, 2 * heads + h, head_size).astype(low)
        probs = head_probs(query, key, same, head_size ** (-0.5))
        yield query_unit, query_factor, key_unit, key_factor, query, key, value, probs


def fill_rows(target, mine, other):
    rows = mine.shape[1]
    core = lax.axis_index("dp") % 2
    for source, place in ((mine, core), (other, 1 - core)):
        target[pl.ds(pl.multiple_of(place * rows, 16), rows), :] = jnp.concatenate(
            [source[j] for j in range(source.shape[0])], axis=1
        )


def attention_forward_kernel(head_size, heads, *refs):
    (patch, shift, scale, weight, bias, gains, cos_rows, sin_rows, meta, seg_col) = refs[:10]
    proj_mine, proj_other = refs[10:12]
    hidden_out, rows_out, attended_out, terms_out, proj = refs[12:]

    @pl.when(pl.program_id(0) == 0)
    def _():
        fill_rows(proj, proj_mine, proj_other)

    cosine, sine = rotary_of(meta[0], cos_rows[...], sin_rows[...])
    values = patch[0].astype(full)
    count, width = values.shape
    normed = values * lax.rsqrt(jnp.mean(values * values, axis=1, keepdims=True) + epsilon)
    hidden = normed.reshape(count // SPAN, SPAN, width) * (1.0 + scale[0]) + shift[0]
    hidden = hidden.reshape(count, width).astype(low)
    hidden_out[0] = hidden
    rows = dot(hidden, weight[...]) + bias[...]
    rows_out[0] = rows
    pieces = []
    refs = (rows, gains[...], cosine, sine, meta[0, :, 0:1], seg_col[0])
    for *_, value, probs in attention_block(head_size, heads, refs):
        pieces.append(dot(probs.astype(low), value)[:, :head_size])
    attended = jnp.concatenate(pieces, axis=1).astype(low)
    attended_out[0] = attended
    terms_out[0] = dot(attended, proj[...]).astype(low)


def cut_columns(parts, total):
    cols = parts.shape[3]
    for j in range(parts.shape[0]):
        parts[j] = total[:, j * cols : (j + 1) * cols].astype(low).reshape(parts.shape[1:])


def attention_backward_kernel(head_size, heads, *refs):
    (grad, rows, weight, gains, cos_rows, sin_rows, meta, seg_col, proj) = refs[:9]
    hidden, attended = refs[9:11]
    terms_out, bias_out, gains_out, qkv_parts, proj_parts = refs[11:16]
    qkv_total, proj_total = refs[16:]

    @pl.when(pl.program_id(0) == 0)
    def _():
        bias_out[...] = jnp.zeros_like(bias_out)
        gains_out[...] = jnp.zeros_like(gains_out)
        qkv_total[...] = jnp.zeros_like(qkv_total)
        proj_total[...] = jnp.zeros_like(proj_total)

    score_scale = head_size ** (-0.5)
    gain_values = gains[...]
    cos_tab, sin_tab = rotary_of(meta[0], cos_rows[...], sin_rows[...])
    grad_attended = dot_t(grad[0], proj[...])
    values = rows[0]
    grad_queries, grad_keys, grad_values = [], [], []
    gain_sums = [jnp.zeros((1, LANES), full), jnp.zeros((1, LANES), full)]

    def raw_grad(rotated, unit, factor, which):
        back = rotated * cos_tab - pair_of(rotated, head_size) * sin_tab
        gain_sums[which] = gain_sums[which] + jnp.sum(back * unit, axis=0, keepdims=True)
        turned = back * gain_values[which : which + 1]
        mean = jnp.sum(turned * unit, axis=1, keepdims=True) * (1.0 / head_size)
        return ((turned - unit * mean) * factor)[:, :head_size]

    refs = (values, gain_values, cos_tab, sin_tab, meta[0, :, 0:1], seg_col[0])
    for h, parts in enumerate(attention_block(head_size, heads, refs)):
        query_unit, query_factor, key_unit, key_factor, query, key, value, probs = parts
        grad_head = head_of(grad_attended, h, head_size).astype(low)
        grad_probs = dot_t(grad_head, value)
        row_dot = jnp.sum(probs * grad_probs, axis=1, keepdims=True)
        grad_scores = (probs * (grad_probs - row_dot)).astype(low)
        grad_values.append(outer_grad(probs.astype(low), grad_head)[:, :head_size])
        grad_queries.append(
            raw_grad(dot(grad_scores, key) * score_scale, query_unit, query_factor, 0)
        )
        grad_keys.append(
            raw_grad(outer_grad(grad_scores, query) * score_scale, key_unit, key_factor, 1)
        )
    result = jnp.concatenate(grad_queries + grad_keys + grad_values, axis=1).astype(low)
    bias_out[...] += jnp.sum(result.astype(full), axis=0, keepdims=True)
    gains_out[0:1, :] += gain_sums[0]
    gains_out[1:2, :] += gain_sums[1]
    terms_out[0] = dot_t(result, weight[...]).astype(low)
    qkv_total[...] += outer_grad(hidden[0], result)
    proj_total[...] += outer_grad(attended[0], grad[0])

    @pl.when(pl.program_id(0) == pl.num_programs(0) - 1)
    def _():
        qkv_parts[...] = qkv_total[...].astype(low).reshape(qkv_parts.shape)
        cut_columns(proj_parts, proj_total[...])


def ffn_kernel(*refs):
    (own_hidden, hiddens, own_cot, cots, gate, up, down_mine, down_other, bias) = refs[:9]
    hidden_terms, ffn_terms, bias_out, up_parts, down_parts = refs[9:14]
    down, up_total, down_total = refs[14:]
    step = pl.program_id(0)

    @pl.when(step == 0)
    def _():
        bias_out[...] = jnp.zeros_like(bias_out)
        up_total[...] = jnp.zeros_like(up_total)
        down_total[...] = jnp.zeros_like(down_total)
        fill_rows(down, down_mine, down_other)

    count, width = own_hidden.shape
    units = down.shape[0]
    hidden = jnp.where(step == 0, own_hidden[...], hiddens[0])
    cot = jnp.where(step == 0, own_cot[...], cots[0])
    grad_branch = cot.astype(full).reshape(count // SPAN, SPAN, width) * gate[0]
    grad_branch = grad_branch.reshape(count, width).astype(low)
    grad_gated = dot_t(grad_branch, down[...])
    gate_up = dot(hidden, up[...]) + bias[...]
    gate_part, up_part = gate_up[:, :units], gate_up[:, units:]
    sigmoid = jax.nn.sigmoid(gate_part)
    silu = gate_part * sigmoid
    gated = (silu * up_part).astype(low)
    slope = sigmoid * (1.0 + gate_part * (1.0 - sigmoid))
    grad_gate = (grad_gated * up_part * slope).astype(low)
    grad_up = (grad_gated * silu).astype(low)
    grads = jnp.concatenate([grad_gate, grad_up], axis=1)
    bias_out[...] += jnp.sum(grads.astype(full), axis=0, keepdims=True)
    hidden_terms[0] = dot_t(grads, up[...]).astype(low)
    ffn_terms[0] = dot(gated, down[...]).astype(low)
    up_total[...] += outer_grad(hidden, grads)
    down_total[...] += outer_grad(gated, grad_branch)

    @pl.when(step == pl.num_programs(0) - 1)
    def _():
        up_parts[...] = up_total[...].astype(low).reshape(up_parts.shape)
        cut_columns(down_parts, down_total[...])


def split_kernel(groups, source, target):
    count, _, cols = source.shape
    part = cols // groups
    for p in range(count):
        pieces = []
        for t in range(groups):
            block, at = divmod(t * count + p, groups)
            pieces.append(source[block, :, at * part : (at + 1) * part])
        target[p] = jnp.concatenate(pieces, axis=1)


def merge_kernel(groups, source, target):
    count, _, cols = source.shape
    part = cols // groups
    for z in range(count):
        pieces = []
        for at in range(groups):
            t, p = divmod(z * groups + at, count)
            pieces.append(source[p, :, t * part : (t + 1) * part])
        target[z] = jnp.concatenate(pieces, axis=1)


def whole_call(kernel, values):
    return pl.pallas_call(kernel, out_shape=jax.ShapeDtypeStruct(values.shape, values.dtype))(values)


def block_call(kernel, inputs, blocked, out_blocks, out_whole, scratch, steps, flops):
    def block_spec(shape, mark=1):
        tail = (0,) * (len(shape) - 1)
        if mark == 2:
            return pl.BlockSpec((1,) + shape[1:], lambda p: (jnp.maximum(p - 1, 0),) + tail)
        return pl.BlockSpec((1,) + shape[1:], lambda p: (p,) + tail)

    def whole_spec(shape):
        return pl.BlockSpec(shape, lambda p: (0,) * len(shape))

    return pl.pallas_call(
        kernel,
        grid=(steps,),
        out_shape=[jax.ShapeDtypeStruct(*o) for o in out_blocks + out_whole],
        in_specs=[
            block_spec(v.shape, b) if b else whole_spec(v.shape) for v, b in zip(inputs, blocked)
        ],
        out_specs=[block_spec(o[0]) for o in out_blocks] + [whole_spec(o[0]) for o in out_whole],
        scratch_shapes=[pltpu.VMEM(*o) for o in scratch],
        cost_estimate=pl.CostEstimate(
            flops=flops,
            bytes_accessed=sum(v.size * v.dtype.itemsize for v in inputs),
            transcendentals=flops // 1024,
        ),
    )(*inputs)


def make_plane(z_size):
    def per_device(
        patches,
        conditions,
        segment_ids,
        grid_coords,
        mod_weight,
        mod_bias,
        qkv_weight,
        qkv_bias,
        qk_gains,
        proj_weight,
        proj_bias,
        up_weight,
        up_bias,
        down_weight,
        down_bias,
        out_cotangent,
    ):
        row_count, width = patches.shape
        slots = conditions.shape[0]
        spans = row_count // SPAN
        head_size = width // HEADS
        heads = HEADS // PLANE
        part_cols = width // PLANE
        score_scale = head_size ** (-0.5)
        dp_index = lax.axis_index("dp")
        z_index = lax.axis_index("fsdp")
        chip = dp_index >> 1
        core = dp_index & 1
        upper = core == 1
        mod_rows, mod_cols = mod_weight.shape
        rows_all = PLANE * row_count
        shard = qkv_weight.shape[0]

        def halves(values):
            return values.reshape(2, row_count // 2, width)

        def core_order(mine, other):
            return jnp.where(upper, other, mine), jnp.where(upper, mine, other)

        cond_full = conditions.astype(full)
        silu_low = jax.nn.silu(cond_full).astype(low)
        vector = jnp.concatenate(
            [qkv_bias, proj_bias, up_bias, down_bias, qk_gains[0], qk_gains[1]]
        )[None]
        meta = jnp.concatenate([segment_ids[None], grid_coords], axis=0)
        cols_qkv = qkv_weight.shape[1]
        cols_proj = proj_weight.shape[1]
        plan = gather_moves(Z_HOPS + [SELF], 0, 0, lambda me, peer: (me.dp, me.z))
        plan += gather_moves(Z_HOPS, 1, 1, by_z)
        plan += gather_moves(Z_HOPS, 3, 3, by_z)
        plan += gather_moves(Z_HOPS + [SELF], 4, 4, by_z)
        plan += gather_moves(PLANE_HOPS + [SELF], 5, 5, by_chip)
        plan += [(hop, 0, by_dp, 0, by_dp, (0, 1, 2, 3)) for hop in DP_HOPS if hop != SELF]
        plan += relayed(2, 2, chip_place, len(plan))
        silu_all, qkv_z, patch_all, proj_z, vectors, meta_all = exchange(
            1,
            [silu_low, qkv_weight, halves(patches), proj_weight, vector, meta],
            [
                ((2 * PLANE, z_size, slots, width), low),
                ((z_size, shard, cols_qkv), low),
                ((PLANE, 2, row_count // 2, width), low),
                ((z_size, shard, cols_proj), low),
                ((z_size,) + vector.shape, low),
                ((PLANE,) + meta.shape, jnp.int32),
            ],
            plan,
        )

        qkv_z, up_later = tie(qkv_z, up_weight)
        up_z = lax.all_gather(up_later, "fsdp", axis=0, tiled=False)
        qkv_z = put(qkv_z, qkv_weight, z_index)
        proj_z = put(proj_z, proj_weight, z_index)
        patch_all = put(patch_all.reshape(PLANE, row_count, width), patches, chip)

        silu_all = silu_all.reshape(-1, width)
        silu_cols = lax.dynamic_slice_in_dim(silu_all, dp_index * mod_rows, mod_rows, axis=1)
        mod_part = dot(silu_cols, mod_weight).reshape(2 * PLANE, z_size * slots, mod_cols)
        qkv_pieces = whole_call(functools.partial(split_kernel, 3), qkv_z)
        plan = [
            (hop, 0, to_chip, 0, by_dp, None) for hop in PLANE_HOPS
        ]
        plan += [
            (hop, 1, lambda me, peer: (peer.dp,), 1, lambda me, peer: (me.dp,), None)
            for hop in DP_HOPS
            if hop != SELF
        ]
        plan.append((CORE_HOP, 2, None, 2, None, None))
        for number, (dy, dx, dc, dz) in enumerate(PLANE_HOPS):
            from_hop = lambda me, peer, dy=dy, dx=dx: (me.hop(dy, dx, 0, 0).dp,)
            plan.append((CORE_HOP, 0, from_hop, 0, from_hop, (number,)))
        plan.append((CORE_HOP, 0, by_chip, 0, by_dp, None))
        qkv_slice, mod_parts, proj_other = exchange(
            2,
            [qkv_pieces, mod_part, proj_z],
            [
                ((2 * PLANE, shard, 3 * part_cols), low),
                (mod_part.shape, full),
                (proj_z.shape, low),
            ],
            plan,
        )
        qkv_slice = put(
            qkv_slice, lax.dynamic_index_in_dim(qkv_pieces, chip, 0, keepdims=False), dp_index
        )
        mod_parts = put(
            mod_parts, lax.dynamic_index_in_dim(mod_part, dp_index, 0, keepdims=False), dp_index
        )
        qkv_slice = qkv_slice.reshape(-1, 3 * part_cols)
        mod_sum = (jnp.sum(mod_parts, axis=0) + mod_bias.astype(full)).reshape(
            z_size, slots, mod_cols
        )
        plan = [
            (hop, 0, to_z, 0, lambda me, peer: (me.chip, me.z), None) for hop in Z_HOPS + [SELF]
        ]
        plan += [(hop, 0, by_chip, 0, by_chip, (0, 1, 2, 3)) for hop in PLANE_HOPS]
        (group_mod,) = exchange(
            3, [mod_sum], [((PLANE, z_size, slots, mod_cols), full)], plan
        )
        group_mod = group_mod.transpose(0, 2, 1, 3).reshape(PLANE, slots, z_size * mod_cols)
        modulation = lax.dynamic_index_in_dim(group_mod, chip, 0, keepdims=False)

        group_mod, (cot_later, up_z) = tie(group_mod, (out_cotangent, up_z))
        cot_blocks = [cross(cot_later, hop) for hop in range(1, PLANE)]
        units = up_weight.shape[1] // 2

        def up_piece(hop):
            to = chip ^ hop
            parts = []
            for t in range(2):
                block = lax.dynamic_index_in_dim(up_z, 2 * t + (to >> 1), 0, keepdims=False)
                parts.append(jnp.where((to & 1) == 1, block[:, units:], block[:, :units]))
            return jnp.concatenate(parts, axis=1)

        up_blocks = [up_piece(0)] + [cross(up_piece(hop), hop) for hop in range(1, PLANE)]
        segments = meta_all[:, 0].reshape(-1)
        meta_rows = meta_all.transpose(0, 2, 1)
        seg_col = meta_all[:, 0][:, None, :]
        cos_rows, sin_rows = rotary_rows(head_size)

        gain_cols = qk_gains.shape[1]
        sizes = [qkv_bias.shape[0], proj_bias.shape[0], up_bias.shape[0], down_bias.shape[0]]
        vectors = vectors[:, 0].astype(full)
        bounds = [0]
        for size in sizes + [gain_cols, gain_cols]:
            bounds.append(bounds[-1] + size)
        pieces = [vectors[:, bounds[k] : bounds[k + 1]] for k in range(6)]
        qkv_vector, proj_vector, up_vector, down_vector, gain_q, gain_k = [
            p.reshape(-1) for p in pieces
        ]

        def own_columns(flat, groups):
            parts = flat.reshape(groups, PLANE, -1)
            return lax.dynamic_slice_in_dim(parts, chip, 1, axis=1).reshape(-1)

        seg_spans = segments.reshape(PLANE, spans, SPAN)[:, :, 0]
        hot = (seg_spans[:, :, None] == jnp.arange(slots, dtype=jnp.int32)).astype(full)
        group_spans = jnp.sum(hot[:, :, :, None] * group_mod[:, None], axis=2)
        own_spans_ids = segment_ids.reshape(spans, SPAN)[:, 0]
        own_hot = (own_spans_ids[:, None] == jnp.arange(slots, dtype=jnp.int32)).astype(full)
        own_spans = jnp.sum(own_hot[:, :, None] * modulation[None], axis=1)

        def spread(values):
            count = values.shape[0]
            return jnp.broadcast_to(values[:, None, :], (count, SPAN, width)).reshape(
                count * SPAN, width
            )

        def per_row(k):
            return spread(own_spans[:, k * width : (k + 1) * width])

        def per_row_all(k):
            return spread(
                group_spans[:, :, k * width : (k + 1) * width].reshape(PLANE * spans, width)
            )

        def core_swap(source, out, count):
            return [
                (
                    CORE_HOP,
                    source,
                    lambda me, peer, k=k: (k, peer.core),
                    out,
                    lambda me, peer, k=k: (k,),
                    None,
                )
                for k in range(count)
            ]

        def half_of(parts):
            return ((parts.shape[0],) + parts.shape[2:], low)

        def sum_cores(parts, other):
            mine = jnp.where(upper, parts[:, 1], parts[:, 0])
            return (mine.astype(full) + other.astype(full)).astype(low)

        def own_of(values, index):
            return lax.dynamic_index_in_dim(values, index, 0, keepdims=False)

        def z_sum_of(blocks, sent):
            return block_sum(blocks, own_of(sent, z_index))

        def plane_gather(identity, values, *more):
            (out,) = exchange(
                identity,
                [values],
                [((PLANE,) + values.shape, low)],
                gather_moves(PLANE_HOPS, 0, 0, by_chip),
            )
            return put(out, values, chip).reshape(rows_all, width)

        scatter_plan = slotted(PLANE_HOPS, 0, to_chip, 0)
        others = (PLANE - 1, row_count, width)

        def plane_scatter(values):
            return values.astype(low).reshape(PLANE, row_count, width)

        def block_sum(blocks, own):
            return own.astype(full) + jnp.sum(blocks.astype(full), axis=0)

        def plane_sum_of(blocks, sent):
            return block_sum(blocks, lax.dynamic_index_in_dim(sent, chip, 0, keepdims=False))

        def group_span(k):
            return group_spans[:, :, None, k * width : (k + 1) * width]

        gain_pad = jnp.zeros((2, LANES), full)
        gains = lax.dynamic_update_slice(gain_pad, jnp.stack([gain_q, gain_k]), (0, 0))
        hidden_one, qkv_rows, attended_low, attn_terms, proj_slice = block_call(
            functools.partial(attention_forward_kernel, head_size, heads),
            [
                patch_all,
                group_span(0),
                group_span(1),
                qkv_slice,
                own_columns(qkv_vector, 3)[None],
                gains,
                cos_rows,
                sin_rows,
                meta_rows,
                seg_col,
                proj_z,
                proj_other,
            ],
            [1, 1, 1, 0, 0, 0, 0, 0, 1, 1, 0, 0],
            [
                ((PLANE, row_count, width), low),
                ((PLANE, row_count, 3 * part_cols), full),
                ((PLANE, row_count, part_cols), low),
                ((PLANE, row_count, width), low),
            ],
            [((part_cols, width), low)],
            [],
            PLANE,
            rows_all * width * 8 * part_cols,
        )
        attn_terms, (cot_blocks, up_blocks) = tie(attn_terms, (cot_blocks, up_blocks))
        plan = scatter_plan + gather_moves(Z_HOPS, 1, 1, by_z)
        for number, hop in enumerate([SELF] + PLANE_HOPS):
            plan.append(
                (CORE_HOP, 2 + number, None, 2, lambda me, peer, hop=hop: (me.hop(*hop).dp,), None)
            )
        branch_blocks, down_z, up_slice = exchange(
            4,
            [attn_terms, down_weight] + up_blocks,
            [
                (others, low),
                ((z_size,) + down_weight.shape, low),
                ((2 * PLANE,) + up_weight.shape, low),
            ],
            plan,
        )
        for hop in range(PLANE):
            up_slice = put(up_slice, up_blocks[hop], dp_index ^ (2 * hop))
        up_slice = up_slice.reshape(-1, up_weight.shape[1])
        down_z = put(down_z, down_weight, z_index)
        branch_attn = plane_sum_of(branch_blocks, attn_terms) + proj_vector

        patch_full = patches.astype(full)
        scale_one = rms_scale(patch_full)
        normed_one = patch_full * scale_one
        middle = patch_full + per_row(2) * branch_attn
        scale_two = rms_scale(middle)
        normed_two = middle * scale_two
        hidden_two = (normed_two * (1.0 + per_row(4)) + per_row(3)).astype(low)

        hidden_blocks, down_other = exchange(
            5,
            [halves(hidden_two), down_z],
            [((PLANE - 1, 2, row_count // 2, width), low), (down_z.shape, low)],
            relayed(0, 0, hop_place, 0) + [(CORE_HOP, 1, None, 1, None, None)],
        )
        gate_spans = xor_order(group_spans[:, :, 5 * width :], chip, PLANE)
        hidden_two_terms, ffn_terms, up_bias_cols, up_parts, down_parts = block_call(
            ffn_kernel,
            [
                hidden_two,
                hidden_blocks.reshape(others),
                out_cotangent,
                jnp.stack(cot_blocks),
                gate_spans[:, :, None],
                up_slice,
                down_z,
                down_other,
                own_columns(up_vector, 2)[None],
            ],
            [0, 2, 0, 2, 1, 0, 0, 0, 0],
            [((PLANE, row_count, width), low), ((PLANE, row_count, width), low)],
            [
                ((1, 2 * units), full),
                ((PLANE, 2, shard, 2 * units), low),
                ((z_size, 2) + down_weight.shape, low),
            ],
            [((units, width), low), ((width, 2 * units), full), ((units, width), full)],
            PLANE,
            rows_all * width * 18 * units,
        )
        hop_scatter = [
            (hop, 0, lambda me, peer, n=n: (n + 1,), 0, lambda me, peer, n=n: (n,), None)
            for n, hop in enumerate(PLANE_HOPS)
        ]
        hidden_two_blocks, down_other, up_other = exchange(
            6,
            [hidden_two_terms, down_parts, up_parts],
            [(others, low), half_of(down_parts), half_of(up_parts)],
            hop_scatter + core_swap(1, 1, z_size) + core_swap(2, 2, PLANE),
        )
        grad_hidden_two = block_sum(hidden_two_blocks, hidden_two_terms[0])
        down_mine = sum_cores(down_parts, down_other)
        up_mine = sum_cores(up_parts, up_other)

        grad_out = out_cotangent.astype(full)
        own_gbf = (grad_out * per_row(5)).astype(low).astype(full)
        down_bias_grad = jnp.sum(own_gbf, axis=0)
        grad_middle = grad_out + norm_backward(
            grad_hidden_two * (1.0 + per_row(4)), normed_two, scale_two
        )
        grad_gate_attn = grad_middle * branch_attn
        grad_branch_attn = (grad_middle * per_row(2)).astype(low)
        proj_bias_grad = jnp.sum(grad_branch_attn.astype(full), axis=0)
        grad_branch_all, down_blocks = exchange(
            7,
            [halves(grad_branch_attn), down_mine],
            [
                ((PLANE, 2, row_count // 2, width), low),
                ((z_size - 1,) + down_mine.shape[1:], low),
            ],
            relayed(0, 0, chip_place, 0) + slotted(Z_HOPS, 1, to_z, 1),
        )
        grad_branch_all = put(
            grad_branch_all.reshape(PLANE, row_count, width), grad_branch_attn, chip
        )
        down_grad = z_sum_of(down_blocks, down_mine)

        grad_branch_all, (ffn_terms, up_mine) = tie(grad_branch_all, (ffn_terms, up_mine))
        ffn_blocks = [cross(ffn_terms[hop], hop) for hop in range(1, PLANE)]
        up_moved = [cross(own_of(up_mine, chip ^ hop), hop) for hop in range(1, PLANE)]

        hidden_one_terms, qkv_bias_cols, gain_grads, qkv_parts, proj_parts = block_call(
            functools.partial(attention_backward_kernel, head_size, heads),
            [
                grad_branch_all,
                qkv_rows,
                qkv_slice,
                gains,
                cos_rows,
                sin_rows,
                meta_rows,
                seg_col,
                proj_slice,
                hidden_one,
                attended_low,
            ],
            [1, 1, 0, 0, 0, 0, 1, 1, 0, 1, 1],
            [((PLANE, row_count, width), low)],
            [
                ((1, 3 * part_cols), full),
                ((2, LANES), full),
                ((PLANE, 2, shard, 3 * part_cols), low),
                ((z_size, 2) + proj_weight.shape, low),
            ],
            [((width, 3 * part_cols), full), ((part_cols, width), full)],
            PLANE,
            rows_all * width * 18 * part_cols,
        )
        gain_q_grad, gain_k_grad = gain_grads[0, :head_size], gain_grads[1, :head_size]
        hidden_one_terms, (ffn_blocks, up_moved) = tie(hidden_one_terms, (ffn_blocks, up_moved))
        up_moved = [own_of(up_mine, chip)] + up_moved

        def up_columns(p, t):
            parts = [v[:, t * units : (t + 1) * units] for v in up_moved]
            odd, high = ((chip ^ p) & 1) == 1, ((chip ^ p) & 2) == 2
            return jnp.where(
                high, jnp.where(odd, parts[3], parts[2]), jnp.where(odd, parts[1], parts[0])
            )

        up_wide = jnp.stack(
            [
                jnp.concatenate([up_columns(p, t), up_columns(p + 1, t)], axis=1)
                for t in range(2)
                for p in (0, 2)
            ]
        )
        up_grad = lax.psum_scatter(up_wide, "fsdp", scatter_dimension=0, tiled=False).astype(full)
        hidden_one_blocks, qkv_other, proj_other = exchange(
            8,
            [hidden_one_terms, qkv_parts, proj_parts],
            [(others, low), half_of(qkv_parts), half_of(proj_parts)],
            scatter_plan + core_swap(1, 1, PLANE) + core_swap(2, 2, z_size),
        )
        grad_hidden_one = plane_sum_of(hidden_one_blocks, hidden_one_terms)
        branch_ffn = ffn_terms[0].astype(full) + down_vector
        for block in ffn_blocks:
            branch_ffn = branch_ffn + block.astype(full)
        block_out = (middle + per_row(5) * branch_ffn).astype(low)
        grad_gate_ffn = grad_out * branch_ffn
        qkv_mine = sum_cores(qkv_parts, qkv_other)
        proj_mine = sum_cores(proj_parts, proj_other)
        patch_grad = (
            grad_middle + norm_backward(grad_hidden_one * (1.0 + per_row(1)), normed_one, scale_one)
        ).astype(low)

        def span_sum(values):
            return jnp.sum(values.reshape(spans, SPAN, width), axis=1)

        grad_spans = jnp.concatenate(
            [
                span_sum(grad_hidden_one),
                span_sum(grad_hidden_one * normed_one),
                span_sum(grad_gate_attn),
                span_sum(grad_hidden_two),
                span_sum(grad_hidden_two * normed_two),
                span_sum(grad_gate_ffn),
            ],
            axis=1,
        )
        grad_modulation = jnp.sum(own_hot[:, :, None] * grad_spans[:, None, :], axis=0).astype(low)
        grad_mod = grad_modulation.reshape(slots, z_size, mod_cols).transpose(1, 0, 2)

        def place(flat, groups):
            spot = (jnp.arange(PLANE) == chip).astype(full)
            return (flat.reshape(groups, 1, -1) * spot[None, :, None]).reshape(-1)

        rows = [
            place(qkv_bias_cols, 3),
            proj_bias_grad,
            place(up_bias_cols, 2),
            down_bias_grad,
            gain_q_grad,
            gain_k_grad,
        ]
        vector_grad = jnp.concatenate([r.reshape(z_size, 1, -1) for r in rows], axis=2)
        plan = [
            (hop, 1, to_z, 1, lambda me, peer: (me.dp, me.z), None) for hop in Z_HOPS + [SELF]
        ]
        plan += [(hop, 2, to_z, 2, by_z, None) for hop in Z_HOPS + [SELF]]
        plan += [(hop, 0, to_chip, 0, by_chip, None) for hop in PLANE_HOPS]
        plan += [(hop, 1, by_dp, 1, by_dp, (0, 1, 2, 3)) for hop in DP_HOPS if hop != SELF]
        plan += slotted(Z_HOPS, 3, to_z, 3)
        qkv_moved, grad_mod, vector_parts, proj_blocks = exchange(
            9,
            [qkv_mine, grad_mod, vector_grad, proj_mine],
            [
                (qkv_mine.shape, low),
                ((2 * PLANE, z_size, slots, mod_cols), low),
                (vector_grad.shape, full),
                ((z_size - 1,) + proj_mine.shape[1:], low),
            ],
            plan,
        )
        proj_grad = z_sum_of(proj_blocks, proj_mine)
        qkv_wide = whole_call(
            functools.partial(merge_kernel, 3), put(qkv_moved, own_of(qkv_mine, chip), chip)
        )
        grad_mod = grad_mod.reshape(-1, mod_cols)
        vector_sum = jnp.sum(vector_parts, axis=0)
        cond_part = dot_t(grad_mod, mod_weight).reshape(2 * PLANE, z_size, slots, mod_rows)
        plan = slotted(Z_HOPS, 0, to_z, 0)
        plan += [
            (
                hop,
                1,
                lambda me, peer: (peer.dp, peer.z),
                1,
                lambda me, peer: (me.dp, me.z),
                None,
            )
            for hop in ALL_HOPS
        ]
        plan += gather_moves(DP_HOPS, 2, 2, by_dp)
        qkv_blocks, cond_parts, vector_parts = exchange(
            10,
            [qkv_wide, cond_part, vector_sum],
            [
                ((z_size - 1,) + qkv_wide.shape[1:], low),
                (cond_part.shape, full),
                ((2 * PLANE,) + vector_sum.shape, full),
            ],
            plan,
        )
        qkv_grad = z_sum_of(qkv_blocks, qkv_wide)
        mod_bias_grad = jnp.sum(grad_mod.astype(full), axis=0)
        mod_grad = outer_grad(silu_cols, grad_mod)
        cond_part = jnp.sum(cond_parts, axis=1)
        cond_grad = (
            cond_part.transpose(1, 0, 2).reshape(slots, width) * silu_slope(cond_full)
        ).astype(low)
        vector_grad = jnp.sum(vector_parts, axis=0)[0]
        out = [vector_grad[bounds[k] : bounds[k + 1]] for k in range(6)]
        return (
            block_out,
            patch_grad,
            cond_grad,
            mod_grad,
            mod_bias_grad,
            qkv_grad,
            out[0],
            jnp.stack([out[4], out[5]]),
            proj_grad,
            out[1],
            up_grad,
            out[2],
            down_grad,
            out[3],
        )

    return per_device


def solution(mesh):
    if mesh.shape["dp"] == 2 * PLANE and mesh.shape["fsdp"] == 4:
        body = make_plane(mesh.shape["fsdp"])
    else:
        body = make_plain(mesh.shape["dp"], mesh.shape["fsdp"])
    rows = P(("dp", "fsdp"), None)
    matrix = P("dp", "fsdp")
    vector = P("fsdp")
    gains = P(None, "fsdp")
    return jax.shard_map(
        body,
        mesh=mesh,
        in_specs=(
            rows,
            rows,
            P(("dp", "fsdp")),
            P(None, ("dp", "fsdp")),
            matrix,
            vector,
            matrix,
            vector,
            gains,
            matrix,
            vector,
            matrix,
            vector,
            matrix,
            vector,
            rows,
        ),
        out_specs=(
            rows,
            rows,
            rows,
            matrix,
            vector,
            matrix,
            vector,
            gains,
            matrix,
            vector,
            matrix,
            vector,
            matrix,
            vector,
        ),
        check_vma=False,
    )
```

```python
import functools

import jax
import jax.numpy as jnp
import numpy as np
from jax import lax
from jax.experimental import pallas as pl
from jax.experimental.pallas import tpu as pltpu
from jax.sharding import PartitionSpec as P

HEADS = 16
SPAN = 64
SIDE = 16

epsilon = 1e-06
low = jnp.bfloat16
full = jnp.float32


def rms_scale(values):
    return lax.rsqrt(jnp.mean(values * values, axis=-1, keepdims=True) + epsilon)


def norm_backward(grad_normed, normed, factor):
    return factor * (grad_normed - normed * jnp.mean(grad_normed * normed, axis=-1, keepdims=True))


def rotary_tables(coord_rows, quarter):
    frequencies = 10000.0 ** (-jnp.arange(quarter, dtype=full) / quarter)
    row_angle = coord_rows[0].astype(full)[:, None, None] * frequencies
    col_angle = coord_rows[1].astype(full)[:, None, None] * frequencies
    return (jnp.cos(row_angle), jnp.sin(row_angle), jnp.cos(col_angle), jnp.sin(col_angle))


def rotate(values, tables, direction):
    half_size = values.shape[-1] // 2
    quarter = half_size // 2
    pieces_out = []
    for which_half in range(2):
        cosine = tables[2 * which_half]
        sine_tab = direction * tables[2 * which_half + 1]
        start_col = which_half * half_size
        first_part = values[..., start_col : start_col + quarter]
        second = values[..., start_col + quarter : start_col + half_size]
        pieces_out.append(first_part * cosine - second * sine_tab)
        pieces_out.append(second * cosine + first_part * sine_tab)
    return jnp.concatenate(pieces_out, axis=-1)


def dot(left, right):
    return jnp.dot(left, right, preferred_element_type=full)


def dot_t(left, right):
    return lax.dot_general(left, right, (((1,), (1,)), ((), ())), preferred_element_type=full)


def outer_grad(left, right):
    return lax.dot_general(left, right, (((0,), (0,)), ((), ())), preferred_element_type=full)


def silu_slope(values):
    sigmoid_gate = jax.nn.sigmoid(values)
    return sigmoid_gate * (1.0 + values * (1.0 - sigmoid_gate))


def swap(values, axis, size, bit):
    return lax.ppermute(values, axis, [(k, k ^ bit) for k in range(size)])


def bits_of(size):
    return [1 << b for b in range(size.bit_length() - 1)]


def gather_small(values, axis, size):
    index = lax.axis_index(axis)
    for bit in bits_of(size):
        other = swap(values, axis, size, bit)
        upper = (index & bit) != 0
        values = jnp.concatenate(
            [jnp.where(upper, other, values), jnp.where(upper, values, other)], axis=0
        )
    return values


def scatter_sum_small(values, axis, size):
    index = lax.axis_index(axis)
    for bit in reversed(bits_of(size)):
        half = values.shape[0] // 2
        upper = (index & bit) != 0
        first, second = values[:half], values[half:]
        values = jnp.where(upper, second, first) + swap(
            jnp.where(upper, first, second), axis, size, bit
        )
    return values


def sum_small(values, axis, size):
    for bit in bits_of(size):
        values = values + swap(values, axis, size, bit)
    return values


def xor_order(values, index, size):
    tail = values.shape[1:]
    for bit in bits_of(size):
        paired = values.reshape((size // (2 * bit), 2, bit) + tail)
        values = jnp.where((index & bit) != 0, jnp.flip(paired, axis=1), paired)
        values = values.reshape((size,) + tail)
    return values


def exchange_small(values, axis, size):
    index = lax.axis_index(axis)
    tail = values.shape[1:]
    values = xor_order(values, index, size)
    for bit in bits_of(size):
        paired = values.reshape((size // (2 * bit), 2, bit) + tail)
        moved = swap(paired[:, 1], axis, size, bit)
        values = jnp.stack([paired[:, 0], moved], axis=1).reshape((size,) + tail)
    return xor_order(values, index, size)


def gather_weight(weight, dp_size, fsdp_size):
    rows, cols = weight.shape
    whole = lax.all_gather(weight, ("dp", "fsdp"), axis=0, tiled=False)
    whole = whole.reshape(dp_size, fsdp_size, rows, cols).transpose(1, 0, 2, 3)
    return whole.reshape(fsdp_size, dp_size * rows, cols)


def scatter_grad(blocks, dp_size):
    rows, cols = blocks[0].shape
    parts = jnp.stack([b.reshape(dp_size, rows // dp_size, cols) for b in blocks], axis=1)
    parts = lax.psum_scatter(parts, "dp", scatter_dimension=0, tiled=False)
    return lax.psum_scatter(parts, "fsdp", scatter_dimension=0, tiled=False).astype(full)


def masked_scores(query_low, key_low, same_item, score_scale):
    scores = jnp.einsum("qhd,khd->hqk", query_low, key_low, preferred_element_type=full)
    return jnp.where(same_item, scores * score_scale, -1e30)


def make_plain(dp_size, fsdp_size):
    def per_device(
        patches,
        conditions,
        segment_ids,
        grid_coords,
        mod_weight,
        mod_bias,
        qkv_weight,
        qkv_bias,
        qk_gains,
        proj_weight,
        proj_bias,
        up_weight,
        up_bias,
        down_weight,
        down_bias,
        out_cotangent,
    ):
        row_count, model_width = patches.shape
        slots = conditions.shape[0]
        spans = row_count // SPAN
        head_size = model_width // HEADS
        score_scale = head_size ** (-0.5)
        head_shape = (row_count, HEADS, head_size)
        dp_index = lax.axis_index("dp")
        mod_rows, mod_cols = mod_weight.shape

        qkv_full = gather_weight(qkv_weight, dp_size, fsdp_size)
        proj_full = gather_weight(proj_weight, dp_size, fsdp_size)
        up_full = gather_weight(up_weight, dp_size, fsdp_size)
        down_full = gather_weight(down_weight, dp_size, fsdp_size)

        gain_cols = qk_gains.shape[1]
        sizes = [qkv_bias.shape[0], proj_bias.shape[0], up_bias.shape[0], down_bias.shape[0]]
        vector = jnp.concatenate(
            [qkv_bias, proj_bias, up_bias, down_bias, qk_gains[0], qk_gains[1]]
        )
        vectors = gather_small(vector[None], "fsdp", fsdp_size).astype(full)
        bounds = [0]
        for size in sizes + [gain_cols, gain_cols]:
            bounds.append(bounds[-1] + size)
        pieces = [vectors[:, bounds[k] : bounds[k + 1]] for k in range(6)]
        qkv_vector, proj_vector, up_vector, down_vector, gain_q, gain_k = [
            p.reshape(-1) for p in pieces
        ]

        cond_full = conditions.astype(full)
        silu_low = jax.nn.silu(cond_full).astype(low)
        silu_all = gather_small(
            gather_small(silu_low[None], "fsdp", fsdp_size)[None], "dp", dp_size
        ).reshape(dp_size * fsdp_size * slots, model_width)
        silu_cols = lax.dynamic_slice_in_dim(silu_all, dp_index * mod_rows, mod_rows, axis=1)
        mod_part = dot(silu_cols, mod_weight).reshape(dp_size, fsdp_size, slots, mod_cols)
        mod_sum = scatter_sum_small(mod_part, "dp", dp_size)[0] + mod_bias.astype(full)
        modulation = exchange_small(mod_sum, "fsdp", fsdp_size)
        modulation = modulation.transpose(1, 0, 2).reshape(slots, fsdp_size * mod_cols)
        span_ids = segment_ids.reshape(spans, SPAN)[:, 0]
        span_hot = (span_ids[:, None] == jnp.arange(slots, dtype=jnp.int32)[None, :]).astype(full)
        span_mod = jnp.sum(span_hot[:, :, None] * modulation[None], axis=1)

        def per_row(k):
            part = span_mod[:, k * model_width : (k + 1) * model_width]
            return jnp.broadcast_to(part[:, None, :], (spans, SPAN, model_width)).reshape(
                row_count, model_width
            )

        shift_attn, scale_attn, gate_attn, shift_ffn, scale_ffn, gate_ffn = map(per_row, range(6))

        def cols_of(blocks):
            return jnp.concatenate(blocks, axis=1)

        def forward_dot(rows_low, weight_full):
            return cols_of([dot(rows_low, weight_full[j]) for j in range(fsdp_size)])

        def split(values):
            width = values.shape[1] // fsdp_size
            return [values[:, j * width : (j + 1) * width] for j in range(fsdp_size)]

        def backward_dot(grad_low, weight_full):
            parts = split(grad_low)
            total = dot_t(parts[0], weight_full[0])
            for j in range(1, fsdp_size):
                total = total + dot_t(parts[j], weight_full[j])
            return total

        def weight_grad(rows_low, grad_low):
            return scatter_grad(
                [outer_grad(rows_low, part).astype(low) for part in split(grad_low)], dp_size
            )

        tables = rotary_tables(grid_coords, head_size // 4)
        patch_full = patches.astype(full)
        scale_one = rms_scale(patch_full)
        normed_one = patch_full * scale_one
        hidden_one = (normed_one * (1.0 + scale_attn) + shift_attn).astype(low)
        qkv_rows = forward_dot(hidden_one, qkv_full) + qkv_vector
        query_raw = qkv_rows[:, 0:model_width].reshape(head_shape)
        key_raw = qkv_rows[:, model_width : 2 * model_width].reshape(head_shape)
        value_low = qkv_rows[:, 2 * model_width :].reshape(head_shape).astype(low)
        query_scale = rms_scale(query_raw)
        query_unit = query_raw * query_scale
        key_scale = rms_scale(key_raw)
        key_unit = key_raw * key_scale
        query_low = rotate(query_unit * gain_q, tables, 1.0).astype(low)
        key_low = rotate(key_unit * gain_k, tables, 1.0).astype(low)
        same_item = (segment_ids[:, None] == segment_ids[None, :])[None]
        scores = masked_scores(query_low, key_low, same_item, score_scale)
        exponentials = jnp.exp(scores - jnp.max(scores, axis=-1, keepdims=True))
        probs = exponentials / jnp.sum(exponentials, axis=-1, keepdims=True)
        probs_low = probs.astype(low)
        attended_low = (
            jnp.einsum("hqk,khd->qhd", probs_low, value_low, preferred_element_type=full)
            .reshape(row_count, model_width)
            .astype(low)
        )
        branch_attn = forward_dot(attended_low, proj_full) + proj_vector
        middle = patch_full + gate_attn * branch_attn
        scale_two = rms_scale(middle)
        normed_two = middle * scale_two
        hidden_two = (normed_two * (1.0 + scale_ffn) + shift_ffn).astype(low)
        gate_up = forward_dot(hidden_two, up_full) + up_vector
        hidden_units = gate_up.shape[1] // 2
        gate_part = gate_up[:, :hidden_units]
        up_part = gate_up[:, hidden_units:]
        gated_low = (jax.nn.silu(gate_part) * up_part).astype(low)
        branch_ffn = forward_dot(gated_low, down_full) + down_vector
        block_out = (middle + gate_ffn * branch_ffn).astype(low)

        grad_out = out_cotangent.astype(full)
        grad_gate_ffn = grad_out * branch_ffn
        grad_branch_ffn = (grad_out * gate_ffn).astype(low)
        down_bias_grad = jnp.sum(grad_branch_ffn.astype(full), axis=0)
        grad_gated = backward_dot(grad_branch_ffn, down_full)
        down_grad = weight_grad(gated_low, grad_branch_ffn)
        grad_gate_up = jnp.concatenate(
            [grad_gated * up_part * silu_slope(gate_part), grad_gated * jax.nn.silu(gate_part)],
            axis=1,
        ).astype(low)
        up_bias_grad = jnp.sum(grad_gate_up.astype(full), axis=0)
        grad_hidden_two = backward_dot(grad_gate_up, up_full)
        up_grad = weight_grad(hidden_two, grad_gate_up)
        grad_middle = grad_out + norm_backward(
            grad_hidden_two * (1.0 + scale_ffn), normed_two, scale_two
        )
        grad_gate_attn = grad_middle * branch_attn
        grad_branch_attn = (grad_middle * gate_attn).astype(low)
        proj_bias_grad = jnp.sum(grad_branch_attn.astype(full), axis=0)
        grad_attended = backward_dot(grad_branch_attn, proj_full).astype(low).reshape(head_shape)
        proj_grad = weight_grad(attended_low, grad_branch_attn)
        grad_probs = jnp.einsum(
            "qhd,khd->hqk", grad_attended, value_low, preferred_element_type=full
        )
        row_dot = jnp.sum(probs * grad_probs, axis=-1, keepdims=True)
        grad_scores = (probs * (grad_probs - row_dot)).astype(low)
        grad_values = jnp.einsum(
            "hqk,qhd->khd", probs_low, grad_attended, preferred_element_type=full
        )
        grad_query_rot = score_scale * jnp.einsum(
            "hqk,khd->qhd", grad_scores, key_low, preferred_element_type=full
        )
        grad_key_rot = score_scale * jnp.einsum(
            "hqk,qhd->khd", grad_scores, query_low, preferred_element_type=full
        )
        back_query = rotate(grad_query_rot, tables, -1.0)
        back_key = rotate(grad_key_rot, tables, -1.0)
        gain_q_grad = jnp.sum(back_query * query_unit, axis=(0, 1))
        gain_k_grad = jnp.sum(back_key * key_unit, axis=(0, 1))
        grad_query_raw = norm_backward(back_query * gain_q, query_unit, query_scale)
        grad_key_raw = norm_backward(back_key * gain_k, key_unit, key_scale)
        grad_qkv = jnp.concatenate(
            [
                grad_query_raw.reshape(row_count, model_width),
                grad_key_raw.reshape(row_count, model_width),
                grad_values.reshape(row_count, model_width),
            ],
            axis=1,
        ).astype(low)
        qkv_grad = weight_grad(hidden_one, grad_qkv)
        qkv_bias_grad = jnp.sum(grad_qkv.astype(full), axis=0)
        grad_hidden_one = backward_dot(grad_qkv, qkv_full)
        patch_grad = (
            grad_middle + norm_backward(grad_hidden_one * (1.0 + scale_attn), normed_one, scale_one)
        ).astype(low)

        def span_sum(values):
            return jnp.sum(values.reshape(spans, SPAN, model_width), axis=1)

        grad_spans = jnp.concatenate(
            [
                span_sum(grad_hidden_one),
                span_sum(grad_hidden_one * normed_one),
                span_sum(grad_gate_attn),
                span_sum(grad_hidden_two),
                span_sum(grad_hidden_two * normed_two),
                span_sum(grad_gate_ffn),
            ],
            axis=1,
        )
        grad_modulation = jnp.sum(span_hot[:, :, None] * grad_spans[:, None, :], axis=0).astype(low)
        grad_mod = grad_modulation.reshape(slots, fsdp_size, mod_cols).transpose(1, 0, 2)
        grad_mod = exchange_small(grad_mod, "fsdp", fsdp_size)
        grad_mod = gather_small(grad_mod[None], "dp", dp_size).reshape(-1, mod_cols)
        mod_bias_grad = jnp.sum(grad_mod.astype(full), axis=0)
        mod_grad = outer_grad(silu_cols, grad_mod)
        cond_part = dot_t(grad_mod, mod_weight).reshape(dp_size, fsdp_size, slots, mod_rows)
        cond_part = scatter_sum_small(cond_part.transpose(1, 0, 2, 3), "fsdp", fsdp_size)[0]
        cond_part = exchange_small(cond_part, "dp", dp_size)
        cond_grad = (
            cond_part.transpose(1, 0, 2).reshape(slots, model_width) * silu_slope(cond_full)
        ).astype(low)

        rows = [qkv_bias_grad, proj_bias_grad, up_bias_grad, down_bias_grad, gain_q_grad, gain_k_grad]
        vector_grad = jnp.concatenate([r.reshape(fsdp_size, -1) for r in rows], axis=1)
        vector_grad = scatter_sum_small(vector_grad, "fsdp", fsdp_size)
        vector_grad = sum_small(vector_grad, "dp", dp_size)[0]
        out = [vector_grad[bounds[k] : bounds[k + 1]] for k in range(6)]
        return (
            block_out,
            patch_grad,
            cond_grad,
            mod_grad,
            mod_bias_grad,
            qkv_grad,
            out[0],
            jnp.stack([out[4], out[5]]),
            proj_grad,
            out[1],
            up_grad,
            out[2],
            down_grad,
            out[3],
        )

    return per_device


PLANE = 4


def cross(values, hop):
    return lax.ppermute(values, "dp", [(k, k ^ (2 * hop)) for k in range(2 * PLANE)])


def partner(values):
    return lax.ppermute(values, "dp", [(k, k ^ 1) for k in range(2 * PLANE)])


def along(values, hop, size):
    return lax.ppermute(values, "fsdp", [(k, k ^ hop) for k in range(size)])


def plane_blocks(values):
    return [values] + [cross(values, hop) for hop in range(1, PLANE)]


def plane_sum(blocks):
    total = blocks[0]
    for hop in range(1, PLANE):
        total = total + cross(blocks[hop].astype(low), hop).astype(full)
    return total


def z_blocks(values, index, size):
    blocks = jnp.stack([values] + [along(values, hop, size) for hop in range(1, size)])
    return xor_order(blocks, index, size)


def z_exchange(values, index, size):
    values = xor_order(values, index, size)
    moved = jnp.stack([values[0]] + [along(values[hop], hop, size) for hop in range(1, size)])
    return xor_order(moved, index, size)


def z_sum_own(values, index, size):
    values = xor_order(values, index, size)
    total = values[0].astype(full)
    for hop in range(1, size):
        total = total + along(values[hop], hop, size).astype(full)
    return total


class Place:
    def __init__(self, y, x, core, z):
        self.y, self.x, self.core, self.z = y, x, core, z
        self.chip = 2 * y + x
        self.dp = 2 * self.chip + core

    def hop(self, dy, dx, dc, dz):
        low_z, high_z = self.z % 2, self.z // 2
        low_z = 1 - low_z if dz & 1 else low_z
        high_z = 1 - high_z if dz & 2 else high_z
        return Place(
            1 - self.y if dy else self.y,
            1 - self.x if dx else self.x,
            1 - self.core if dc else self.core,
            2 * high_z + low_z,
        )


SELF = (0, 0, 0, 0)
PLANE_HOPS = [(0, 1, 0, 0), (1, 0, 0, 0), (1, 1, 0, 0)]
Z_HOPS = [(0, 0, 0, 1), (0, 0, 0, 2), (0, 0, 0, 3)]
CORE_HOP = (0, 0, 1, 0)
DP_HOPS = [(dy, dx, dc, 0) for dy in (0, 1) for dx in (0, 1) for dc in (0, 1)]
ALL_HOPS = [(dy, dx, dc, dz) for dz in range(4) for dy, dx, dc, _ in DP_HOPS]
GROUP_HOPS = [(dy, dx, 0, dz) for dz in range(4) for dy in (0, 1) for dx in (0, 1)]


class Copies:
    def __init__(self, plan, ins, outs, send, recv):
        self.plan, self.ins, self.outs, self.send, self.recv = plan, ins, outs, send, recv

    def here(self):
        dp_index = lax.axis_index("dp")
        return Place(dp_index // 4, (dp_index // 2) % 2, dp_index % 2, lax.axis_index("fsdp"))

    def greet(self):
        hops = []
        for move in self.plan:
            if move[0] != SELF and move[0] not in hops:
                hops.append(move[0])
        barrier = pltpu.get_barrier_semaphore()
        for hop in hops:
            peer = self.here().hop(*hop)
            pl.semaphore_signal(
                barrier,
                1,
                device_id={"dp": peer.dp, "fsdp": peer.z},
                device_id_type=pl.DeviceIdType.MESH,
            )
        pl.semaphore_wait(barrier, len(hops))

    def copy(self, number):
        hop, source, source_at, out, out_at, after = self.plan[number]
        me = self.here()
        peer = me.hop(*hop)
        src = (self.ins if after is None else self.outs)[source]
        src = src if source_at is None else src.at[source_at(me, peer)]
        dst = self.outs[out]
        dst = dst if out_at is None else dst.at[out_at(me, peer)]
        if hop == SELF:
            return pltpu.make_async_copy(src, dst, self.send.at[number])
        return pltpu.make_async_remote_copy(
            src_ref=src,
            dst_ref=dst,
            send_sem=self.send.at[number],
            recv_sem=self.recv.at[number],
            device_id={"dp": peer.dp, "fsdp": peer.z},
            device_id_type=pl.DeviceIdType.MESH,
        )

    def start(self, number):
        self.copy(number).start()

    def wait_arrival(self, number):
        if self.plan[number][0] == SELF:
            self.copy(number).wait()
        else:
            self.copy(number).wait_recv()

    def finish(self, arrived=()):
        for number, move in enumerate(self.plan):
            if number not in arrived:
                self.wait_arrival(number)
            if move[0] != SELF:
                self.copy(number).wait_send()


def exchange(identity, inputs, out_shapes, plan):
    def kernel(*refs):
        ins, outs = refs[: len(inputs)], refs[len(inputs) : len(inputs) + len(out_shapes)]
        copies = Copies(plan, ins, outs, *refs[-2:])
        copies.greet()
        done = set()
        for number, move in enumerate(plan):
            for earlier in move[5] or ():
                if earlier not in done:
                    copies.wait_arrival(earlier)
                    done.add(earlier)
            copies.start(number)
        copies.finish(done)

    anywhere = pl.BlockSpec(memory_space=pl.ANY)
    return pl.pallas_call(
        kernel,
        out_shape=[jax.ShapeDtypeStruct(shape, dtype) for shape, dtype in out_shapes],
        in_specs=[anywhere] * len(inputs),
        out_specs=[anywhere] * len(out_shapes),
        scratch_shapes=[
            pltpu.SemaphoreType.DMA((len(plan),)),
            pltpu.SemaphoreType.DMA((len(plan),)),
        ],
        compiler_params=pltpu.CompilerParams(collective_id=identity, has_side_effects=True),
    )(*inputs)


def gather_moves(hops, source, out, out_at):
    return [(hop, source, None, out, out_at, None) for hop in hops]


def by_chip(me, peer):
    return (me.chip,)


def by_dp(me, peer):
    return (me.dp,)


def by_z(me, peer):
    return (me.z,)


def by_core(me, peer):
    return (me.core,)


def tie(first, second):
    return lax.optimization_barrier((first, second))


def put(values, own, *at):
    start = tuple(at) + (0,) * (values.ndim - len(at))
    return lax.dynamic_update_slice(values, own.reshape((1,) * len(at) + own.shape), start)


HOP_X, HOP_Y = PLANE_HOPS[0], PLANE_HOPS[1]


def relayed(source, out, place, first):
    def at(hop, half):
        return lambda me, peer: (place(me, hop), half)

    def onto(hop, half):
        return lambda me, peer: (place(peer, hop), half)

    def part(half):
        return lambda me, peer: (half,)

    diagonal = PLANE_HOPS[2]
    return [
        (HOP_X, source, part(0), out, onto(HOP_X, 0), None),
        (HOP_Y, source, part(1), out, onto(HOP_Y, 1), None),
        (HOP_X, source, part(1), out, onto(HOP_X, 1), None),
        (HOP_Y, source, part(0), out, onto(HOP_Y, 0), None),
        (HOP_Y, out, at(HOP_X, 0), out, onto(diagonal, 0), (first,)),
        (HOP_X, out, at(HOP_Y, 1), out, onto(diagonal, 1), (first + 1,)),
    ]


def chip_place(me, hop):
    return me.hop(*hop).chip


def hop_place(me, hop):
    return PLANE_HOPS.index(hop)


def slotted(hops, source, source_at, out):
    return [
        (hop, source, source_at, out, lambda me, peer, n=n: (n,), None)
        for n, hop in enumerate(hops)
    ]


def to_chip(me, peer):
    return (peer.chip,)


def to_z(me, peer):
    return (peer.z,)


LANES = 128


def head_of(values, number, head_size):
    part = values[:, number * head_size : (number + 1) * head_size]
    pad = jnp.zeros((values.shape[0], LANES - head_size), values.dtype)
    return jnp.concatenate([part, pad], axis=1)


def pair_of(values, head_size):
    quarter = head_size // 4
    lane = lax.broadcasted_iota(jnp.int32, values.shape, 1)
    second = (lane // quarter) % 2 == 1
    return jnp.where(
        second, pltpu.roll(values, quarter, 1), pltpu.roll(values, LANES - quarter, 1)
    )


def unit_of(raw, head_size):
    factor = lax.rsqrt(jnp.sum(raw * raw, axis=1, keepdims=True) * (1.0 / head_size) + epsilon)
    return raw * factor, factor


def head_probs(query, key, same, score_scale):
    scores = jnp.where(same, dot_t(query, key) * score_scale, -1e30)
    exponentials = jnp.exp(scores - jnp.max(scores, axis=1, keepdims=True))
    return exponentials * (1.0 / jnp.sum(exponentials, axis=1, keepdims=True))


def rotary_rows(head_size):
    quarter = head_size // 4
    frequencies = np.float32(10000.0) ** (-np.arange(quarter, dtype=np.float32) / quarter)
    angles = np.arange(SIDE, dtype=np.float32)[:, None] * frequencies.astype(np.float32)
    cosine = np.zeros((2, SIDE, LANES), np.float32)
    sine = np.zeros((2, SIDE, LANES), np.float32)
    for k in range(2):
        first = 2 * quarter * k
        cosine[k, :, first : first + 2 * quarter] = np.tile(np.cos(angles), (1, 2))
        sine[k, :, first : first + quarter] = -np.sin(angles)
        sine[k, :, first + quarter : first + 2 * quarter] = np.sin(angles)
    return jnp.asarray(cosine.reshape(-1, LANES)), jnp.asarray(sine.reshape(-1, LANES))


def rotary_of(meta, cosine_rows, sine_rows):
    place = lax.broadcasted_iota(jnp.int32, (meta.shape[0], 2 * SIDE), 1)
    hot = (meta[:, 1:2] == place) | (meta[:, 2:3] + SIDE == place)
    hot = hot.astype(full)
    take = functools.partial(jnp.dot, preferred_element_type=full, precision=lax.Precision.HIGHEST)
    return take(hot, cosine_rows), take(hot, sine_rows)


def attention_block(head_size, heads, refs):
    (rows, gains, cosine, sine, seg_row, seg_col) = refs
    same = seg_row == seg_col
    gain_q, gain_k = gains[0:1], gains[1:2]
    for h in range(heads):
        query_unit, query_factor = unit_of(head_of(rows, h, head_size), head_size)
        key_unit, key_factor = unit_of(head_of(rows, heads + h, head_size), head_size)
        query = query_unit * gain_q
        key = key_unit * gain_k
        query = (query * cosine + pair_of(query, head_size) * sine).astype(low)
        key = (key * cosine + pair_of(key, head_size) * sine).astype(low)
        value = head_of(rows, 2 * heads + h, head_size).astype(low)
        probs = head_probs(query, key, same, head_size ** (-0.5))
        yield query_unit, query_factor, key_unit, key_factor, query, key, value, probs


def fill_rows(target, mine, other):
    rows = mine.shape[1]
    core = lax.axis_index("dp") % 2
    for source, place in ((mine, core), (other, 1 - core)):
        target[pl.ds(pl.multiple_of(place * rows, 16), rows), :] = jnp.concatenate(
            [source[j] for j in range(source.shape[0])], axis=1
        )


def attention_forward_kernel(head_size, heads, copies, rest, *refs):
    (patch, shift, scale, weight, bias, gains, cos_rows, sin_rows, meta, seg_col) = refs[:10]
    proj_mine, proj_other = refs[10:12]
    hidden_out, rows_out, attended_out, terms_out, proj = refs[12:]

    @pl.when(pl.program_id(0) == 0)
    def _():
        copies.greet()
        for number in range(len(copies.plan)):
            copies.start(number)
        fill_rows(proj, proj_mine, proj_other)

    cosine, sine = rotary_of(meta[0], cos_rows[...], sin_rows[...])
    values = patch[0].astype(full)
    count, width = values.shape
    normed = values * lax.rsqrt(jnp.mean(values * values, axis=1, keepdims=True) + epsilon)
    hidden = normed.reshape(count // SPAN, SPAN, width) * (1.0 + scale[0]) + shift[0]
    hidden = hidden.reshape(count, width).astype(low)
    hidden_out[0] = hidden
    rows = dot(hidden, weight[...]) + bias[...]
    rows_out[0] = rows
    pieces = []
    refs = (rows, gains[...], cosine, sine, meta[0, :, 0:1], seg_col[0])
    for *_, value, probs in attention_block(head_size, heads, refs):
        pieces.append(dot(probs.astype(low), value)[:, :head_size])
    attended = jnp.concatenate(pieces, axis=1).astype(low)
    attended_out[0] = attended
    terms_out[0] = dot(attended, proj[...]).astype(low)

    @pl.when(pl.program_id(0) == pl.num_programs(0) - 1)
    def _():
        copies.finish()


def cut_columns(parts, total):
    cols = parts.shape[3]
    for j in range(parts.shape[0]):
        parts[j] = total[:, j * cols : (j + 1) * cols].astype(low).reshape(parts.shape[1:])


def attention_backward_kernel(head_size, heads, copies, rest, *refs):
    (grad, rows, weight, gains, cos_rows, sin_rows, meta, seg_col, proj) = refs[:9]
    hidden, attended = refs[9:11]
    terms_out, bias_out, gains_out, qkv_parts, proj_parts = refs[11:16]
    qkv_total, proj_total = refs[16:]

    @pl.when(pl.program_id(0) == 0)
    def _():
        bias_out[...] = jnp.zeros_like(bias_out)
        gains_out[...] = jnp.zeros_like(gains_out)
        qkv_total[...] = jnp.zeros_like(qkv_total)
        proj_total[...] = jnp.zeros_like(proj_total)
        copies.greet()
        for number in range(len(copies.plan)):
            copies.start(number)

    score_scale = head_size ** (-0.5)
    gain_values = gains[...]
    cos_tab, sin_tab = rotary_of(meta[0], cos_rows[...], sin_rows[...])
    grad_attended = dot_t(grad[0], proj[...])
    values = rows[0]
    grad_queries, grad_keys, grad_values = [], [], []
    gain_sums = [jnp.zeros((1, LANES), full), jnp.zeros((1, LANES), full)]

    def raw_grad(rotated, unit, factor, which):
        back = rotated * cos_tab - pair_of(rotated, head_size) * sin_tab
        gain_sums[which] = gain_sums[which] + jnp.sum(back * unit, axis=0, keepdims=True)
        turned = back * gain_values[which : which + 1]
        mean = jnp.sum(turned * unit, axis=1, keepdims=True) * (1.0 / head_size)
        return ((turned - unit * mean) * factor)[:, :head_size]

    refs = (values, gain_values, cos_tab, sin_tab, meta[0, :, 0:1], seg_col[0])
    for h, parts in enumerate(attention_block(head_size, heads, refs)):
        query_unit, query_factor, key_unit, key_factor, query, key, value, probs = parts
        grad_head = head_of(grad_attended, h, head_size).astype(low)
        grad_probs = dot_t(grad_head, value)
        row_dot = jnp.sum(probs * grad_probs, axis=1, keepdims=True)
        grad_scores = (probs * (grad_probs - row_dot)).astype(low)
        grad_values.append(outer_grad(probs.astype(low), grad_head)[:, :head_size])
        grad_queries.append(
            raw_grad(dot(grad_scores, key) * score_scale, query_unit, query_factor, 0)
        )
        grad_keys.append(
            raw_grad(outer_grad(grad_scores, query) * score_scale, key_unit, key_factor, 1)
        )
    result = jnp.concatenate(grad_queries + grad_keys + grad_values, axis=1).astype(low)
    bias_out[...] += jnp.sum(result.astype(full), axis=0, keepdims=True)
    gains_out[0:1, :] += gain_sums[0]
    gains_out[1:2, :] += gain_sums[1]
    terms_out[0] = dot_t(result, weight[...]).astype(low)
    qkv_total[...] += outer_grad(hidden[0], result)
    proj_total[...] += outer_grad(attended[0], grad[0])

    @pl.when(pl.program_id(0) == pl.num_programs(0) - 1)
    def _():
        qkv_parts[...] = qkv_total[...].astype(low).reshape(qkv_parts.shape)
        cut_columns(proj_parts, proj_total[...])
        copies.finish()


def ffn_kernel(copies, rest, *refs):
    (own_hidden, hiddens, own_cot, cots, gate, up_mine, up_other) = refs[:7]
    (down_mine, down_other, bias) = refs[7:10]
    ffn_terms, hidden_terms, bias_out, up_parts, down_parts = refs[10:15]
    down, up, up_total, down_total, terms = refs[15:]
    copies.ins = [terms]
    step = pl.program_id(0)

    @pl.when(step == 0)
    def _():
        bias_out[...] = jnp.zeros_like(bias_out)
        up_total[...] = jnp.zeros_like(up_total)
        down_total[...] = jnp.zeros_like(down_total)
        copies.greet()
        fill_rows(down, down_mine, down_other)
        rows = up_mine.shape[1]
        core = lax.axis_index("dp") % 2
        for source, place in ((up_mine, core), (up_other, 1 - core)):
            for p in range(source.shape[0]):
                at = pl.multiple_of((2 * p + place) * rows, 16)
                up[pl.ds(at, rows), :] = source[p]

    count, width = own_hidden.shape
    last = pl.num_programs(0) - 1
    units = down.shape[0]
    hidden = jnp.where(step == last, own_hidden[...], hiddens[0])
    cot = jnp.where(step == last, own_cot[...], cots[0])
    grad_branch = cot.astype(full).reshape(count // SPAN, SPAN, width) * gate[0]
    grad_branch = grad_branch.reshape(count, width).astype(low)
    grad_gated = dot_t(grad_branch, down[...])
    gate_up = dot(hidden, up[...]) + bias[...]
    gate_part, up_part = gate_up[:, :units], gate_up[:, units:]
    sigmoid = jax.nn.sigmoid(gate_part)
    silu = gate_part * sigmoid
    gated = (silu * up_part).astype(low)
    slope = sigmoid * (1.0 + gate_part * (1.0 - sigmoid))
    grad_gate = (grad_gated * up_part * slope).astype(low)
    grad_up = (grad_gated * silu).astype(low)
    grads = jnp.concatenate([grad_gate, grad_up], axis=1)
    bias_out[...] += jnp.sum(grads.astype(full), axis=0, keepdims=True)

    for number in range(PLANE - 1):
        @pl.when(step == number + 1)
        def _(number=number):
            copies.start(number)

    hidden_term = dot_t(grads, up[...]).astype(low)

    @pl.when(step < last)
    def _():
        terms[step] = hidden_term

    @pl.when(step == last)
    def _():
        hidden_terms[...] = hidden_term

    ffn_terms[0] = dot(gated, down[...]).astype(low)
    up_total[...] += outer_grad(hidden, grads)
    down_total[...] += outer_grad(gated, grad_branch)

    @pl.when(step == pl.num_programs(0) - 1)
    def _():
        up_parts[...] = up_total[...].astype(low).reshape(up_parts.shape)
        cut_columns(down_parts, down_total[...])
        copies.finish()


def split_kernel(groups, source, target):
    count, _, cols = source.shape
    part = cols // groups
    for p in range(count):
        pieces = []
        for t in range(groups):
            block, at = divmod(t * count + p, groups)
            pieces.append(source[block, :, at * part : (at + 1) * part])
        target[p] = jnp.concatenate(pieces, axis=1)


def merge_kernel(groups, source, target):
    count, _, cols = source.shape
    part = cols // groups
    for z in range(count):
        pieces = []
        for at in range(groups):
            t, p = divmod(z * groups + at, count)
            pieces.append(source[p, :, t * part : (t + 1) * part])
        target[z] = jnp.concatenate(pieces, axis=1)


def whole_call(kernel, values):
    return pl.pallas_call(kernel, out_shape=jax.ShapeDtypeStruct(values.shape, values.dtype))(values)


def block_call(
    kernel, inputs, blocked, out_blocks, out_whole, scratch, steps, flops, identity, moved, landed, plan
):
    def block_spec(shape, mark=1):
        tail = (0,) * (len(shape) - 1)
        if mark == 2:
            return pl.BlockSpec((1,) + shape[1:], lambda p: ((p + 2) % 3,) + tail)
        return pl.BlockSpec((1,) + shape[1:], lambda p: (p,) + tail)

    def whole_spec(shape):
        return pl.BlockSpec(shape, lambda p: (0,) * len(shape))

    anywhere = pl.BlockSpec(memory_space=pl.ANY)
    counts = [len(inputs), len(moved), len(out_blocks) + len(out_whole), len(landed)]
    cuts = np.cumsum(counts).tolist()

    def body(*refs):
        ins, sources = refs[: cuts[0]], refs[cuts[0] : cuts[1]]
        outs, targets = refs[cuts[1] : cuts[2]], refs[cuts[2] : cuts[3]]
        rest, send, recv = refs[cuts[3] : -2], refs[-2], refs[-1]
        kernel(Copies(plan, sources, targets, send, recv), rest, *ins, *outs, *rest)

    return pl.pallas_call(
        body,
        grid=(steps,),
        out_shape=[jax.ShapeDtypeStruct(*o) for o in out_blocks + out_whole + landed],
        in_specs=[
            block_spec(v.shape, b) if b else whole_spec(v.shape) for v, b in zip(inputs, blocked)
        ]
        + [anywhere] * len(moved),
        out_specs=[block_spec(o[0]) for o in out_blocks]
        + [whole_spec(o[0]) for o in out_whole]
        + [anywhere] * len(landed),
        scratch_shapes=[pltpu.VMEM(*o) for o in scratch]
        + [pltpu.SemaphoreType.DMA((len(plan),)), pltpu.SemaphoreType.DMA((len(plan),))],
        compiler_params=pltpu.CompilerParams(collective_id=identity, has_side_effects=True),
        cost_estimate=pl.CostEstimate(
            flops=flops,
            bytes_accessed=sum(v.size * v.dtype.itemsize for v in inputs),
            transcendentals=flops // 1024,
        ),
    )(*inputs, *moved)


def make_plane(z_size):
    def per_device(
        patches,
        conditions,
        segment_ids,
        grid_coords,
        mod_weight,
        mod_bias,
        qkv_weight,
        qkv_bias,
        qk_gains,
        proj_weight,
        proj_bias,
        up_weight,
        up_bias,
        down_weight,
        down_bias,
        out_cotangent,
    ):
        row_count, width = patches.shape
        slots = conditions.shape[0]
        spans = row_count // SPAN
        head_size = width // HEADS
        heads = HEADS // PLANE
        part_cols = width // PLANE
        score_scale = head_size ** (-0.5)
        dp_index = lax.axis_index("dp")
        z_index = lax.axis_index("fsdp")
        chip = dp_index >> 1
        core = dp_index & 1
        upper = core == 1
        mod_rows, mod_cols = mod_weight.shape
        rows_all = PLANE * row_count
        shard = qkv_weight.shape[0]

        def halves(values):
            return values.reshape(2, row_count // 2, width)

        def core_order(mine, other):
            return jnp.where(upper, other, mine), jnp.where(upper, mine, other)

        cond_full = conditions.astype(full)
        silu_low = jax.nn.silu(cond_full).astype(low)
        vector = jnp.concatenate(
            [qkv_bias, proj_bias, up_bias, down_bias, qk_gains[0], qk_gains[1]]
        )[None]
        meta = jnp.concatenate([segment_ids[None], grid_coords], axis=0)
        cols_qkv = qkv_weight.shape[1]
        cols_proj = proj_weight.shape[1]
        plan = gather_moves(Z_HOPS + [SELF], 0, 0, lambda me, peer: (me.dp, me.z))
        plan += gather_moves(Z_HOPS, 1, 1, by_z)
        plan += gather_moves(Z_HOPS, 3, 3, by_z)
        plan += gather_moves(Z_HOPS + [SELF], 4, 4, by_z)
        plan += gather_moves(PLANE_HOPS + [SELF], 5, 5, by_chip)
        plan += [(hop, 0, by_dp, 0, by_dp, (0, 1, 2, 3)) for hop in DP_HOPS if hop != SELF]
        plan += relayed(2, 2, chip_place, len(plan))
        plan += relayed(6, 6, hop_place, len(plan))
        silu_all, qkv_z, patch_all, proj_z, vectors, meta_all, cot_blocks = exchange(
            1,
            [
                silu_low,
                qkv_weight,
                halves(patches),
                proj_weight,
                vector,
                meta,
                halves(out_cotangent),
            ],
            [
                ((2 * PLANE, z_size, slots, width), low),
                ((z_size, shard, cols_qkv), low),
                ((PLANE, 2, row_count // 2, width), low),
                ((z_size, shard, cols_proj), low),
                ((z_size,) + vector.shape, low),
                ((PLANE,) + meta.shape, jnp.int32),
                ((PLANE - 1, 2, row_count // 2, width), low),
            ],
            plan,
        )

        qkv_z, up_later = tie(qkv_z, up_weight)
        up_z = lax.all_gather(up_later, "fsdp", axis=0, tiled=False)
        qkv_z = put(qkv_z, qkv_weight, z_index)
        proj_z = put(proj_z, proj_weight, z_index)
        patch_all = put(patch_all.reshape(PLANE, row_count, width), patches, chip)

        silu_all = silu_all.reshape(-1, width)
        silu_cols = lax.dynamic_slice_in_dim(silu_all, dp_index * mod_rows, mod_rows, axis=1)
        mod_part = dot(silu_cols, mod_weight).reshape(2 * PLANE, z_size * slots, mod_cols)
        qkv_pieces = whole_call(functools.partial(split_kernel, 3), qkv_z)
        plan = [
            (hop, 0, to_chip, 0, by_dp, None) for hop in PLANE_HOPS
        ]
        plan += [
            (hop, 1, lambda me, peer: (peer.dp,), 1, lambda me, peer: (me.dp,), None)
            for hop in DP_HOPS
            if hop != SELF
        ]
        plan.append((CORE_HOP, 2, None, 2, None, None))
        for number, (dy, dx, dc, dz) in enumerate(PLANE_HOPS):
            from_hop = lambda me, peer, dy=dy, dx=dx: (me.hop(dy, dx, 0, 0).dp,)
            plan.append((CORE_HOP, 0, from_hop, 0, from_hop, (number,)))
        plan.append((CORE_HOP, 0, by_chip, 0, by_dp, None))
        qkv_slice, mod_parts, proj_other = exchange(
            2,
            [qkv_pieces, mod_part, proj_z],
            [
                ((2 * PLANE, shard, 3 * part_cols), low),
                (mod_part.shape, full),
                (proj_z.shape, low),
            ],
            plan,
        )
        qkv_slice = put(
            qkv_slice, lax.dynamic_index_in_dim(qkv_pieces, chip, 0, keepdims=False), dp_index
        )
        mod_parts = put(
            mod_parts, lax.dynamic_index_in_dim(mod_part, dp_index, 0, keepdims=False), dp_index
        )
        qkv_slice = qkv_slice.reshape(-1, 3 * part_cols)
        mod_sum = (jnp.sum(mod_parts, axis=0) + mod_bias.astype(full)).reshape(
            z_size, slots, mod_cols
        )
        plan = [
            (hop, 0, to_z, 0, lambda me, peer: (me.chip, me.z), None) for hop in Z_HOPS + [SELF]
        ]
        plan += [(hop, 0, by_chip, 0, by_chip, (0, 1, 2, 3)) for hop in PLANE_HOPS]
        (group_mod,) = exchange(
            3, [mod_sum], [((PLANE, z_size, slots, mod_cols), full)], plan
        )
        group_mod = group_mod.transpose(0, 2, 1, 3).reshape(PLANE, slots, z_size * mod_cols)
        modulation = lax.dynamic_index_in_dim(group_mod, chip, 0, keepdims=False)

        units = up_weight.shape[1] // 2
        up_pieces = whole_call(functools.partial(split_kernel, 2), up_z)
        segments = meta_all[:, 0].reshape(-1)
        meta_rows = meta_all.transpose(0, 2, 1)
        seg_col = meta_all[:, 0][:, None, :]
        cos_rows, sin_rows = rotary_rows(head_size)

        gain_cols = qk_gains.shape[1]
        sizes = [qkv_bias.shape[0], proj_bias.shape[0], up_bias.shape[0], down_bias.shape[0]]
        vectors = vectors[:, 0].astype(full)
        bounds = [0]
        for size in sizes + [gain_cols, gain_cols]:
            bounds.append(bounds[-1] + size)
        pieces = [vectors[:, bounds[k] : bounds[k + 1]] for k in range(6)]
        qkv_vector, proj_vector, up_vector, down_vector, gain_q, gain_k = [
            p.reshape(-1) for p in pieces
        ]

        def own_columns(flat, groups):
            parts = flat.reshape(groups, PLANE, -1)
            return lax.dynamic_slice_in_dim(parts, chip, 1, axis=1).reshape(-1)

        seg_spans = segments.reshape(PLANE, spans, SPAN)[:, :, 0]
        hot = (seg_spans[:, :, None] == jnp.arange(slots, dtype=jnp.int32)).astype(full)
        group_spans = jnp.sum(hot[:, :, :, None] * group_mod[:, None], axis=2)
        own_spans_ids = segment_ids.reshape(spans, SPAN)[:, 0]
        own_hot = (own_spans_ids[:, None] == jnp.arange(slots, dtype=jnp.int32)).astype(full)
        own_spans = jnp.sum(own_hot[:, :, None] * modulation[None], axis=1)

        def spread(values):
            count = values.shape[0]
            return jnp.broadcast_to(values[:, None, :], (count, SPAN, width)).reshape(
                count * SPAN, width
            )

        def per_row(k):
            return spread(own_spans[:, k * width : (k + 1) * width])

        def per_row_all(k):
            return spread(
                group_spans[:, :, k * width : (k + 1) * width].reshape(PLANE * spans, width)
            )

        def core_swap(source, out, count):
            return [
                (
                    CORE_HOP,
                    source,
                    lambda me, peer, k=k: (k, peer.core),
                    out,
                    lambda me, peer, k=k: (k,),
                    None,
                )
                for k in range(count)
            ]

        def half_of(parts):
            return ((parts.shape[0],) + parts.shape[2:], low)

        def sum_cores(parts, other):
            mine = jnp.where(upper, parts[:, 1], parts[:, 0])
            return (mine.astype(full) + other.astype(full)).astype(low)

        def own_of(values, index):
            return lax.dynamic_index_in_dim(values, index, 0, keepdims=False)

        def z_sum_of(blocks, sent):
            return block_sum(blocks, own_of(sent, z_index))

        def plane_gather(identity, values, *more):
            (out,) = exchange(
                identity,
                [values],
                [((PLANE,) + values.shape, low)],
                gather_moves(PLANE_HOPS, 0, 0, by_chip),
            )
            return put(out, values, chip).reshape(rows_all, width)

        scatter_plan = slotted(PLANE_HOPS, 0, to_chip, 0)
        others = (PLANE - 1, row_count, width)

        def plane_scatter(values):
            return values.astype(low).reshape(PLANE, row_count, width)

        def block_sum(blocks, own):
            return own.astype(full) + jnp.sum(blocks.astype(full), axis=0)

        def plane_sum_of(blocks, sent):
            return block_sum(blocks, lax.dynamic_index_in_dim(sent, chip, 0, keepdims=False))

        def group_span(k):
            return group_spans[:, :, None, k * width : (k + 1) * width]

        gain_pad = jnp.zeros((2, LANES), full)
        gains = lax.dynamic_update_slice(gain_pad, jnp.stack([gain_q, gain_k]), (0, 0))
        hidden_one, qkv_rows, attended_low, attn_terms, proj_slice, up_same = block_call(
            functools.partial(attention_forward_kernel, head_size, heads),
            [
                patch_all,
                group_span(0),
                group_span(1),
                qkv_slice,
                own_columns(qkv_vector, 3)[None],
                gains,
                cos_rows,
                sin_rows,
                meta_rows,
                seg_col,
                proj_z,
                proj_other,
            ],
            [1, 1, 1, 0, 0, 0, 0, 0, 1, 1, 0, 0],
            [
                ((PLANE, row_count, width), low),
                ((PLANE, row_count, 3 * part_cols), full),
                ((PLANE, row_count, part_cols), low),
                ((PLANE, row_count, width), low),
            ],
            [((part_cols, width), low)],
            [],
            PLANE,
            rows_all * width * 8 * part_cols,
            11,
            [up_pieces],
            [(up_pieces.shape, low)],
            [(hop, 0, to_chip, 0, by_chip, None) for hop in PLANE_HOPS + [SELF]],
        )
        plan = scatter_plan + gather_moves(Z_HOPS, 1, 1, by_z)
        plan.append((CORE_HOP, 2, None, 2, None, None))
        branch_blocks, down_z, up_other = exchange(
            4,
            [attn_terms, down_weight, up_same],
            [
                (others, low),
                ((z_size,) + down_weight.shape, low),
                (up_same.shape, low),
            ],
            plan,
        )
        down_z = put(down_z, down_weight, z_index)
        branch_attn = plane_sum_of(branch_blocks, attn_terms) + proj_vector

        patch_full = patches.astype(full)
        scale_one = rms_scale(patch_full)
        normed_one = patch_full * scale_one
        middle = patch_full + per_row(2) * branch_attn
        scale_two = rms_scale(middle)
        normed_two = middle * scale_two
        hidden_two = (normed_two * (1.0 + per_row(4)) + per_row(3)).astype(low)

        hidden_blocks, down_other = exchange(
            5,
            [halves(hidden_two), down_z],
            [((PLANE - 1, 2, row_count // 2, width), low), (down_z.shape, low)],
            relayed(0, 0, hop_place, 0) + [(CORE_HOP, 1, None, 1, None, None)],
        )
        steps = PLANE_HOPS[2:] + PLANE_HOPS[:2]
        gate_spans = xor_order(group_spans[:, :, 5 * width :], chip, PLANE)
        gate_spans = jnp.stack([gate_spans[k] for k in (3, 1, 2, 0)])
        ffn_terms, own_terms, up_bias_cols, up_parts, down_parts, hidden_two_blocks = block_call(
            ffn_kernel,
            [
                hidden_two,
                hidden_blocks.reshape(others),
                out_cotangent,
                cot_blocks.reshape(others),
                gate_spans[:, :, None],
                up_same,
                up_other,
                down_z,
                down_other,
                own_columns(up_vector, 2)[None],
            ],
            [0, 2, 0, 2, 1, 0, 0, 0, 0, 0],
            [((PLANE, row_count, width), low)],
            [
                ((row_count, width), low),
                ((1, 2 * units), full),
                ((PLANE, 2, shard, 2 * units), low),
                ((z_size, 2) + down_weight.shape, low),
            ],
            [
                ((units, width), low),
                ((width, 2 * units), low),
                ((width, 2 * units), full),
                ((units, width), full),
                (others, low),
            ],
            PLANE,
            rows_all * width * 18 * units,
            6,
            [],
            [(others, low)],
            [
                (hop, 0, lambda me, peer, k=k: (k,), 0, lambda me, peer, k=k: (k,), None)
                for k, hop in enumerate(steps)
            ],
        )
        grad_hidden_two = block_sum(hidden_two_blocks, own_terms)

        grad_out = out_cotangent.astype(full)
        own_gbf = (grad_out * per_row(5)).astype(low).astype(full)
        down_bias_grad = jnp.sum(own_gbf, axis=0)
        grad_middle = grad_out + norm_backward(
            grad_hidden_two * (1.0 + per_row(4)), normed_two, scale_two
        )
        grad_gate_attn = grad_middle * branch_attn
        grad_branch_attn = (grad_middle * per_row(2)).astype(low)
        proj_bias_grad = jnp.sum(grad_branch_attn.astype(full), axis=0)
        grad_branch_all, down_swapped, up_swapped = exchange(
            7,
            [halves(grad_branch_attn), down_parts, up_parts],
            [
                ((PLANE, 2, row_count // 2, width), low),
                half_of(down_parts),
                half_of(up_parts),
            ],
            relayed(0, 0, chip_place, 0)
            + core_swap(1, 1, z_size)
            + core_swap(2, 2, PLANE),
        )
        down_mine = sum_cores(down_parts, down_swapped)
        up_mine = sum_cores(up_parts, up_swapped)
        grad_branch_all = put(
            grad_branch_all.reshape(PLANE, row_count, width), grad_branch_attn, chip
        )
        plan = [
            (hop, 0, lambda me, peer, k=k: (k,), 0, lambda me, peer, k=k: (k,), None)
            for k, hop in enumerate(steps)
        ]
        plan += [(hop, 1, to_chip, 1, by_chip, None) for hop in PLANE_HOPS + [SELF]]
        plan += slotted(Z_HOPS, 2, to_z, 2)
        (
            hidden_one_terms,
            qkv_bias_cols,
            gain_grads,
            qkv_parts,
            proj_parts,
            ffn_blocks,
            up_moved,
            down_blocks,
        ) = block_call(
            functools.partial(attention_backward_kernel, head_size, heads),
            [
                grad_branch_all,
                qkv_rows,
                qkv_slice,
                gains,
                cos_rows,
                sin_rows,
                meta_rows,
                seg_col,
                proj_slice,
                hidden_one,
                attended_low,
            ],
            [1, 1, 0, 0, 0, 0, 1, 1, 0, 1, 1],
            [((PLANE, row_count, width), low)],
            [
                ((1, 3 * part_cols), full),
                ((2, LANES), full),
                ((PLANE, 2, shard, 3 * part_cols), low),
                ((z_size, 2) + proj_weight.shape, low),
            ],
            [((width, 3 * part_cols), full), ((part_cols, width), full)],
            PLANE,
            rows_all * width * 18 * part_cols,
            12,
            [ffn_terms, up_mine, down_mine],
            [
                (others, low),
                (up_mine.shape, low),
                ((z_size - 1,) + down_mine.shape[1:], low),
            ],
            plan,
        )
        gain_q_grad, gain_k_grad = gain_grads[0, :head_size], gain_grads[1, :head_size]
        up_wide = whole_call(functools.partial(merge_kernel, 2), up_moved)
        hidden_one_terms, up_wide = tie(hidden_one_terms, up_wide)
        up_grad = lax.psum_scatter(up_wide, "fsdp", scatter_dimension=0, tiled=False).astype(full)
        hidden_one_blocks, qkv_other, proj_other = exchange(
            8,
            [hidden_one_terms, qkv_parts, proj_parts],
            [(others, low), half_of(qkv_parts), half_of(proj_parts)],
            scatter_plan + core_swap(1, 1, PLANE) + core_swap(2, 2, z_size),
        )
        grad_hidden_one = plane_sum_of(hidden_one_blocks, hidden_one_terms)
        branch_ffn = block_sum(ffn_blocks, ffn_terms[PLANE - 1]) + down_vector
        down_grad = z_sum_of(down_blocks, down_mine)
        block_out = (middle + per_row(5) * branch_ffn).astype(low)
        grad_gate_ffn = grad_out * branch_ffn
        qkv_mine = sum_cores(qkv_parts, qkv_other)
        proj_mine = sum_cores(proj_parts, proj_other)
        patch_grad = (
            grad_middle + norm_backward(grad_hidden_one * (1.0 + per_row(1)), normed_one, scale_one)
        ).astype(low)

        def span_sum(values):
            return jnp.sum(values.reshape(spans, SPAN, width), axis=1)

        grad_spans = jnp.concatenate(
            [
                span_sum(grad_hidden_one),
                span_sum(grad_hidden_one * normed_one),
                span_sum(grad_gate_attn),
                span_sum(grad_hidden_two),
                span_sum(grad_hidden_two * normed_two),
                span_sum(grad_gate_ffn),
            ],
            axis=1,
        )
        grad_modulation = jnp.sum(own_hot[:, :, None] * grad_spans[:, None, :], axis=0).astype(low)
        grad_mod = grad_modulation.reshape(slots, z_size, mod_cols).transpose(1, 0, 2)

        def place(flat, groups):
            spot = (jnp.arange(PLANE) == chip).astype(full)
            return (flat.reshape(groups, 1, -1) * spot[None, :, None]).reshape(-1)

        rows = [
            place(qkv_bias_cols, 3),
            proj_bias_grad,
            place(up_bias_cols, 2),
            down_bias_grad,
            gain_q_grad,
            gain_k_grad,
        ]
        vector_grad = jnp.concatenate([r.reshape(z_size, 1, -1) for r in rows], axis=2)
        plan = [
            (hop, 1, to_z, 1, lambda me, peer: (me.dp, me.z), None) for hop in Z_HOPS + [SELF]
        ]
        plan += [(hop, 2, to_z, 2, by_z, None) for hop in Z_HOPS + [SELF]]
        plan += [(hop, 0, to_chip, 0, by_chip, None) for hop in PLANE_HOPS]
        plan += [(hop, 1, by_dp, 1, by_dp, (0, 1, 2, 3)) for hop in DP_HOPS if hop != SELF]
        plan += slotted(Z_HOPS, 3, to_z, 3)
        qkv_moved, grad_mod, vector_parts, proj_blocks = exchange(
            9,
            [qkv_mine, grad_mod, vector_grad, proj_mine],
            [
                (qkv_mine.shape, low),
                ((2 * PLANE, z_size, slots, mod_cols), low),
                (vector_grad.shape, full),
                ((z_size - 1,) + proj_mine.shape[1:], low),
            ],
            plan,
        )
        proj_grad = z_sum_of(proj_blocks, proj_mine)
        qkv_wide = whole_call(
            functools.partial(merge_kernel, 3), put(qkv_moved, own_of(qkv_mine, chip), chip)
        )
        grad_mod = grad_mod.reshape(-1, mod_cols)
        vector_sum = jnp.sum(vector_parts, axis=0)
        cond_part = dot_t(grad_mod, mod_weight).reshape(2 * PLANE, z_size, slots, mod_rows)
        plan = slotted(Z_HOPS, 0, to_z, 0)
        plan += [
            (
                hop,
                1,
                lambda me, peer: (peer.dp, peer.z),
                1,
                lambda me, peer: (me.dp, me.z),
                None,
            )
            for hop in ALL_HOPS
        ]
        plan += gather_moves(DP_HOPS, 2, 2, by_dp)
        qkv_blocks, cond_parts, vector_parts = exchange(
            10,
            [qkv_wide, cond_part, vector_sum],
            [
                ((z_size - 1,) + qkv_wide.shape[1:], low),
                (cond_part.shape, full),
                ((2 * PLANE,) + vector_sum.shape, full),
            ],
            plan,
        )
        qkv_grad = z_sum_of(qkv_blocks, qkv_wide)
        mod_bias_grad = jnp.sum(grad_mod.astype(full), axis=0)
        mod_grad = outer_grad(silu_cols, grad_mod)
        cond_part = jnp.sum(cond_parts, axis=1)
        cond_grad = (
            cond_part.transpose(1, 0, 2).reshape(slots, width) * silu_slope(cond_full)
        ).astype(low)
        vector_grad = jnp.sum(vector_parts, axis=0)[0]
        out = [vector_grad[bounds[k] : bounds[k + 1]] for k in range(6)]
        return (
            block_out,
            patch_grad,
            cond_grad,
            mod_grad,
            mod_bias_grad,
            qkv_grad,
            out[0],
            jnp.stack([out[4], out[5]]),
            proj_grad,
            out[1],
            up_grad,
            out[2],
            down_grad,
            out[3],
        )

    return per_device


def solution(mesh):
    if mesh.shape["dp"] == 2 * PLANE and mesh.shape["fsdp"] == 4:
        body = make_plane(mesh.shape["fsdp"])
    else:
        body = make_plain(mesh.shape["dp"], mesh.shape["fsdp"])
    rows = P(("dp", "fsdp"), None)
    matrix = P("dp", "fsdp")
    vector = P("fsdp")
    gains = P(None, "fsdp")
    return jax.shard_map(
        body,
        mesh=mesh,
        in_specs=(
            rows,
            rows,
            P(("dp", "fsdp")),
            P(None, ("dp", "fsdp")),
            matrix,
            vector,
            matrix,
            vector,
            gains,
            matrix,
            vector,
            matrix,
            vector,
            matrix,
            vector,
            rows,
        ),
        out_specs=(
            rows,
            rows,
            rows,
            matrix,
            vector,
            matrix,
            vector,
            gains,
            matrix,
            vector,
            matrix,
            vector,
            matrix,
            vector,
        ),
        check_vma=False,
    )
```

```python
import functools

import jax
import jax.numpy as jnp
import numpy as np
from jax import lax
from jax.experimental import pallas as pl
from jax.experimental.pallas import tpu as pltpu
from jax.sharding import PartitionSpec as P

HEADS = 16
SPAN = 64
SIDE = 16

epsilon = 1e-06
low = jnp.bfloat16
full = jnp.float32


def rms_scale(values):
    return lax.rsqrt(jnp.mean(values * values, axis=-1, keepdims=True) + epsilon)


def norm_backward(grad_normed, normed, factor):
    return factor * (grad_normed - normed * jnp.mean(grad_normed * normed, axis=-1, keepdims=True))


def rotary_tables(coord_rows, quarter):
    frequencies = 10000.0 ** (-jnp.arange(quarter, dtype=full) / quarter)
    row_angle = coord_rows[0].astype(full)[:, None, None] * frequencies
    col_angle = coord_rows[1].astype(full)[:, None, None] * frequencies
    return (jnp.cos(row_angle), jnp.sin(row_angle), jnp.cos(col_angle), jnp.sin(col_angle))


def rotate(values, tables, direction):
    half_size = values.shape[-1] // 2
    quarter = half_size // 2
    pieces_out = []
    for which_half in range(2):
        cosine = tables[2 * which_half]
        sine_tab = direction * tables[2 * which_half + 1]
        start_col = which_half * half_size
        first_part = values[..., start_col : start_col + quarter]
        second = values[..., start_col + quarter : start_col + half_size]
        pieces_out.append(first_part * cosine - second * sine_tab)
        pieces_out.append(second * cosine + first_part * sine_tab)
    return jnp.concatenate(pieces_out, axis=-1)


def dot(left, right):
    return jnp.dot(left, right, preferred_element_type=full)


def dot_t(left, right):
    return lax.dot_general(left, right, (((1,), (1,)), ((), ())), preferred_element_type=full)


def outer_grad(left, right):
    return lax.dot_general(left, right, (((0,), (0,)), ((), ())), preferred_element_type=full)


def silu_slope(values):
    sigmoid_gate = jax.nn.sigmoid(values)
    return sigmoid_gate * (1.0 + values * (1.0 - sigmoid_gate))


def swap(values, axis, size, bit):
    return lax.ppermute(values, axis, [(k, k ^ bit) for k in range(size)])


def bits_of(size):
    return [1 << b for b in range(size.bit_length() - 1)]


def gather_small(values, axis, size):
    index = lax.axis_index(axis)
    for bit in bits_of(size):
        other = swap(values, axis, size, bit)
        upper = (index & bit) != 0
        values = jnp.concatenate(
            [jnp.where(upper, other, values), jnp.where(upper, values, other)], axis=0
        )
    return values


def scatter_sum_small(values, axis, size):
    index = lax.axis_index(axis)
    for bit in reversed(bits_of(size)):
        half = values.shape[0] // 2
        upper = (index & bit) != 0
        first, second = values[:half], values[half:]
        values = jnp.where(upper, second, first) + swap(
            jnp.where(upper, first, second), axis, size, bit
        )
    return values


def sum_small(values, axis, size):
    for bit in bits_of(size):
        values = values + swap(values, axis, size, bit)
    return values


def xor_order(values, index, size):
    tail = values.shape[1:]
    for bit in bits_of(size):
        paired = values.reshape((size // (2 * bit), 2, bit) + tail)
        values = jnp.where((index & bit) != 0, jnp.flip(paired, axis=1), paired)
        values = values.reshape((size,) + tail)
    return values


def exchange_small(values, axis, size):
    index = lax.axis_index(axis)
    tail = values.shape[1:]
    values = xor_order(values, index, size)
    for bit in bits_of(size):
        paired = values.reshape((size // (2 * bit), 2, bit) + tail)
        moved = swap(paired[:, 1], axis, size, bit)
        values = jnp.stack([paired[:, 0], moved], axis=1).reshape((size,) + tail)
    return xor_order(values, index, size)


def gather_weight(weight, dp_size, fsdp_size):
    rows, cols = weight.shape
    whole = lax.all_gather(weight, ("dp", "fsdp"), axis=0, tiled=False)
    whole = whole.reshape(dp_size, fsdp_size, rows, cols).transpose(1, 0, 2, 3)
    return whole.reshape(fsdp_size, dp_size * rows, cols)


def scatter_grad(blocks, dp_size):
    rows, cols = blocks[0].shape
    parts = jnp.stack([b.reshape(dp_size, rows // dp_size, cols) for b in blocks], axis=1)
    parts = lax.psum_scatter(parts, "dp", scatter_dimension=0, tiled=False)
    return lax.psum_scatter(parts, "fsdp", scatter_dimension=0, tiled=False).astype(full)


def masked_scores(query_low, key_low, same_item, score_scale):
    scores = jnp.einsum("qhd,khd->hqk", query_low, key_low, preferred_element_type=full)
    return jnp.where(same_item, scores * score_scale, -1e30)


def make_plain(dp_size, fsdp_size):
    def per_device(
        patches,
        conditions,
        segment_ids,
        grid_coords,
        mod_weight,
        mod_bias,
        qkv_weight,
        qkv_bias,
        qk_gains,
        proj_weight,
        proj_bias,
        up_weight,
        up_bias,
        down_weight,
        down_bias,
        out_cotangent,
    ):
        row_count, model_width = patches.shape
        slots = conditions.shape[0]
        spans = row_count // SPAN
        head_size = model_width // HEADS
        score_scale = head_size ** (-0.5)
        head_shape = (row_count, HEADS, head_size)
        dp_index = lax.axis_index("dp")
        mod_rows, mod_cols = mod_weight.shape

        qkv_full = gather_weight(qkv_weight, dp_size, fsdp_size)
        proj_full = gather_weight(proj_weight, dp_size, fsdp_size)
        up_full = gather_weight(up_weight, dp_size, fsdp_size)
        down_full = gather_weight(down_weight, dp_size, fsdp_size)

        gain_cols = qk_gains.shape[1]
        sizes = [qkv_bias.shape[0], proj_bias.shape[0], up_bias.shape[0], down_bias.shape[0]]
        vector = jnp.concatenate(
            [qkv_bias, proj_bias, up_bias, down_bias, qk_gains[0], qk_gains[1]]
        )
        vectors = gather_small(vector[None], "fsdp", fsdp_size).astype(full)
        bounds = [0]
        for size in sizes + [gain_cols, gain_cols]:
            bounds.append(bounds[-1] + size)
        pieces = [vectors[:, bounds[k] : bounds[k + 1]] for k in range(6)]
        qkv_vector, proj_vector, up_vector, down_vector, gain_q, gain_k = [
            p.reshape(-1) for p in pieces
        ]

        cond_full = conditions.astype(full)
        silu_low = jax.nn.silu(cond_full).astype(low)
        silu_all = gather_small(
            gather_small(silu_low[None], "fsdp", fsdp_size)[None], "dp", dp_size
        ).reshape(dp_size * fsdp_size * slots, model_width)
        silu_cols = lax.dynamic_slice_in_dim(silu_all, dp_index * mod_rows, mod_rows, axis=1)
        mod_part = dot(silu_cols, mod_weight).reshape(dp_size, fsdp_size, slots, mod_cols)
        mod_sum = scatter_sum_small(mod_part, "dp", dp_size)[0] + mod_bias.astype(full)
        modulation = exchange_small(mod_sum, "fsdp", fsdp_size)
        modulation = modulation.transpose(1, 0, 2).reshape(slots, fsdp_size * mod_cols)
        span_ids = segment_ids.reshape(spans, SPAN)[:, 0]
        span_hot = (span_ids[:, None] == jnp.arange(slots, dtype=jnp.int32)[None, :]).astype(full)
        span_mod = jnp.sum(span_hot[:, :, None] * modulation[None], axis=1)

        def per_row(k):
            part = span_mod[:, k * model_width : (k + 1) * model_width]
            return jnp.broadcast_to(part[:, None, :], (spans, SPAN, model_width)).reshape(
                row_count, model_width
            )

        shift_attn, scale_attn, gate_attn, shift_ffn, scale_ffn, gate_ffn = map(per_row, range(6))

        def cols_of(blocks):
            return jnp.concatenate(blocks, axis=1)

        def forward_dot(rows_low, weight_full):
            return cols_of([dot(rows_low, weight_full[j]) for j in range(fsdp_size)])

        def split(values):
            width = values.shape[1] // fsdp_size
            return [values[:, j * width : (j + 1) * width] for j in range(fsdp_size)]

        def backward_dot(grad_low, weight_full):
            parts = split(grad_low)
            total = dot_t(parts[0], weight_full[0])
            for j in range(1, fsdp_size):
                total = total + dot_t(parts[j], weight_full[j])
            return total

        def weight_grad(rows_low, grad_low):
            return scatter_grad(
                [outer_grad(rows_low, part).astype(low) for part in split(grad_low)], dp_size
            )

        tables = rotary_tables(grid_coords, head_size // 4)
        patch_full = patches.astype(full)
        scale_one = rms_scale(patch_full)
        normed_one = patch_full * scale_one
        hidden_one = (normed_one * (1.0 + scale_attn) + shift_attn).astype(low)
        qkv_rows = forward_dot(hidden_one, qkv_full) + qkv_vector
        query_raw = qkv_rows[:, 0:model_width].reshape(head_shape)
        key_raw = qkv_rows[:, model_width : 2 * model_width].reshape(head_shape)
        value_low = qkv_rows[:, 2 * model_width :].reshape(head_shape).astype(low)
        query_scale = rms_scale(query_raw)
        query_unit = query_raw * query_scale
        key_scale = rms_scale(key_raw)
        key_unit = key_raw * key_scale
        query_low = rotate(query_unit * gain_q, tables, 1.0).astype(low)
        key_low = rotate(key_unit * gain_k, tables, 1.0).astype(low)
        same_item = (segment_ids[:, None] == segment_ids[None, :])[None]
        scores = masked_scores(query_low, key_low, same_item, score_scale)
        exponentials = jnp.exp(scores - jnp.max(scores, axis=-1, keepdims=True))
        probs = exponentials / jnp.sum(exponentials, axis=-1, keepdims=True)
        probs_low = probs.astype(low)
        attended_low = (
            jnp.einsum("hqk,khd->qhd", probs_low, value_low, preferred_element_type=full)
            .reshape(row_count, model_width)
            .astype(low)
        )
        branch_attn = forward_dot(attended_low, proj_full) + proj_vector
        middle = patch_full + gate_attn * branch_attn
        scale_two = rms_scale(middle)
        normed_two = middle * scale_two
        hidden_two = (normed_two * (1.0 + scale_ffn) + shift_ffn).astype(low)
        gate_up = forward_dot(hidden_two, up_full) + up_vector
        hidden_units = gate_up.shape[1] // 2
        gate_part = gate_up[:, :hidden_units]
        up_part = gate_up[:, hidden_units:]
        gated_low = (jax.nn.silu(gate_part) * up_part).astype(low)
        branch_ffn = forward_dot(gated_low, down_full) + down_vector
        block_out = (middle + gate_ffn * branch_ffn).astype(low)

        grad_out = out_cotangent.astype(full)
        grad_gate_ffn = grad_out * branch_ffn
        grad_branch_ffn = (grad_out * gate_ffn).astype(low)
        down_bias_grad = jnp.sum(grad_branch_ffn.astype(full), axis=0)
        grad_gated = backward_dot(grad_branch_ffn, down_full)
        down_grad = weight_grad(gated_low, grad_branch_ffn)
        grad_gate_up = jnp.concatenate(
            [grad_gated * up_part * silu_slope(gate_part), grad_gated * jax.nn.silu(gate_part)],
            axis=1,
        ).astype(low)
        up_bias_grad = jnp.sum(grad_gate_up.astype(full), axis=0)
        grad_hidden_two = backward_dot(grad_gate_up, up_full)
        up_grad = weight_grad(hidden_two, grad_gate_up)
        grad_middle = grad_out + norm_backward(
            grad_hidden_two * (1.0 + scale_ffn), normed_two, scale_two
        )
        grad_gate_attn = grad_middle * branch_attn
        grad_branch_attn = (grad_middle * gate_attn).astype(low)
        proj_bias_grad = jnp.sum(grad_branch_attn.astype(full), axis=0)
        grad_attended = backward_dot(grad_branch_attn, proj_full).astype(low).reshape(head_shape)
        proj_grad = weight_grad(attended_low, grad_branch_attn)
        grad_probs = jnp.einsum(
            "qhd,khd->hqk", grad_attended, value_low, preferred_element_type=full
        )
        row_dot = jnp.sum(probs * grad_probs, axis=-1, keepdims=True)
        grad_scores = (probs * (grad_probs - row_dot)).astype(low)
        grad_values = jnp.einsum(
            "hqk,qhd->khd", probs_low, grad_attended, preferred_element_type=full
        )
        grad_query_rot = score_scale * jnp.einsum(
            "hqk,khd->qhd", grad_scores, key_low, preferred_element_type=full
        )
        grad_key_rot = score_scale * jnp.einsum(
            "hqk,qhd->khd", grad_scores, query_low, preferred_element_type=full
        )
        back_query = rotate(grad_query_rot, tables, -1.0)
        back_key = rotate(grad_key_rot, tables, -1.0)
        gain_q_grad = jnp.sum(back_query * query_unit, axis=(0, 1))
        gain_k_grad = jnp.sum(back_key * key_unit, axis=(0, 1))
        grad_query_raw = norm_backward(back_query * gain_q, query_unit, query_scale)
        grad_key_raw = norm_backward(back_key * gain_k, key_unit, key_scale)
        grad_qkv = jnp.concatenate(
            [
                grad_query_raw.reshape(row_count, model_width),
                grad_key_raw.reshape(row_count, model_width),
                grad_values.reshape(row_count, model_width),
            ],
            axis=1,
        ).astype(low)
        qkv_grad = weight_grad(hidden_one, grad_qkv)
        qkv_bias_grad = jnp.sum(grad_qkv.astype(full), axis=0)
        grad_hidden_one = backward_dot(grad_qkv, qkv_full)
        patch_grad = (
            grad_middle + norm_backward(grad_hidden_one * (1.0 + scale_attn), normed_one, scale_one)
        ).astype(low)

        def span_sum(values):
            return jnp.sum(values.reshape(spans, SPAN, model_width), axis=1)

        grad_spans = jnp.concatenate(
            [
                span_sum(grad_hidden_one),
                span_sum(grad_hidden_one * normed_one),
                span_sum(grad_gate_attn),
                span_sum(grad_hidden_two),
                span_sum(grad_hidden_two * normed_two),
                span_sum(grad_gate_ffn),
            ],
            axis=1,
        )
        grad_modulation = jnp.sum(span_hot[:, :, None] * grad_spans[:, None, :], axis=0).astype(low)
        grad_mod = grad_modulation.reshape(slots, fsdp_size, mod_cols).transpose(1, 0, 2)
        grad_mod = exchange_small(grad_mod, "fsdp", fsdp_size)
        grad_mod = gather_small(grad_mod[None], "dp", dp_size).reshape(-1, mod_cols)
        mod_bias_grad = jnp.sum(grad_mod.astype(full), axis=0)
        mod_grad = outer_grad(silu_cols, grad_mod)
        cond_part = dot_t(grad_mod, mod_weight).reshape(dp_size, fsdp_size, slots, mod_rows)
        cond_part = scatter_sum_small(cond_part.transpose(1, 0, 2, 3), "fsdp", fsdp_size)[0]
        cond_part = exchange_small(cond_part, "dp", dp_size)
        cond_grad = (
            cond_part.transpose(1, 0, 2).reshape(slots, model_width) * silu_slope(cond_full)
        ).astype(low)

        rows = [qkv_bias_grad, proj_bias_grad, up_bias_grad, down_bias_grad, gain_q_grad, gain_k_grad]
        vector_grad = jnp.concatenate([r.reshape(fsdp_size, -1) for r in rows], axis=1)
        vector_grad = scatter_sum_small(vector_grad, "fsdp", fsdp_size)
        vector_grad = sum_small(vector_grad, "dp", dp_size)[0]
        out = [vector_grad[bounds[k] : bounds[k + 1]] for k in range(6)]
        return (
            block_out,
            patch_grad,
            cond_grad,
            mod_grad,
            mod_bias_grad,
            qkv_grad,
            out[0],
            jnp.stack([out[4], out[5]]),
            proj_grad,
            out[1],
            up_grad,
            out[2],
            down_grad,
            out[3],
        )

    return per_device


PLANE = 4


def cross(values, hop):
    return lax.ppermute(values, "dp", [(k, k ^ (2 * hop)) for k in range(2 * PLANE)])


def partner(values):
    return lax.ppermute(values, "dp", [(k, k ^ 1) for k in range(2 * PLANE)])


def along(values, hop, size):
    return lax.ppermute(values, "fsdp", [(k, k ^ hop) for k in range(size)])


def plane_blocks(values):
    return [values] + [cross(values, hop) for hop in range(1, PLANE)]


def plane_sum(blocks):
    total = blocks[0]
    for hop in range(1, PLANE):
        total = total + cross(blocks[hop].astype(low), hop).astype(full)
    return total


def z_blocks(values, index, size):
    blocks = jnp.stack([values] + [along(values, hop, size) for hop in range(1, size)])
    return xor_order(blocks, index, size)


def z_exchange(values, index, size):
    values = xor_order(values, index, size)
    moved = jnp.stack([values[0]] + [along(values[hop], hop, size) for hop in range(1, size)])
    return xor_order(moved, index, size)


def z_sum_own(values, index, size):
    values = xor_order(values, index, size)
    total = values[0].astype(full)
    for hop in range(1, size):
        total = total + along(values[hop], hop, size).astype(full)
    return total


class Place:
    def __init__(self, y, x, core, z):
        self.y, self.x, self.core, self.z = y, x, core, z
        self.chip = 2 * y + x
        self.dp = 2 * self.chip + core

    def hop(self, dy, dx, dc, dz):
        low_z, high_z = self.z % 2, self.z // 2
        low_z = 1 - low_z if dz & 1 else low_z
        high_z = 1 - high_z if dz & 2 else high_z
        return Place(
            1 - self.y if dy else self.y,
            1 - self.x if dx else self.x,
            1 - self.core if dc else self.core,
            2 * high_z + low_z,
        )


SELF = (0, 0, 0, 0)
PLANE_HOPS = [(0, 1, 0, 0), (1, 0, 0, 0), (1, 1, 0, 0)]
Z_HOPS = [(0, 0, 0, 1), (0, 0, 0, 2), (0, 0, 0, 3)]
CORE_HOP = (0, 0, 1, 0)
DP_HOPS = [(dy, dx, dc, 0) for dy in (0, 1) for dx in (0, 1) for dc in (0, 1)]
ALL_HOPS = [(dy, dx, dc, dz) for dz in range(4) for dy, dx, dc, _ in DP_HOPS]
GROUP_HOPS = [(dy, dx, 0, dz) for dz in range(4) for dy in (0, 1) for dx in (0, 1)]


class Copies:
    def __init__(self, plan, ins, outs, send, recv):
        self.plan, self.ins, self.outs, self.send, self.recv = plan, ins, outs, send, recv

    def here(self):
        dp_index = lax.axis_index("dp")
        return Place(dp_index // 4, (dp_index // 2) % 2, dp_index % 2, lax.axis_index("fsdp"))

    def greet(self):
        hops = []
        for move in self.plan:
            if move[0] != SELF and move[0] not in hops:
                hops.append(move[0])
        barrier = pltpu.get_barrier_semaphore()
        for hop in hops:
            peer = self.here().hop(*hop)
            pl.semaphore_signal(
                barrier,
                1,
                device_id={"dp": peer.dp, "fsdp": peer.z},
                device_id_type=pl.DeviceIdType.MESH,
            )
        pl.semaphore_wait(barrier, len(hops))

    def copy(self, number):
        hop, source, source_at, out, out_at, after = self.plan[number]
        me = self.here()
        peer = me.hop(*hop)
        src = (self.ins if after is None else self.outs)[source]
        src = src if source_at is None else src.at[source_at(me, peer)]
        dst = self.outs[out]
        dst = dst if out_at is None else dst.at[out_at(me, peer)]
        if hop == SELF:
            return pltpu.make_async_copy(src, dst, self.send.at[number])
        return pltpu.make_async_remote_copy(
            src_ref=src,
            dst_ref=dst,
            send_sem=self.send.at[number],
            recv_sem=self.recv.at[number],
            device_id={"dp": peer.dp, "fsdp": peer.z},
            device_id_type=pl.DeviceIdType.MESH,
        )

    def start(self, number):
        self.copy(number).start()

    def wait_arrival(self, number):
        if self.plan[number][0] == SELF:
            self.copy(number).wait()
        else:
            self.copy(number).wait_recv()

    def finish(self, arrived=()):
        for number, move in enumerate(self.plan):
            if number not in arrived:
                self.wait_arrival(number)
            if move[0] != SELF:
                self.copy(number).wait_send()


def exchange(identity, inputs, out_shapes, plan):
    def kernel(*refs):
        ins, outs = refs[: len(inputs)], refs[len(inputs) : len(inputs) + len(out_shapes)]
        copies = Copies(plan, ins, outs, *refs[-2:])
        copies.greet()
        done = set()
        for number, move in enumerate(plan):
            for earlier in move[5] or ():
                if earlier not in done:
                    copies.wait_arrival(earlier)
                    done.add(earlier)
            copies.start(number)
        copies.finish(done)

    anywhere = pl.BlockSpec(memory_space=pl.ANY)
    return pl.pallas_call(
        kernel,
        out_shape=[jax.ShapeDtypeStruct(shape, dtype) for shape, dtype in out_shapes],
        in_specs=[anywhere] * len(inputs),
        out_specs=[anywhere] * len(out_shapes),
        scratch_shapes=[
            pltpu.SemaphoreType.DMA((len(plan),)),
            pltpu.SemaphoreType.DMA((len(plan),)),
        ],
        compiler_params=pltpu.CompilerParams(collective_id=identity, has_side_effects=True),
    )(*inputs)


def gather_moves(hops, source, out, out_at):
    return [(hop, source, None, out, out_at, None) for hop in hops]


def by_chip(me, peer):
    return (me.chip,)


def by_dp(me, peer):
    return (me.dp,)


def by_z(me, peer):
    return (me.z,)


def by_core(me, peer):
    return (me.core,)


def tie(first, second):
    return lax.optimization_barrier((first, second))


def put(values, own, *at):
    start = tuple(at) + (0,) * (values.ndim - len(at))
    return lax.dynamic_update_slice(values, own.reshape((1,) * len(at) + own.shape), start)


HOP_X, HOP_Y = PLANE_HOPS[0], PLANE_HOPS[1]


def relayed(source, out, place, first):
    def at(hop, half):
        return lambda me, peer: (place(me, hop), half)

    def onto(hop, half):
        return lambda me, peer: (place(peer, hop), half)

    def part(half):
        return lambda me, peer: (half,)

    diagonal = PLANE_HOPS[2]
    return [
        (HOP_X, source, part(0), out, onto(HOP_X, 0), None),
        (HOP_Y, source, part(1), out, onto(HOP_Y, 1), None),
        (HOP_X, source, part(1), out, onto(HOP_X, 1), None),
        (HOP_Y, source, part(0), out, onto(HOP_Y, 0), None),
        (HOP_Y, out, at(HOP_X, 0), out, onto(diagonal, 0), (first,)),
        (HOP_X, out, at(HOP_Y, 1), out, onto(diagonal, 1), (first + 1,)),
    ]


def chip_place(me, hop):
    return me.hop(*hop).chip


def hop_place(me, hop):
    return PLANE_HOPS.index(hop)


def slotted(hops, source, source_at, out):
    return [
        (hop, source, source_at, out, lambda me, peer, n=n: (n,), None)
        for n, hop in enumerate(hops)
    ]


def to_chip(me, peer):
    return (peer.chip,)


def to_z(me, peer):
    return (peer.z,)


LANES = 128


def head_of(values, number, head_size):
    part = values[:, number * head_size : (number + 1) * head_size]
    pad = jnp.zeros((values.shape[0], LANES - head_size), values.dtype)
    return jnp.concatenate([part, pad], axis=1)


def pair_of(values, head_size):
    quarter = head_size // 4
    lane = lax.broadcasted_iota(jnp.int32, values.shape, 1)
    second = (lane // quarter) % 2 == 1
    return jnp.where(
        second, pltpu.roll(values, quarter, 1), pltpu.roll(values, LANES - quarter, 1)
    )


def unit_of(raw, head_size):
    factor = lax.rsqrt(jnp.sum(raw * raw, axis=1, keepdims=True) * (1.0 / head_size) + epsilon)
    return raw * factor, factor


def head_probs(query, key, same, score_scale):
    scores = jnp.where(same, dot_t(query, key) * score_scale, -1e30)
    exponentials = jnp.exp(scores - jnp.max(scores, axis=1, keepdims=True))
    return exponentials * (1.0 / jnp.sum(exponentials, axis=1, keepdims=True))


def rotary_rows(head_size):
    quarter = head_size // 4
    frequencies = np.float32(10000.0) ** (-np.arange(quarter, dtype=np.float32) / quarter)
    angles = np.arange(SIDE, dtype=np.float32)[:, None] * frequencies.astype(np.float32)
    cosine = np.zeros((2, SIDE, LANES), np.float32)
    sine = np.zeros((2, SIDE, LANES), np.float32)
    for k in range(2):
        first = 2 * quarter * k
        cosine[k, :, first : first + 2 * quarter] = np.tile(np.cos(angles), (1, 2))
        sine[k, :, first : first + quarter] = -np.sin(angles)
        sine[k, :, first + quarter : first + 2 * quarter] = np.sin(angles)
    return jnp.asarray(cosine.reshape(-1, LANES)), jnp.asarray(sine.reshape(-1, LANES))


def rotary_of(meta, cosine_rows, sine_rows):
    place = lax.broadcasted_iota(jnp.int32, (meta.shape[0], 2 * SIDE), 1)
    hot = (meta[:, 1:2] == place) | (meta[:, 2:3] + SIDE == place)
    hot = hot.astype(full)
    take = functools.partial(jnp.dot, preferred_element_type=full, precision=lax.Precision.HIGHEST)
    return take(hot, cosine_rows), take(hot, sine_rows)


def attention_block(head_size, heads, refs):
    (rows, gains, cosine, sine, seg_row, seg_col) = refs
    same = seg_row == seg_col
    gain_q, gain_k = gains[0:1], gains[1:2]
    for h in range(heads):
        query_unit, query_factor = unit_of(head_of(rows, h, head_size), head_size)
        key_unit, key_factor = unit_of(head_of(rows, heads + h, head_size), head_size)
        query = query_unit * gain_q
        key = key_unit * gain_k
        query = (query * cosine + pair_of(query, head_size) * sine).astype(low)
        key = (key * cosine + pair_of(key, head_size) * sine).astype(low)
        value = head_of(rows, 2 * heads + h, head_size).astype(low)
        probs = head_probs(query, key, same, head_size ** (-0.5))
        yield query_unit, query_factor, key_unit, key_factor, query, key, value, probs


def fill_rows(target, mine, other):
    rows = mine.shape[1]
    core = lax.axis_index("dp") % 2
    for source, place in ((mine, core), (other, 1 - core)):
        target[pl.ds(pl.multiple_of(place * rows, 16), rows), :] = jnp.concatenate(
            [source[j] for j in range(source.shape[0])], axis=1
        )


def attention_forward_kernel(head_size, heads, copies, rest, *refs):
    (own_patch, patches, shift, scale, weight, bias, gains, cos_rows, sin_rows) = refs[:9]
    meta, seg_col, proj_mine, proj_other = refs[9:13]
    hidden_out, rows_out, attended_out, own_terms, proj, terms = refs[13:]
    copies.ins = list(copies.ins) + [terms]
    step, last = pl.program_id(0), pl.num_programs(0) - 1
    first = len(copies.plan) - (PLANE - 1)

    @pl.when(step == 0)
    def _():
        copies.greet()
        for number in range(first):
            copies.start(number)
        fill_rows(proj, proj_mine, proj_other)

    cosine, sine = rotary_of(meta[0], cos_rows[...], sin_rows[...])
    values = jnp.where(step == last, own_patch[...], patches[0]).astype(full)
    count, width = values.shape
    normed = values * lax.rsqrt(jnp.mean(values * values, axis=1, keepdims=True) + epsilon)
    hidden = normed.reshape(count // SPAN, SPAN, width) * (1.0 + scale[0]) + shift[0]
    hidden = hidden.reshape(count, width).astype(low)
    hidden_out[0] = hidden
    rows = dot(hidden, weight[...]) + bias[...]
    rows_out[0] = rows
    pieces = []
    refs = (rows, gains[...], cosine, sine, meta[0, :, 0:1], seg_col[0])
    for *_, value, probs in attention_block(head_size, heads, refs):
        pieces.append(dot(probs.astype(low), value)[:, :head_size])
    attended = jnp.concatenate(pieces, axis=1).astype(low)
    attended_out[0] = attended

    for number in range(PLANE - 1):
        @pl.when(step == number + 1)
        def _(number=number):
            copies.start(first + number)

    term = dot(attended, proj[...]).astype(low)

    @pl.when(step < last)
    def _():
        terms[step] = term

    @pl.when(step == last)
    def _():
        own_terms[...] = term
        copies.finish()


def cut_columns(parts, total):
    cols = parts.shape[3]
    for j in range(parts.shape[0]):
        parts[j] = total[:, j * cols : (j + 1) * cols].astype(low).reshape(parts.shape[1:])


def attention_backward_kernel(head_size, heads, copies, rest, *refs):
    (own_grad, grads, rows, weight, gains, cos_rows, sin_rows, meta, seg_col, proj) = refs[:10]
    hidden, attended = refs[10:12]
    terms_out, bias_out, gains_out, qkv_parts, proj_parts = refs[12:17]
    qkv_total, proj_total = refs[17:]

    @pl.when(pl.program_id(0) == 0)
    def _():
        bias_out[...] = jnp.zeros_like(bias_out)
        gains_out[...] = jnp.zeros_like(gains_out)
        qkv_total[...] = jnp.zeros_like(qkv_total)
        proj_total[...] = jnp.zeros_like(proj_total)
        copies.greet()
        for number in range(len(copies.plan)):
            copies.start(number)

    score_scale = head_size ** (-0.5)
    gain_values = gains[...]
    cos_tab, sin_tab = rotary_of(meta[0], cos_rows[...], sin_rows[...])
    own_step = pl.program_id(0) == pl.num_programs(0) - 1
    grad = jnp.where(own_step, own_grad[...], grads[0])
    grad_attended = dot_t(grad, proj[...])
    values = rows[0]
    grad_queries, grad_keys, grad_values = [], [], []
    gain_sums = [jnp.zeros((1, LANES), full), jnp.zeros((1, LANES), full)]

    def raw_grad(rotated, unit, factor, which):
        back = rotated * cos_tab - pair_of(rotated, head_size) * sin_tab
        gain_sums[which] = gain_sums[which] + jnp.sum(back * unit, axis=0, keepdims=True)
        turned = back * gain_values[which : which + 1]
        mean = jnp.sum(turned * unit, axis=1, keepdims=True) * (1.0 / head_size)
        return ((turned - unit * mean) * factor)[:, :head_size]

    refs = (values, gain_values, cos_tab, sin_tab, meta[0, :, 0:1], seg_col[0])
    for h, parts in enumerate(attention_block(head_size, heads, refs)):
        query_unit, query_factor, key_unit, key_factor, query, key, value, probs = parts
        grad_head = head_of(grad_attended, h, head_size).astype(low)
        grad_probs = dot_t(grad_head, value)
        row_dot = jnp.sum(probs * grad_probs, axis=1, keepdims=True)
        grad_scores = (probs * (grad_probs - row_dot)).astype(low)
        grad_values.append(outer_grad(probs.astype(low), grad_head)[:, :head_size])
        grad_queries.append(
            raw_grad(dot(grad_scores, key) * score_scale, query_unit, query_factor, 0)
        )
        grad_keys.append(
            raw_grad(outer_grad(grad_scores, query) * score_scale, key_unit, key_factor, 1)
        )
    result = jnp.concatenate(grad_queries + grad_keys + grad_values, axis=1).astype(low)
    bias_out[...] += jnp.sum(result.astype(full), axis=0, keepdims=True)
    gains_out[0:1, :] += gain_sums[0]
    gains_out[1:2, :] += gain_sums[1]
    terms_out[0] = dot_t(result, weight[...]).astype(low)
    qkv_total[...] += outer_grad(hidden[0], result)
    proj_total[...] += outer_grad(attended[0], grad)

    @pl.when(pl.program_id(0) == pl.num_programs(0) - 1)
    def _():
        qkv_parts[...] = qkv_total[...].astype(low).reshape(qkv_parts.shape)
        cut_columns(proj_parts, proj_total[...])
        copies.finish()


def ffn_kernel(copies, rest, *refs):
    (own_hidden, hiddens, own_cot, cots, gate, up_mine, up_other) = refs[:7]
    (down_mine, down_other, bias) = refs[7:10]
    ffn_terms, hidden_terms, bias_out, up_parts, down_parts = refs[10:15]
    down, up, up_total, down_total, terms = refs[15:]
    copies.ins = [terms]
    step = pl.program_id(0)

    @pl.when(step == 0)
    def _():
        bias_out[...] = jnp.zeros_like(bias_out)
        up_total[...] = jnp.zeros_like(up_total)
        down_total[...] = jnp.zeros_like(down_total)
        copies.greet()
        fill_rows(down, down_mine, down_other)
        rows = up_mine.shape[1]
        core = lax.axis_index("dp") % 2
        for source, place in ((up_mine, core), (up_other, 1 - core)):
            for p in range(source.shape[0]):
                at = pl.multiple_of((2 * p + place) * rows, 16)
                up[pl.ds(at, rows), :] = source[p]

    count, width = own_hidden.shape
    last = pl.num_programs(0) - 1
    units = down.shape[0]
    hidden = jnp.where(step == last, own_hidden[...], hiddens[0])
    cot = jnp.where(step == last, own_cot[...], cots[0])
    grad_branch = cot.astype(full).reshape(count // SPAN, SPAN, width) * gate[0]
    grad_branch = grad_branch.reshape(count, width).astype(low)
    grad_gated = dot_t(grad_branch, down[...])
    gate_up = dot(hidden, up[...]) + bias[...]
    gate_part, up_part = gate_up[:, :units], gate_up[:, units:]
    sigmoid = jax.nn.sigmoid(gate_part)
    silu = gate_part * sigmoid
    gated = (silu * up_part).astype(low)
    slope = sigmoid * (1.0 + gate_part * (1.0 - sigmoid))
    grad_gate = (grad_gated * up_part * slope).astype(low)
    grad_up = (grad_gated * silu).astype(low)
    grads = jnp.concatenate([grad_gate, grad_up], axis=1)
    bias_out[...] += jnp.sum(grads.astype(full), axis=0, keepdims=True)

    for number in range(PLANE - 1):
        @pl.when(step == number + 1)
        def _(number=number):
            copies.start(number)

    hidden_term = dot_t(grads, up[...]).astype(low)

    @pl.when(step < last)
    def _():
        terms[step] = hidden_term

    @pl.when(step == last)
    def _():
        hidden_terms[...] = hidden_term

    ffn_terms[0] = dot(gated, down[...]).astype(low)
    up_total[...] += outer_grad(hidden, grads)
    down_total[...] += outer_grad(gated, grad_branch)

    @pl.when(step == pl.num_programs(0) - 1)
    def _():
        up_parts[...] = up_total[...].astype(low).reshape(up_parts.shape)
        cut_columns(down_parts, down_total[...])
        copies.finish()


def tail_kernel(*refs):
    (patch, cot, middle, branch, grad_middle, grad_two, one_blocks, one_own) = refs[:8]
    ffn_blocks, ffn_own, spans, bias, patch_grad, block_out, sums = refs[8:]

    def total(own, blocks):
        return own[0].astype(full) + sum(blocks[k].astype(full) for k in range(PLANE - 1))

    def mean(values):
        return jnp.mean(values, axis=1, keepdims=True)

    values, mid, grad_mid = patch[...].astype(full), middle[...], grad_middle[...]
    scale_one = lax.rsqrt(mean(values * values) + epsilon)
    normed_one = values * scale_one
    grad_one = total(one_own, one_blocks)
    scaled = grad_one * (1.0 + spans[0, 1:2])
    backward = scale_one * (scaled - normed_one * mean(scaled * normed_one))
    patch_grad[...] = (grad_mid + backward).astype(low)
    normed_two = mid * lax.rsqrt(mean(mid * mid) + epsilon)
    branch_ffn = total(ffn_own, ffn_blocks) + bias[...]
    block_out[...] = (mid + spans[0, 5:6] * branch_ffn).astype(low)
    grads = [
        grad_one,
        grad_one * normed_one,
        grad_mid * branch[...],
        grad_two[...],
        grad_two[...] * normed_two,
        cot[...].astype(full) * branch_ffn,
    ]
    for k, values in enumerate(grads):
        sums[0, k : k + 1] = jnp.sum(values, axis=0, keepdims=True)


def tail_call(rows, groups, spans, bias):
    count, _, width = spans.shape
    row = pl.BlockSpec((SPAN, width), lambda p: (p, 0))
    group = pl.BlockSpec((PLANE - 1, SPAN, width), lambda p: (0, p, 0))
    own = pl.BlockSpec((1, SPAN, width), lambda p: (PLANE - 1, p, 0))
    span = pl.BlockSpec((1,) + spans.shape[1:], lambda p: (p, 0, 0))
    whole = pl.BlockSpec((1, width), lambda p: (0, 0))
    result = jax.ShapeDtypeStruct(rows[0].shape, low)
    return pl.pallas_call(
        tail_kernel,
        grid=(count,),
        out_shape=[result, result, jax.ShapeDtypeStruct(spans.shape, full)],
        in_specs=[row] * 6 + [group, own, group, own, span, whole],
        out_specs=[row, row, span],
    )(*rows, *groups, spans, bias)


def split_kernel(groups, *refs):
    target, first = refs[-1], 0
    for source in refs[:-1]:
        count, rows, cols = source.shape
        part = cols // groups
        for p in range(count):
            pieces = []
            for t in range(groups):
                block, at = divmod(t * count + p, groups)
                pieces.append(source[block, :, at * part : (at + 1) * part])
            target[p, first : first + rows] = jnp.concatenate(pieces, axis=1)
        first += rows


def merge_kernel(groups, source, target):
    count, _, cols = source.shape
    part = cols // groups
    for z in range(count):
        pieces = []
        for at in range(groups):
            t, p = divmod(z * groups + at, count)
            pieces.append(source[p, :, t * part : (t + 1) * part])
        target[z] = jnp.concatenate(pieces, axis=1)


def whole_call(kernel, *values):
    count, _, cols = values[0].shape
    rows = sum(v.shape[1] for v in values)
    return pl.pallas_call(
        kernel, out_shape=jax.ShapeDtypeStruct((count, rows, cols), values[0].dtype)
    )(*values)


def block_call(
    kernel, inputs, blocked, out_blocks, out_whole, scratch, steps, flops, identity, moved, landed, plan
):
    def block_spec(shape, mark=1):
        tail = (0,) * (len(shape) - 1)
        if mark == 2:
            return pl.BlockSpec((1,) + shape[1:], lambda p: ((p + 2) % 3,) + tail)
        return pl.BlockSpec((1,) + shape[1:], lambda p: (p,) + tail)

    def whole_spec(shape):
        return pl.BlockSpec(shape, lambda p: (0,) * len(shape))

    anywhere = pl.BlockSpec(memory_space=pl.ANY)
    counts = [len(inputs), len(moved), len(out_blocks) + len(out_whole), len(landed)]
    cuts = np.cumsum(counts).tolist()

    def body(*refs):
        ins, sources = refs[: cuts[0]], refs[cuts[0] : cuts[1]]
        outs, targets = refs[cuts[1] : cuts[2]], refs[cuts[2] : cuts[3]]
        rest, send, recv = refs[cuts[3] : -2], refs[-2], refs[-1]
        kernel(Copies(plan, sources, targets, send, recv), rest, *ins, *outs, *rest)

    return pl.pallas_call(
        body,
        grid=(steps,),
        out_shape=[jax.ShapeDtypeStruct(*o) for o in out_blocks + out_whole + landed],
        in_specs=[
            block_spec(v.shape, b) if b else whole_spec(v.shape) for v, b in zip(inputs, blocked)
        ]
        + [anywhere] * len(moved),
        out_specs=[block_spec(o[0]) for o in out_blocks]
        + [whole_spec(o[0]) for o in out_whole]
        + [anywhere] * len(landed),
        scratch_shapes=[pltpu.VMEM(*o) for o in scratch]
        + [pltpu.SemaphoreType.DMA((len(plan),)), pltpu.SemaphoreType.DMA((len(plan),))],
        compiler_params=pltpu.CompilerParams(collective_id=identity, has_side_effects=True),
        cost_estimate=pl.CostEstimate(
            flops=flops,
            bytes_accessed=sum(v.size * v.dtype.itemsize for v in inputs),
            transcendentals=flops // 1024,
        ),
    )(*inputs, *moved)


def make_plane(z_size):
    def per_device(
        patches,
        conditions,
        segment_ids,
        grid_coords,
        mod_weight,
        mod_bias,
        qkv_weight,
        qkv_bias,
        qk_gains,
        proj_weight,
        proj_bias,
        up_weight,
        up_bias,
        down_weight,
        down_bias,
        out_cotangent,
    ):
        row_count, width = patches.shape
        slots = conditions.shape[0]
        spans = row_count // SPAN
        head_size = width // HEADS
        heads = HEADS // PLANE
        part_cols = width // PLANE
        score_scale = head_size ** (-0.5)
        dp_index = lax.axis_index("dp")
        z_index = lax.axis_index("fsdp")
        chip = dp_index >> 1
        core = dp_index & 1
        upper = core == 1
        mod_rows, mod_cols = mod_weight.shape
        rows_all = PLANE * row_count
        shard = qkv_weight.shape[0]

        def halves(values):
            return values.reshape(2, row_count // 2, width)

        def core_order(mine, other):
            return jnp.where(upper, other, mine), jnp.where(upper, mine, other)

        cond_full = conditions.astype(full)
        silu_low = jax.nn.silu(cond_full).astype(low)
        vector = jnp.concatenate(
            [qkv_bias, proj_bias, up_bias, down_bias, qk_gains[0], qk_gains[1]]
        )[None]
        meta = jnp.concatenate([segment_ids[None], grid_coords], axis=0)
        cols_qkv = qkv_weight.shape[1]
        cols_proj = proj_weight.shape[1]
        plan = gather_moves(Z_HOPS + [SELF], 0, 0, lambda me, peer: (me.dp, me.z))
        plan += gather_moves(Z_HOPS + [SELF], 1, 1, by_z)
        plan += gather_moves(Z_HOPS + [SELF], 3, 3, by_z)
        plan += gather_moves(Z_HOPS + [SELF], 4, 4, by_z)
        plan += gather_moves(PLANE_HOPS + [SELF], 5, 5, by_chip)
        plan += [(hop, 0, by_dp, 0, by_dp, (0, 1, 2, 3)) for hop in DP_HOPS if hop != SELF]
        plan += relayed(2, 2, hop_place, len(plan))
        plan += relayed(6, 6, hop_place, len(plan))
        silu_all, qkv_z, patch_blocks, proj_z, vectors, meta_all, cot_blocks = exchange(
            1,
            [
                silu_low,
                qkv_weight,
                halves(patches),
                proj_weight,
                vector,
                meta,
                halves(out_cotangent),
            ],
            [
                ((2 * PLANE, z_size, slots, width), low),
                ((z_size, shard, cols_qkv), low),
                ((PLANE - 1, 2, row_count // 2, width), low),
                ((z_size, shard, cols_proj), low),
                ((z_size,) + vector.shape, low),
                ((PLANE,) + meta.shape, jnp.int32),
                ((PLANE - 1, 2, row_count // 2, width), low),
            ],
            plan,
        )

        up_cut = shard // 48 * 32
        up_cols = up_weight.shape[1]
        up_part = lambda me, peer: (pl.ds(0, up_cut),)
        up_rest = lambda me, peer: (pl.ds(up_cut, shard - up_cut),)

        silu_all = silu_all.reshape(-1, width)
        silu_cols = lax.dynamic_slice_in_dim(silu_all, dp_index * mod_rows, mod_rows, axis=1)
        mod_part = dot(silu_cols, mod_weight).reshape(2 * PLANE, z_size * slots, mod_cols)
        qkv_pieces = whole_call(functools.partial(split_kernel, 3), qkv_z)
        plan = [
            (hop, 0, to_chip, 0, by_dp, None) for hop in PLANE_HOPS
        ]
        plan += [
            (hop, 1, lambda me, peer: (peer.dp,), 1, lambda me, peer: (me.dp,), None)
            for hop in DP_HOPS
        ]
        plan.append((CORE_HOP, 2, None, 2, None, None))
        plan.append((SELF, 0, to_chip, 0, by_dp, None))
        plan += [(hop, 3, up_part, 3, by_z, None) for hop in Z_HOPS + [SELF]]
        for number, (dy, dx, dc, dz) in enumerate(PLANE_HOPS):
            from_hop = lambda me, peer, dy=dy, dx=dx: (me.hop(dy, dx, 0, 0).dp,)
            plan.append((CORE_HOP, 0, from_hop, 0, from_hop, (number,)))
        plan.append((CORE_HOP, 0, by_chip, 0, by_dp, None))
        qkv_slice, mod_parts, proj_other, up_z_part = exchange(
            2,
            [qkv_pieces, mod_part, proj_z, up_weight],
            [
                ((2 * PLANE, shard, 3 * part_cols), low),
                (mod_part.shape, full),
                (proj_z.shape, low),
                ((z_size, up_cut, up_cols), low),
            ],
            plan,
        )
        qkv_slice = qkv_slice.reshape(-1, 3 * part_cols)
        mod_sum = (jnp.sum(mod_parts, axis=0) + mod_bias.astype(full)).reshape(
            z_size, slots, mod_cols
        )
        plan = [
            (hop, 0, to_z, 0, lambda me, peer: (me.chip, me.z), None) for hop in Z_HOPS + [SELF]
        ]
        plan += [(hop, 0, by_chip, 0, by_chip, (0, 1, 2, 3)) for hop in PLANE_HOPS]
        plan += [(hop, 1, up_rest, 1, by_z, None) for hop in Z_HOPS + [SELF]]
        group_mod, up_z_rest = exchange(
            3,
            [mod_sum, up_weight],
            [
                ((PLANE, z_size, slots, mod_cols), full),
                ((z_size, shard - up_cut, up_cols), low),
            ],
            plan,
        )
        group_mod = group_mod.transpose(0, 2, 1, 3).reshape(PLANE, slots, z_size * mod_cols)
        modulation = lax.dynamic_index_in_dim(group_mod, chip, 0, keepdims=False)

        units = up_weight.shape[1] // 2
        up_pieces = whole_call(functools.partial(split_kernel, 2), up_z_part, up_z_rest)
        segments = meta_all[:, 0].reshape(-1)

        def in_steps(values):
            values = xor_order(values, chip, PLANE)
            return jnp.stack([values[k] for k in (3, 1, 2, 0)])

        meta_steps = in_steps(meta_all)
        meta_rows = meta_steps.transpose(0, 2, 1)
        seg_col = meta_steps[:, 0][:, None, :]
        cos_rows, sin_rows = rotary_rows(head_size)

        gain_cols = qk_gains.shape[1]
        sizes = [qkv_bias.shape[0], proj_bias.shape[0], up_bias.shape[0], down_bias.shape[0]]
        vectors = vectors[:, 0].astype(full)
        bounds = [0]
        for size in sizes + [gain_cols, gain_cols]:
            bounds.append(bounds[-1] + size)
        pieces = [vectors[:, bounds[k] : bounds[k + 1]] for k in range(6)]
        qkv_vector, proj_vector, up_vector, down_vector, gain_q, gain_k = [
            p.reshape(-1) for p in pieces
        ]

        def own_columns(flat, groups):
            parts = flat.reshape(groups, PLANE, -1)
            return lax.dynamic_slice_in_dim(parts, chip, 1, axis=1).reshape(-1)

        assert spans == slots
        many = (meta_all[:, 0, row_count - 1] != 0)[:, None, None]
        group_spans = jnp.where(many, group_mod, group_mod[:, :1])
        own_many = segment_ids[row_count - 1] != 0
        own_spans = jnp.where(own_many, modulation, modulation[:1])

        def spread(values):
            count = values.shape[0]
            return jnp.broadcast_to(values[:, None, :], (count, SPAN, width)).reshape(
                count * SPAN, width
            )

        def per_row(k):
            return spread(own_spans[:, k * width : (k + 1) * width])

        def per_row_all(k):
            return spread(
                group_spans[:, :, k * width : (k + 1) * width].reshape(PLANE * spans, width)
            )

        def core_swap(source, out, count):
            return [
                (
                    CORE_HOP,
                    source,
                    lambda me, peer, k=k: (k, peer.core),
                    out,
                    lambda me, peer, k=k: (k,),
                    None,
                )
                for k in range(count)
            ]

        def half_of(parts):
            return ((parts.shape[0],) + parts.shape[2:], low)

        def sum_cores(parts, other):
            mine = lax.dynamic_index_in_dim(parts, core, 1, keepdims=False)
            return (mine.astype(full) + other.astype(full)).astype(low)

        def own_of(values, index):
            return lax.dynamic_index_in_dim(values, index, 0, keepdims=False)

        def z_sum_of(blocks, sent):
            return block_sum(blocks, own_of(sent, z_index))

        def plane_gather(identity, values, *more):
            (out,) = exchange(
                identity,
                [values],
                [((PLANE,) + values.shape, low)],
                gather_moves(PLANE_HOPS, 0, 0, by_chip),
            )
            return put(out, values, chip).reshape(rows_all, width)

        scatter_plan = slotted(PLANE_HOPS, 0, to_chip, 0)
        others = (PLANE - 1, row_count, width)

        def plane_scatter(values):
            return values.astype(low).reshape(PLANE, row_count, width)

        def block_sum(blocks, own):
            return own.astype(full) + jnp.sum(blocks.astype(full), axis=0)

        def plane_sum_of(blocks, sent):
            return block_sum(blocks, lax.dynamic_index_in_dim(sent, chip, 0, keepdims=False))

        def group_span(k):
            return in_steps(group_spans[:, :, None, k * width : (k + 1) * width])

        gain_pad = jnp.zeros((2, LANES), full)
        gains = lax.dynamic_update_slice(gain_pad, jnp.stack([gain_q, gain_k]), (0, 0))
        steps = PLANE_HOPS[2:] + PLANE_HOPS[:2]
        others = (PLANE - 1, row_count, width)

        def in_step(source, out):
            return [
                (hop, source, lambda me, peer, k=k: (k,), out, lambda me, peer, k=k: (k,), None)
                for k, hop in enumerate(steps)
            ]

        plan = [(hop, 0, to_chip, 0, by_chip, None) for hop in PLANE_HOPS + [SELF]]
        plan += gather_moves(Z_HOPS + [SELF], 1, 1, by_z)
        plan += in_step(2, 2)
        (
            hidden_one,
            qkv_rows,
            attended_low,
            attn_terms,
            proj_slice,
            up_same,
            down_z,
            branch_blocks,
        ) = block_call(
            functools.partial(attention_forward_kernel, head_size, heads),
            [
                patches,
                patch_blocks.reshape(others),
                group_span(0),
                group_span(1),
                qkv_slice,
                own_columns(qkv_vector, 3)[None],
                gains,
                cos_rows,
                sin_rows,
                meta_rows,
                seg_col,
                proj_z,
                proj_other,
            ],
            [0, 2, 1, 1, 0, 0, 0, 0, 0, 1, 1, 0, 0],
            [
                ((PLANE, row_count, width), low),
                ((PLANE, row_count, 3 * part_cols), full),
                ((PLANE, row_count, part_cols), low),
            ],
            [((row_count, width), low), ((part_cols, width), low)],
            [(others, low)],
            PLANE,
            rows_all * width * 8 * part_cols,
            11,
            [up_pieces, down_weight],
            [
                (up_pieces.shape, low),
                ((z_size,) + down_weight.shape, low),
                (others, low),
            ],
            plan,
        )
        branch_attn = block_sum(branch_blocks, attn_terms) + proj_vector

        patch_full = patches.astype(full)
        scale_one = rms_scale(patch_full)
        normed_one = patch_full * scale_one
        middle = patch_full + per_row(2) * branch_attn
        scale_two = rms_scale(middle)
        normed_two = middle * scale_two
        hidden_two = (normed_two * (1.0 + per_row(4)) + per_row(3)).astype(low)

        hidden_blocks, down_other, up_other = exchange(
            5,
            [halves(hidden_two), down_z, up_same],
            [((PLANE - 1, 2, row_count // 2, width), low), (down_z.shape, low), (up_same.shape, low)],
            [(CORE_HOP, k, None, k, None, None) for k in (1, 2)] + relayed(0, 0, hop_place, 2),
        )
        gate_spans = in_steps(group_spans[:, :, 5 * width :])
        ffn_terms, own_terms, up_bias_cols, up_parts, down_parts, hidden_two_blocks = block_call(
            ffn_kernel,
            [
                hidden_two,
                hidden_blocks.reshape(others),
                out_cotangent,
                cot_blocks.reshape(others),
                gate_spans[:, :, None],
                up_same,
                up_other,
                down_z,
                down_other,
                own_columns(up_vector, 2)[None],
            ],
            [0, 2, 0, 2, 1, 0, 0, 0, 0, 0],
            [((PLANE, row_count, width), low)],
            [
                ((row_count, width), low),
                ((1, 2 * units), full),
                ((PLANE, 2, shard, 2 * units), low),
                ((z_size, 2) + down_weight.shape, low),
            ],
            [
                ((units, width), low),
                ((width, 2 * units), low),
                ((width, 2 * units), full),
                ((units, width), full),
                (others, low),
            ],
            PLANE,
            rows_all * width * 18 * units,
            6,
            [],
            [(others, low)],
            in_step(0, 0),
        )
        grad_hidden_two = block_sum(hidden_two_blocks, own_terms)

        grad_out = out_cotangent.astype(full)
        own_gbf = (grad_out * per_row(5)).astype(low).astype(full)
        down_bias_grad = jnp.sum(own_gbf, axis=0)
        grad_middle = grad_out + norm_backward(
            grad_hidden_two * (1.0 + per_row(4)), normed_two, scale_two
        )
        grad_branch_attn = (grad_middle * per_row(2)).astype(low)
        proj_bias_grad = jnp.sum(grad_branch_attn.astype(full), axis=0)
        grad_branch_blocks, down_swapped, up_swapped = exchange(
            7,
            [halves(grad_branch_attn), down_parts, up_parts],
            [
                ((PLANE - 1, 2, row_count // 2, width), low),
                half_of(down_parts),
                half_of(up_parts),
            ],
            relayed(0, 0, hop_place, 0)
            + core_swap(1, 1, z_size)
            + core_swap(2, 2, PLANE),
        )
        down_mine = sum_cores(down_parts, down_swapped)
        up_mine = sum_cores(up_parts, up_swapped)
        plan = in_step(0, 0)
        plan += [(hop, 1, to_chip, 1, by_chip, None) for hop in PLANE_HOPS + [SELF]]
        plan += slotted(Z_HOPS, 2, to_z, 2)
        (
            hidden_one_terms,
            qkv_bias_cols,
            gain_grads,
            qkv_parts,
            proj_parts,
            ffn_blocks,
            up_moved,
            down_blocks,
        ) = block_call(
            functools.partial(attention_backward_kernel, head_size, heads),
            [
                grad_branch_attn,
                grad_branch_blocks.reshape(others),
                qkv_rows,
                qkv_slice,
                gains,
                cos_rows,
                sin_rows,
                meta_rows,
                seg_col,
                proj_slice,
                hidden_one,
                attended_low,
            ],
            [0, 2, 1, 0, 0, 0, 0, 1, 1, 0, 1, 1],
            [((PLANE, row_count, width), low)],
            [
                ((1, 3 * part_cols), full),
                ((2, LANES), full),
                ((PLANE, 2, shard, 3 * part_cols), low),
                ((z_size, 2) + proj_weight.shape, low),
            ],
            [((width, 3 * part_cols), full), ((part_cols, width), full)],
            PLANE,
            rows_all * width * 18 * part_cols,
            12,
            [ffn_terms, up_mine, down_mine],
            [
                (others, low),
                (up_mine.shape, low),
                ((z_size - 1,) + down_mine.shape[1:], low),
            ],
            plan,
        )
        gain_q_grad, gain_k_grad = gain_grads[0, :head_size], gain_grads[1, :head_size]
        up_wide = whole_call(functools.partial(merge_kernel, 2), up_moved)
        to_z_part = lambda me, peer: (peer.z, pl.ds(0, up_cut))
        to_z_rest = lambda me, peer: (peer.z, pl.ds(up_cut, shard - up_cut))
        hidden_one_blocks, qkv_other, proj_other, up_blocks = exchange(
            8,
            [hidden_one_terms, qkv_parts, proj_parts, up_wide],
            [
                (others, low),
                half_of(qkv_parts),
                half_of(proj_parts),
                ((z_size - 1, up_cut, up_cols), low),
            ],
            in_step(0, 0)
            + core_swap(1, 1, PLANE)
            + core_swap(2, 2, z_size)
            + slotted(Z_HOPS, 3, to_z_part, 3),
        )
        down_grad = z_sum_of(down_blocks, down_mine)
        qkv_mine = sum_cores(qkv_parts, qkv_other)
        proj_mine = sum_cores(proj_parts, proj_other)
        patch_grad, block_out, grad_spans = tail_call(
            [patches, out_cotangent, middle, branch_attn, grad_middle, grad_hidden_two],
            [hidden_one_blocks, hidden_one_terms, ffn_blocks, ffn_terms],
            own_spans.reshape(spans, -1, width),
            down_vector[None],
        )
        grad_spans = grad_spans.reshape(spans, -1)

        one_image = jnp.concatenate(
            [jnp.sum(grad_spans, axis=0, keepdims=True), jnp.zeros_like(grad_spans[1:])], axis=0
        )
        grad_modulation = jnp.where(own_many, grad_spans, one_image).astype(low)
        grad_mod = grad_modulation.reshape(slots, z_size, mod_cols).transpose(1, 0, 2)

        def place(flat, groups):
            spot = (jnp.arange(PLANE) == chip).astype(full)
            return (flat.reshape(groups, 1, -1) * spot[None, :, None]).reshape(-1)

        rows = [
            place(qkv_bias_cols, 3),
            proj_bias_grad,
            place(up_bias_cols, 2),
            down_bias_grad,
            gain_q_grad,
            gain_k_grad,
        ]
        vector_grad = jnp.concatenate([r.reshape(z_size, 1, -1) for r in rows], axis=2)
        plan = [
            (hop, 1, to_z, 1, lambda me, peer: (me.dp, me.z), None) for hop in Z_HOPS + [SELF]
        ]
        plan += [(hop, 2, to_z, 2, by_z, None) for hop in Z_HOPS + [SELF]]
        plan += [(hop, 0, to_chip, 0, by_chip, None) for hop in PLANE_HOPS + [SELF]]
        plan += [(hop, 1, by_dp, 1, by_dp, (0, 1, 2, 3)) for hop in DP_HOPS if hop != SELF]
        plan += slotted(Z_HOPS, 3, to_z, 3) + slotted(Z_HOPS, 4, to_z_rest, 4)
        qkv_moved, grad_mod, vector_parts, proj_blocks, up_rest_blocks = exchange(
            9,
            [qkv_mine, grad_mod, vector_grad, proj_mine, up_wide],
            [
                (qkv_mine.shape, low),
                ((2 * PLANE, z_size, slots, mod_cols), low),
                (vector_grad.shape, full),
                ((z_size - 1,) + proj_mine.shape[1:], low),
                ((z_size - 1, shard - up_cut, up_cols), low),
            ],
            plan,
        )
        proj_grad = z_sum_of(proj_blocks, proj_mine)
        up_own = own_of(up_wide, z_index)
        up_grad = jnp.concatenate(
            [
                block_sum(up_blocks, up_own[:up_cut]),
                block_sum(up_rest_blocks, up_own[up_cut:]),
            ],
            axis=0,
        )
        qkv_wide = whole_call(functools.partial(merge_kernel, 3), qkv_moved)
        grad_mod = grad_mod.reshape(-1, mod_cols)
        vector_sum = jnp.sum(vector_parts, axis=0)
        cond_part = dot_t(grad_mod, mod_weight).reshape(2 * PLANE, z_size, slots, mod_rows)
        plan = slotted(Z_HOPS, 0, to_z, 0)
        plan += [
            (
                hop,
                1,
                lambda me, peer: (peer.dp, peer.z),
                1,
                lambda me, peer: (me.dp, me.z),
                None,
            )
            for hop in ALL_HOPS
        ]
        plan += gather_moves(DP_HOPS, 2, 2, by_dp)
        qkv_blocks, cond_parts, vector_parts = exchange(
            10,
            [qkv_wide, cond_part, vector_sum],
            [
                ((z_size - 1,) + qkv_wide.shape[1:], low),
                (cond_part.shape, full),
                ((2 * PLANE,) + vector_sum.shape, full),
            ],
            plan,
        )
        qkv_grad = z_sum_of(qkv_blocks, qkv_wide)
        mod_bias_grad = jnp.sum(grad_mod.astype(full), axis=0)
        mod_grad = outer_grad(silu_cols, grad_mod)
        cond_part = jnp.sum(cond_parts, axis=1)
        cond_grad = (
            cond_part.transpose(1, 0, 2).reshape(slots, width) * silu_slope(cond_full)
        ).astype(low)
        vector_grad = jnp.sum(vector_parts, axis=0)[0]
        out = [vector_grad[bounds[k] : bounds[k + 1]] for k in range(6)]
        return (
            block_out,
            patch_grad,
            cond_grad,
            mod_grad,
            mod_bias_grad,
            qkv_grad,
            out[0],
            jnp.stack([out[4], out[5]]),
            proj_grad,
            out[1],
            up_grad,
            out[2],
            down_grad,
            out[3],
        )

    return per_device


def solution(mesh):
    if mesh.shape["dp"] == 2 * PLANE and mesh.shape["fsdp"] == 4:
        body = make_plane(mesh.shape["fsdp"])
    else:
        body = make_plain(mesh.shape["dp"], mesh.shape["fsdp"])
    rows = P(("dp", "fsdp"), None)
    matrix = P("dp", "fsdp")
    vector = P("fsdp")
    gains = P(None, "fsdp")
    return jax.shard_map(
        body,
        mesh=mesh,
        in_specs=(
            rows,
            rows,
            P(("dp", "fsdp")),
            P(None, ("dp", "fsdp")),
            matrix,
            vector,
            matrix,
            vector,
            gains,
            matrix,
            vector,
            matrix,
            vector,
            matrix,
            vector,
            rows,
        ),
        out_specs=(
            rows,
            rows,
            rows,
            matrix,
            vector,
            matrix,
            vector,
            gains,
            matrix,
            vector,
            matrix,
            vector,
            matrix,
            vector,
        ),
        check_vma=False,
    )
```

```python
import functools

import jax
import jax.numpy as jnp
import numpy as np
from jax import lax
from jax.experimental import pallas as pl
from jax.experimental.pallas import tpu as pltpu
from jax.sharding import PartitionSpec as P

HEADS = 16
SPAN = 64
SIDE = 16

epsilon = 1e-06
low = jnp.bfloat16
full = jnp.float32


def rms_scale(values):
    return lax.rsqrt(jnp.mean(values * values, axis=-1, keepdims=True) + epsilon)


def norm_backward(grad_normed, normed, factor):
    return factor * (grad_normed - normed * jnp.mean(grad_normed * normed, axis=-1, keepdims=True))


def rotary_tables(coord_rows, quarter):
    frequencies = 10000.0 ** (-jnp.arange(quarter, dtype=full) / quarter)
    row_angle = coord_rows[0].astype(full)[:, None, None] * frequencies
    col_angle = coord_rows[1].astype(full)[:, None, None] * frequencies
    return (jnp.cos(row_angle), jnp.sin(row_angle), jnp.cos(col_angle), jnp.sin(col_angle))


def rotate(values, tables, direction):
    half_size = values.shape[-1] // 2
    quarter = half_size // 2
    pieces_out = []
    for which_half in range(2):
        cosine = tables[2 * which_half]
        sine_tab = direction * tables[2 * which_half + 1]
        start_col = which_half * half_size
        first_part = values[..., start_col : start_col + quarter]
        second = values[..., start_col + quarter : start_col + half_size]
        pieces_out.append(first_part * cosine - second * sine_tab)
        pieces_out.append(second * cosine + first_part * sine_tab)
    return jnp.concatenate(pieces_out, axis=-1)


def dot(left, right):
    return jnp.dot(left, right, preferred_element_type=full)


def dot_t(left, right):
    return lax.dot_general(left, right, (((1,), (1,)), ((), ())), preferred_element_type=full)


def outer_grad(left, right):
    return lax.dot_general(left, right, (((0,), (0,)), ((), ())), preferred_element_type=full)


def silu_slope(values):
    sigmoid_gate = jax.nn.sigmoid(values)
    return sigmoid_gate * (1.0 + values * (1.0 - sigmoid_gate))


def swap(values, axis, size, bit):
    return lax.ppermute(values, axis, [(k, k ^ bit) for k in range(size)])


def bits_of(size):
    return [1 << b for b in range(size.bit_length() - 1)]


def gather_small(values, axis, size):
    index = lax.axis_index(axis)
    for bit in bits_of(size):
        other = swap(values, axis, size, bit)
        upper = (index & bit) != 0
        values = jnp.concatenate(
            [jnp.where(upper, other, values), jnp.where(upper, values, other)], axis=0
        )
    return values


def scatter_sum_small(values, axis, size):
    index = lax.axis_index(axis)
    for bit in reversed(bits_of(size)):
        half = values.shape[0] // 2
        upper = (index & bit) != 0
        first, second = values[:half], values[half:]
        values = jnp.where(upper, second, first) + swap(
            jnp.where(upper, first, second), axis, size, bit
        )
    return values


def sum_small(values, axis, size):
    for bit in bits_of(size):
        values = values + swap(values, axis, size, bit)
    return values


def xor_order(values, index, size):
    tail = values.shape[1:]
    for bit in bits_of(size):
        paired = values.reshape((size // (2 * bit), 2, bit) + tail)
        values = jnp.where((index & bit) != 0, jnp.flip(paired, axis=1), paired)
        values = values.reshape((size,) + tail)
    return values


def exchange_small(values, axis, size):
    index = lax.axis_index(axis)
    tail = values.shape[1:]
    values = xor_order(values, index, size)
    for bit in bits_of(size):
        paired = values.reshape((size // (2 * bit), 2, bit) + tail)
        moved = swap(paired[:, 1], axis, size, bit)
        values = jnp.stack([paired[:, 0], moved], axis=1).reshape((size,) + tail)
    return xor_order(values, index, size)


def gather_weight(weight, dp_size, fsdp_size):
    rows, cols = weight.shape
    whole = lax.all_gather(weight, ("dp", "fsdp"), axis=0, tiled=False)
    whole = whole.reshape(dp_size, fsdp_size, rows, cols).transpose(1, 0, 2, 3)
    return whole.reshape(fsdp_size, dp_size * rows, cols)


def scatter_grad(blocks, dp_size):
    rows, cols = blocks[0].shape
    parts = jnp.stack([b.reshape(dp_size, rows // dp_size, cols) for b in blocks], axis=1)
    parts = lax.psum_scatter(parts, "dp", scatter_dimension=0, tiled=False)
    return lax.psum_scatter(parts, "fsdp", scatter_dimension=0, tiled=False).astype(full)


def masked_scores(query_low, key_low, same_item, score_scale):
    scores = jnp.einsum("qhd,khd->hqk", query_low, key_low, preferred_element_type=full)
    return jnp.where(same_item, scores * score_scale, -1e30)


def make_plain(dp_size, fsdp_size):
    def per_device(
        patches,
        conditions,
        segment_ids,
        grid_coords,
        mod_weight,
        mod_bias,
        qkv_weight,
        qkv_bias,
        qk_gains,
        proj_weight,
        proj_bias,
        up_weight,
        up_bias,
        down_weight,
        down_bias,
        out_cotangent,
    ):
        row_count, model_width = patches.shape
        slots = conditions.shape[0]
        spans = row_count // SPAN
        head_size = model_width // HEADS
        score_scale = head_size ** (-0.5)
        head_shape = (row_count, HEADS, head_size)
        dp_index = lax.axis_index("dp")
        mod_rows, mod_cols = mod_weight.shape

        qkv_full = gather_weight(qkv_weight, dp_size, fsdp_size)
        proj_full = gather_weight(proj_weight, dp_size, fsdp_size)
        up_full = gather_weight(up_weight, dp_size, fsdp_size)
        down_full = gather_weight(down_weight, dp_size, fsdp_size)

        gain_cols = qk_gains.shape[1]
        sizes = [qkv_bias.shape[0], proj_bias.shape[0], up_bias.shape[0], down_bias.shape[0]]
        vector = jnp.concatenate(
            [qkv_bias, proj_bias, up_bias, down_bias, qk_gains[0], qk_gains[1]]
        )
        vectors = gather_small(vector[None], "fsdp", fsdp_size).astype(full)
        bounds = [0]
        for size in sizes + [gain_cols, gain_cols]:
            bounds.append(bounds[-1] + size)
        pieces = [vectors[:, bounds[k] : bounds[k + 1]] for k in range(6)]
        qkv_vector, proj_vector, up_vector, down_vector, gain_q, gain_k = [
            p.reshape(-1) for p in pieces
        ]

        cond_full = conditions.astype(full)
        silu_low = jax.nn.silu(cond_full).astype(low)
        silu_all = gather_small(
            gather_small(silu_low[None], "fsdp", fsdp_size)[None], "dp", dp_size
        ).reshape(dp_size * fsdp_size * slots, model_width)
        silu_cols = lax.dynamic_slice_in_dim(silu_all, dp_index * mod_rows, mod_rows, axis=1)
        mod_part = dot(silu_cols, mod_weight).reshape(dp_size, fsdp_size, slots, mod_cols)
        mod_sum = scatter_sum_small(mod_part, "dp", dp_size)[0] + mod_bias.astype(full)
        modulation = exchange_small(mod_sum, "fsdp", fsdp_size)
        modulation = modulation.transpose(1, 0, 2).reshape(slots, fsdp_size * mod_cols)
        span_ids = segment_ids.reshape(spans, SPAN)[:, 0]
        span_hot = (span_ids[:, None] == jnp.arange(slots, dtype=jnp.int32)[None, :]).astype(full)
        span_mod = jnp.sum(span_hot[:, :, None] * modulation[None], axis=1)

        def per_row(k):
            part = span_mod[:, k * model_width : (k + 1) * model_width]
            return jnp.broadcast_to(part[:, None, :], (spans, SPAN, model_width)).reshape(
                row_count, model_width
            )

        shift_attn, scale_attn, gate_attn, shift_ffn, scale_ffn, gate_ffn = map(per_row, range(6))

        def cols_of(blocks):
            return jnp.concatenate(blocks, axis=1)

        def forward_dot(rows_low, weight_full):
            return cols_of([dot(rows_low, weight_full[j]) for j in range(fsdp_size)])

        def split(values):
            width = values.shape[1] // fsdp_size
            return [values[:, j * width : (j + 1) * width] for j in range(fsdp_size)]

        def backward_dot(grad_low, weight_full):
            parts = split(grad_low)
            total = dot_t(parts[0], weight_full[0])
            for j in range(1, fsdp_size):
                total = total + dot_t(parts[j], weight_full[j])
            return total

        def weight_grad(rows_low, grad_low):
            return scatter_grad(
                [outer_grad(rows_low, part).astype(low) for part in split(grad_low)], dp_size
            )

        tables = rotary_tables(grid_coords, head_size // 4)
        patch_full = patches.astype(full)
        scale_one = rms_scale(patch_full)
        normed_one = patch_full * scale_one
        hidden_one = (normed_one * (1.0 + scale_attn) + shift_attn).astype(low)
        qkv_rows = forward_dot(hidden_one, qkv_full) + qkv_vector
        query_raw = qkv_rows[:, 0:model_width].reshape(head_shape)
        key_raw = qkv_rows[:, model_width : 2 * model_width].reshape(head_shape)
        value_low = qkv_rows[:, 2 * model_width :].reshape(head_shape).astype(low)
        query_scale = rms_scale(query_raw)
        query_unit = query_raw * query_scale
        key_scale = rms_scale(key_raw)
        key_unit = key_raw * key_scale
        query_low = rotate(query_unit * gain_q, tables, 1.0).astype(low)
        key_low = rotate(key_unit * gain_k, tables, 1.0).astype(low)
        same_item = (segment_ids[:, None] == segment_ids[None, :])[None]
        scores = masked_scores(query_low, key_low, same_item, score_scale)
        exponentials = jnp.exp(scores - jnp.max(scores, axis=-1, keepdims=True))
        probs = exponentials / jnp.sum(exponentials, axis=-1, keepdims=True)
        probs_low = probs.astype(low)
        attended_low = (
            jnp.einsum("hqk,khd->qhd", probs_low, value_low, preferred_element_type=full)
            .reshape(row_count, model_width)
            .astype(low)
        )
        branch_attn = forward_dot(attended_low, proj_full) + proj_vector
        middle = patch_full + gate_attn * branch_attn
        scale_two = rms_scale(middle)
        normed_two = middle * scale_two
        hidden_two = (normed_two * (1.0 + scale_ffn) + shift_ffn).astype(low)
        gate_up = forward_dot(hidden_two, up_full) + up_vector
        hidden_units = gate_up.shape[1] // 2
        gate_part = gate_up[:, :hidden_units]
        up_part = gate_up[:, hidden_units:]
        gated_low = (jax.nn.silu(gate_part) * up_part).astype(low)
        branch_ffn = forward_dot(gated_low, down_full) + down_vector
        block_out = (middle + gate_ffn * branch_ffn).astype(low)

        grad_out = out_cotangent.astype(full)
        grad_gate_ffn = grad_out * branch_ffn
        grad_branch_ffn = (grad_out * gate_ffn).astype(low)
        down_bias_grad = jnp.sum(grad_branch_ffn.astype(full), axis=0)
        grad_gated = backward_dot(grad_branch_ffn, down_full)
        down_grad = weight_grad(gated_low, grad_branch_ffn)
        grad_gate_up = jnp.concatenate(
            [grad_gated * up_part * silu_slope(gate_part), grad_gated * jax.nn.silu(gate_part)],
            axis=1,
        ).astype(low)
        up_bias_grad = jnp.sum(grad_gate_up.astype(full), axis=0)
        grad_hidden_two = backward_dot(grad_gate_up, up_full)
        up_grad = weight_grad(hidden_two, grad_gate_up)
        grad_middle = grad_out + norm_backward(
            grad_hidden_two * (1.0 + scale_ffn), normed_two, scale_two
        )
        grad_gate_attn = grad_middle * branch_attn
        grad_branch_attn = (grad_middle * gate_attn).astype(low)
        proj_bias_grad = jnp.sum(grad_branch_attn.astype(full), axis=0)
        grad_attended = backward_dot(grad_branch_attn, proj_full).astype(low).reshape(head_shape)
        proj_grad = weight_grad(attended_low, grad_branch_attn)
        grad_probs = jnp.einsum(
            "qhd,khd->hqk", grad_attended, value_low, preferred_element_type=full
        )
        row_dot = jnp.sum(probs * grad_probs, axis=-1, keepdims=True)
        grad_scores = (probs * (grad_probs - row_dot)).astype(low)
        grad_values = jnp.einsum(
            "hqk,qhd->khd", probs_low, grad_attended, preferred_element_type=full
        )
        grad_query_rot = score_scale * jnp.einsum(
            "hqk,khd->qhd", grad_scores, key_low, preferred_element_type=full
        )
        grad_key_rot = score_scale * jnp.einsum(
            "hqk,qhd->khd", grad_scores, query_low, preferred_element_type=full
        )
        back_query = rotate(grad_query_rot, tables, -1.0)
        back_key = rotate(grad_key_rot, tables, -1.0)
        gain_q_grad = jnp.sum(back_query * query_unit, axis=(0, 1))
        gain_k_grad = jnp.sum(back_key * key_unit, axis=(0, 1))
        grad_query_raw = norm_backward(back_query * gain_q, query_unit, query_scale)
        grad_key_raw = norm_backward(back_key * gain_k, key_unit, key_scale)
        grad_qkv = jnp.concatenate(
            [
                grad_query_raw.reshape(row_count, model_width),
                grad_key_raw.reshape(row_count, model_width),
                grad_values.reshape(row_count, model_width),
            ],
            axis=1,
        ).astype(low)
        qkv_grad = weight_grad(hidden_one, grad_qkv)
        qkv_bias_grad = jnp.sum(grad_qkv.astype(full), axis=0)
        grad_hidden_one = backward_dot(grad_qkv, qkv_full)
        patch_grad = (
            grad_middle + norm_backward(grad_hidden_one * (1.0 + scale_attn), normed_one, scale_one)
        ).astype(low)

        def span_sum(values):
            return jnp.sum(values.reshape(spans, SPAN, model_width), axis=1)

        grad_spans = jnp.concatenate(
            [
                span_sum(grad_hidden_one),
                span_sum(grad_hidden_one * normed_one),
                span_sum(grad_gate_attn),
                span_sum(grad_hidden_two),
                span_sum(grad_hidden_two * normed_two),
                span_sum(grad_gate_ffn),
            ],
            axis=1,
        )
        grad_modulation = jnp.sum(span_hot[:, :, None] * grad_spans[:, None, :], axis=0).astype(low)
        grad_mod = grad_modulation.reshape(slots, fsdp_size, mod_cols).transpose(1, 0, 2)
        grad_mod = exchange_small(grad_mod, "fsdp", fsdp_size)
        grad_mod = gather_small(grad_mod[None], "dp", dp_size).reshape(-1, mod_cols)
        mod_bias_grad = jnp.sum(grad_mod.astype(full), axis=0)
        mod_grad = outer_grad(silu_cols, grad_mod)
        cond_part = dot_t(grad_mod, mod_weight).reshape(dp_size, fsdp_size, slots, mod_rows)
        cond_part = scatter_sum_small(cond_part.transpose(1, 0, 2, 3), "fsdp", fsdp_size)[0]
        cond_part = exchange_small(cond_part, "dp", dp_size)
        cond_grad = (
            cond_part.transpose(1, 0, 2).reshape(slots, model_width) * silu_slope(cond_full)
        ).astype(low)

        rows = [qkv_bias_grad, proj_bias_grad, up_bias_grad, down_bias_grad, gain_q_grad, gain_k_grad]
        vector_grad = jnp.concatenate([r.reshape(fsdp_size, -1) for r in rows], axis=1)
        vector_grad = scatter_sum_small(vector_grad, "fsdp", fsdp_size)
        vector_grad = sum_small(vector_grad, "dp", dp_size)[0]
        out = [vector_grad[bounds[k] : bounds[k + 1]] for k in range(6)]
        return (
            block_out,
            patch_grad,
            cond_grad,
            mod_grad,
            mod_bias_grad,
            qkv_grad,
            out[0],
            jnp.stack([out[4], out[5]]),
            proj_grad,
            out[1],
            up_grad,
            out[2],
            down_grad,
            out[3],
        )

    return per_device


PLANE = 4


def cross(values, hop):
    return lax.ppermute(values, "dp", [(k, k ^ (2 * hop)) for k in range(2 * PLANE)])


def partner(values):
    return lax.ppermute(values, "dp", [(k, k ^ 1) for k in range(2 * PLANE)])


def along(values, hop, size):
    return lax.ppermute(values, "fsdp", [(k, k ^ hop) for k in range(size)])


def plane_blocks(values):
    return [values] + [cross(values, hop) for hop in range(1, PLANE)]


def plane_sum(blocks):
    total = blocks[0]
    for hop in range(1, PLANE):
        total = total + cross(blocks[hop].astype(low), hop).astype(full)
    return total


def z_blocks(values, index, size):
    blocks = jnp.stack([values] + [along(values, hop, size) for hop in range(1, size)])
    return xor_order(blocks, index, size)


def z_exchange(values, index, size):
    values = xor_order(values, index, size)
    moved = jnp.stack([values[0]] + [along(values[hop], hop, size) for hop in range(1, size)])
    return xor_order(moved, index, size)


def z_sum_own(values, index, size):
    values = xor_order(values, index, size)
    total = values[0].astype(full)
    for hop in range(1, size):
        total = total + along(values[hop], hop, size).astype(full)
    return total


class Place:
    def __init__(self, y, x, core, z):
        self.y, self.x, self.core, self.z = y, x, core, z
        self.chip = 2 * y + x
        self.dp = 2 * self.chip + core

    def hop(self, dy, dx, dc, dz):
        low_z, high_z = self.z % 2, self.z // 2
        low_z = 1 - low_z if dz & 1 else low_z
        high_z = 1 - high_z if dz & 2 else high_z
        return Place(
            1 - self.y if dy else self.y,
            1 - self.x if dx else self.x,
            1 - self.core if dc else self.core,
            2 * high_z + low_z,
        )


SELF = (0, 0, 0, 0)
PLANE_HOPS = [(0, 1, 0, 0), (1, 0, 0, 0), (1, 1, 0, 0)]
Z_HOPS = [(0, 0, 0, 1), (0, 0, 0, 2), (0, 0, 0, 3)]
CORE_HOP = (0, 0, 1, 0)
DP_HOPS = [(dy, dx, dc, 0) for dy in (0, 1) for dx in (0, 1) for dc in (0, 1)]
ALL_HOPS = [(dy, dx, dc, dz) for dz in range(4) for dy, dx, dc, _ in DP_HOPS]
GROUP_HOPS = [(dy, dx, 0, dz) for dz in range(4) for dy in (0, 1) for dx in (0, 1)]


class Copies:
    def __init__(self, plan, ins, outs, send, recv):
        self.plan, self.ins, self.outs, self.send, self.recv = plan, ins, outs, send, recv

    def here(self):
        dp_index = lax.axis_index("dp")
        return Place(dp_index // 4, (dp_index // 2) % 2, dp_index % 2, lax.axis_index("fsdp"))

    def greet(self):
        hops = []
        for move in self.plan:
            if move[0] != SELF and move[0] not in hops:
                hops.append(move[0])
        barrier = pltpu.get_barrier_semaphore()
        for hop in hops:
            peer = self.here().hop(*hop)
            pl.semaphore_signal(
                barrier,
                1,
                device_id={"dp": peer.dp, "fsdp": peer.z},
                device_id_type=pl.DeviceIdType.MESH,
            )
        pl.semaphore_wait(barrier, len(hops))

    def copy(self, number):
        hop, source, source_at, out, out_at, after = self.plan[number]
        me = self.here()
        peer = me.hop(*hop)
        src = (self.ins if after is None else self.outs)[source]
        src = src if source_at is None else src.at[source_at(me, peer)]
        dst = self.outs[out]
        dst = dst if out_at is None else dst.at[out_at(me, peer)]
        if hop == SELF:
            return pltpu.make_async_copy(src, dst, self.send.at[number])
        return pltpu.make_async_remote_copy(
            src_ref=src,
            dst_ref=dst,
            send_sem=self.send.at[number],
            recv_sem=self.recv.at[number],
            device_id={"dp": peer.dp, "fsdp": peer.z},
            device_id_type=pl.DeviceIdType.MESH,
        )

    def start(self, number):
        self.copy(number).start()

    def wait_arrival(self, number):
        if self.plan[number][0] == SELF:
            self.copy(number).wait()
        else:
            self.copy(number).wait_recv()

    def finish(self, arrived=()):
        for number, move in enumerate(self.plan):
            if number not in arrived:
                self.wait_arrival(number)
            if move[0] != SELF:
                self.copy(number).wait_send()


def exchange(identity, inputs, out_shapes, plan, chains=()):
    near, across = (0, 0, 0, 1), (0, 0, 0, 3)
    moves = list(plan)
    for source, out in chains:
        first = len(moves)
        moves += [
            (near, source, None, out, by_z, None),
            (across, source, None, out, by_z, None),
            (across, out, lambda me, peer: (me.hop(*near).z,), out, lambda me, peer: (me.hop(*near).z,), (first,)),
            (near, out, lambda me, peer: (me.hop(*across).z,), out, lambda me, peer: (me.hop(*across).z,), (first + 1,)),
            (near, out, lambda me, peer: (me.hop(0, 0, 0, 2).z,), out, lambda me, peer: (me.hop(0, 0, 0, 2).z,), (first + 2,)),
        ]

    def kernel(*refs):
        ins, outs = refs[: len(inputs)], refs[len(inputs) : len(inputs) + len(out_shapes)]
        copies = Copies(moves, ins, outs, *refs[-2:])
        copies.greet()
        z_index = lax.axis_index("fsdp")
        middle = (z_index + 1) // 2 == 1
        firsts = [len(plan) + 5 * k for k in range(len(chains))]
        for first in firsts:
            copies.start(first)
        if chains:

            @pl.when(middle)
            def _():
                for first in firsts:
                    copies.start(first + 1)

        done = set()

        def follow(wanted):
            for number in wanted:
                for earlier in plan[number][5]:
                    if earlier not in done:
                        copies.wait_arrival(earlier)
                        done.add(earlier)
                copies.start(number)

        later = [number for number, move in enumerate(plan) if move[5] is not None]
        for number, move in enumerate(plan):
            if move[5] is None:
                copies.start(number)
        follow(later[: len(later) // 2])
        if chains:

            @pl.when(middle)
            def _():
                for step in range(3):
                    for first in firsts:
                        copies.wait_arrival(first + step)
                        copies.start(first + step + 2)

        follow(later[len(later) // 2 :])
        for number, move in enumerate(plan):
            if number not in done:
                copies.wait_arrival(number)
            if move[0] != SELF:
                copies.copy(number).wait_send()
        for first in firsts:
            copies.copy(first).wait_send()
        if chains:

            @pl.when(middle)
            def _():
                for first in firsts:
                    for step in range(1, 5):
                        copies.copy(first + step).wait_send()

            @pl.when(jnp.logical_not(middle))
            def _():
                for first in firsts:
                    for step in (0, 3, 4):
                        copies.wait_arrival(first + step)

    anywhere = pl.BlockSpec(memory_space=pl.ANY)
    return pl.pallas_call(
        kernel,
        out_shape=[jax.ShapeDtypeStruct(shape, dtype) for shape, dtype in out_shapes],
        in_specs=[anywhere] * len(inputs),
        out_specs=[anywhere] * len(out_shapes),
        scratch_shapes=[
            pltpu.SemaphoreType.DMA((len(moves),)),
            pltpu.SemaphoreType.DMA((len(moves),)),
        ],
        compiler_params=pltpu.CompilerParams(collective_id=identity, has_side_effects=True),
    )(*inputs)


def gather_moves(hops, source, out, out_at):
    return [(hop, source, None, out, out_at, None) for hop in hops]


def by_chip(me, peer):
    return (me.chip,)


def by_dp(me, peer):
    return (me.dp,)


def by_z(me, peer):
    return (me.z,)


def by_core(me, peer):
    return (me.core,)


def tie(first, second):
    return lax.optimization_barrier((first, second))


def put(values, own, *at):
    start = tuple(at) + (0,) * (values.ndim - len(at))
    return lax.dynamic_update_slice(values, own.reshape((1,) * len(at) + own.shape), start)


HOP_X, HOP_Y = PLANE_HOPS[0], PLANE_HOPS[1]


def relayed(source, out, place, first):
    def at(hop, half):
        return lambda me, peer: (place(me, hop), half)

    def onto(hop, half):
        return lambda me, peer: (place(peer, hop), half)

    def part(half):
        return lambda me, peer: (half,)

    diagonal = PLANE_HOPS[2]
    return [
        (HOP_X, source, part(0), out, onto(HOP_X, 0), None),
        (HOP_Y, source, part(1), out, onto(HOP_Y, 1), None),
        (HOP_X, source, part(1), out, onto(HOP_X, 1), None),
        (HOP_Y, source, part(0), out, onto(HOP_Y, 0), None),
        (HOP_Y, out, at(HOP_X, 0), out, onto(diagonal, 0), (first,)),
        (HOP_X, out, at(HOP_Y, 1), out, onto(diagonal, 1), (first + 1,)),
    ]


def chip_place(me, hop):
    return me.hop(*hop).chip


def hop_place(me, hop):
    return PLANE_HOPS.index(hop)


def slotted(hops, source, source_at, out):
    return [
        (hop, source, source_at, out, lambda me, peer, n=n: (n,), None)
        for n, hop in enumerate(hops)
    ]


def to_chip(me, peer):
    return (peer.chip,)


def to_z(me, peer):
    return (peer.z,)


LANES = 128


def head_of(values, number, head_size):
    part = values[:, number * head_size : (number + 1) * head_size]
    pad = jnp.zeros((values.shape[0], LANES - head_size), values.dtype)
    return jnp.concatenate([part, pad], axis=1)


def pair_of(values, head_size):
    quarter = head_size // 4
    lane = lax.broadcasted_iota(jnp.int32, values.shape, 1)
    second = (lane // quarter) % 2 == 1
    return jnp.where(
        second, pltpu.roll(values, quarter, 1), pltpu.roll(values, LANES - quarter, 1)
    )


def unit_of(raw, head_size):
    factor = lax.rsqrt(jnp.sum(raw * raw, axis=1, keepdims=True) * (1.0 / head_size) + epsilon)
    return raw * factor, factor


def head_probs(query, key, same, score_scale):
    scores = jnp.where(same, dot_t(query, key) * score_scale, -1e30)
    exponentials = jnp.exp(scores - jnp.max(scores, axis=1, keepdims=True))
    return exponentials * (1.0 / jnp.sum(exponentials, axis=1, keepdims=True))


def rotary_rows(head_size):
    quarter = head_size // 4
    frequencies = np.float32(10000.0) ** (-np.arange(quarter, dtype=np.float32) / quarter)
    angles = np.arange(SIDE, dtype=np.float32)[:, None] * frequencies.astype(np.float32)
    cosine = np.zeros((2, SIDE, LANES), np.float32)
    sine = np.zeros((2, SIDE, LANES), np.float32)
    for k in range(2):
        first = 2 * quarter * k
        cosine[k, :, first : first + 2 * quarter] = np.tile(np.cos(angles), (1, 2))
        sine[k, :, first : first + quarter] = -np.sin(angles)
        sine[k, :, first + quarter : first + 2 * quarter] = np.sin(angles)
    return jnp.asarray(cosine.reshape(-1, LANES)), jnp.asarray(sine.reshape(-1, LANES))


def rotary_of(meta, cosine_rows, sine_rows):
    place = lax.broadcasted_iota(jnp.int32, (meta.shape[0], 2 * SIDE), 1)
    hot = (meta[:, 1:2] == place) | (meta[:, 2:3] + SIDE == place)
    hot = hot.astype(full)
    take = functools.partial(jnp.dot, preferred_element_type=full, precision=lax.Precision.HIGHEST)
    return take(hot, cosine_rows), take(hot, sine_rows)


def attention_block(head_size, heads, refs):
    (rows, gains, cosine, sine, seg_row, seg_col) = refs
    same = seg_row == seg_col
    gain_q, gain_k = gains[0:1], gains[1:2]
    for h in range(heads):
        query_unit, query_factor = unit_of(head_of(rows, h, head_size), head_size)
        key_unit, key_factor = unit_of(head_of(rows, heads + h, head_size), head_size)
        query = query_unit * gain_q
        key = key_unit * gain_k
        query = (query * cosine + pair_of(query, head_size) * sine).astype(low)
        key = (key * cosine + pair_of(key, head_size) * sine).astype(low)
        value = head_of(rows, 2 * heads + h, head_size).astype(low)
        probs = head_probs(query, key, same, head_size ** (-0.5))
        yield query_unit, query_factor, key_unit, key_factor, query, key, value, probs


def fill_rows(target, mine, other):
    rows = mine.shape[1]
    core = lax.axis_index("dp") % 2
    for source, place in ((mine, core), (other, 1 - core)):
        target[pl.ds(pl.multiple_of(place * rows, 16), rows), :] = jnp.concatenate(
            [source[j] for j in range(source.shape[0])], axis=1
        )


def attention_forward_kernel(head_size, heads, copies, rest, *refs):
    (own_patch, patches, shift, scale, weight, bias, gains, cos_rows, sin_rows) = refs[:9]
    meta, seg_col, proj_mine, proj_other = refs[9:13]
    hidden_out, rows_out, attended_out, own_terms, proj, terms = refs[13:]
    copies.ins = list(copies.ins) + [terms]
    step, last = pl.program_id(0), pl.num_programs(0) - 1
    first = len(copies.plan) - (PLANE - 1)

    @pl.when(step == 0)
    def _():
        copies.greet()
        for number in range(first):
            copies.start(number)
        fill_rows(proj, proj_mine, proj_other)

    cosine, sine = rotary_of(meta[0], cos_rows[...], sin_rows[...])
    values = jnp.where(step == last, own_patch[...], patches[0]).astype(full)
    count, width = values.shape
    normed = values * lax.rsqrt(jnp.mean(values * values, axis=1, keepdims=True) + epsilon)
    hidden = normed.reshape(count // SPAN, SPAN, width) * (1.0 + scale[0]) + shift[0]
    hidden = hidden.reshape(count, width).astype(low)
    hidden_out[0] = hidden
    rows = dot(hidden, weight[...]) + bias[...]
    rows_out[0] = rows
    pieces = []
    refs = (rows, gains[...], cosine, sine, meta[0, :, 0:1], seg_col[0])
    for *_, value, probs in attention_block(head_size, heads, refs):
        pieces.append(dot(probs.astype(low), value)[:, :head_size])
    attended = jnp.concatenate(pieces, axis=1).astype(low)
    attended_out[0] = attended

    for number in range(PLANE - 1):
        @pl.when(step == number + 1)
        def _(number=number):
            copies.start(first + number)

    term = dot(attended, proj[...]).astype(low)

    @pl.when(step < last)
    def _():
        terms[step] = term

    @pl.when(step == last)
    def _():
        own_terms[...] = term
        copies.finish()


def cut_columns(parts, total):
    cols = parts.shape[3]
    for j in range(parts.shape[0]):
        parts[j] = total[:, j * cols : (j + 1) * cols].astype(low).reshape(parts.shape[1:])


def attention_backward_kernel(head_size, heads, copies, rest, *refs):
    (own_grad, grads, rows, weight, gains, cos_rows, sin_rows, meta, seg_col, proj) = refs[:10]
    hidden, attended = refs[10:12]
    terms_out, bias_out, gains_out, qkv_parts, proj_parts = refs[12:17]
    qkv_total, proj_total = refs[17:]

    @pl.when(pl.program_id(0) == 0)
    def _():
        bias_out[...] = jnp.zeros_like(bias_out)
        gains_out[...] = jnp.zeros_like(gains_out)
        qkv_total[...] = jnp.zeros_like(qkv_total)
        proj_total[...] = jnp.zeros_like(proj_total)
        copies.greet()
        for number in range(len(copies.plan)):
            copies.start(number)

    score_scale = head_size ** (-0.5)
    gain_values = gains[...]
    cos_tab, sin_tab = rotary_of(meta[0], cos_rows[...], sin_rows[...])
    own_step = pl.program_id(0) == pl.num_programs(0) - 1
    grad = jnp.where(own_step, own_grad[...], grads[0])
    grad_attended = dot_t(grad, proj[...])
    values = rows[0]
    grad_queries, grad_keys, grad_values = [], [], []
    gain_sums = [jnp.zeros((1, LANES), full), jnp.zeros((1, LANES), full)]

    def raw_grad(rotated, unit, factor, which):
        back = rotated * cos_tab - pair_of(rotated, head_size) * sin_tab
        gain_sums[which] = gain_sums[which] + jnp.sum(back * unit, axis=0, keepdims=True)
        turned = back * gain_values[which : which + 1]
        mean = jnp.sum(turned * unit, axis=1, keepdims=True) * (1.0 / head_size)
        return ((turned - unit * mean) * factor)[:, :head_size]

    refs = (values, gain_values, cos_tab, sin_tab, meta[0, :, 0:1], seg_col[0])
    for h, parts in enumerate(attention_block(head_size, heads, refs)):
        query_unit, query_factor, key_unit, key_factor, query, key, value, probs = parts
        grad_head = head_of(grad_attended, h, head_size).astype(low)
        grad_probs = dot_t(grad_head, value)
        row_dot = jnp.sum(probs * grad_probs, axis=1, keepdims=True)
        grad_scores = (probs * (grad_probs - row_dot)).astype(low)
        grad_values.append(outer_grad(probs.astype(low), grad_head)[:, :head_size])
        grad_queries.append(
            raw_grad(dot(grad_scores, key) * score_scale, query_unit, query_factor, 0)
        )
        grad_keys.append(
            raw_grad(outer_grad(grad_scores, query) * score_scale, key_unit, key_factor, 1)
        )
    result = jnp.concatenate(grad_queries + grad_keys + grad_values, axis=1).astype(low)
    bias_out[...] += jnp.sum(result.astype(full), axis=0, keepdims=True)
    gains_out[0:1, :] += gain_sums[0]
    gains_out[1:2, :] += gain_sums[1]
    terms_out[0] = dot_t(result, weight[...]).astype(low)
    qkv_total[...] += outer_grad(hidden[0], result)
    proj_total[...] += outer_grad(attended[0], grad)

    @pl.when(pl.program_id(0) == pl.num_programs(0) - 1)
    def _():
        qkv_parts[...] = qkv_total[...].astype(low).reshape(qkv_parts.shape)
        cut_columns(proj_parts, proj_total[...])
        copies.finish()


def ffn_kernel(copies, rest, *refs):
    (own_hidden, hiddens, own_cot, cots, gate, up_mine, up_other) = refs[:7]
    (down_mine, down_other, bias) = refs[7:10]
    hidden_terms, bias_out, ffn_terms, up_parts, down_parts = refs[10:15]
    down, up, terms, all_hidden, all_branch, all_gated, all_grads = refs[15:]
    copies.ins = [terms]
    step = pl.program_id(0)
    count, width = own_hidden.shape
    units = down.shape[0]
    last = PLANE - 1

    @pl.when(step == 0)
    def _():
        copies.greet()
        bias_out[...] = jnp.zeros_like(bias_out)
        fill_rows(down, down_mine, down_other)
        rows = up_mine.shape[1]
        core = lax.axis_index("dp") % 2
        for source, place in ((up_mine, core), (up_other, 1 - core)):
            for p in range(source.shape[0]):
                at = pl.multiple_of((2 * p + place) * rows, 16)
                up[pl.ds(at, rows), :] = source[p]

    @pl.when(step < PLANE)
    def _():
        here = pl.ds(pl.multiple_of(step * count, count), count)
        hidden = jnp.where(step == last, own_hidden[...], hiddens[0])
        cot = jnp.where(step == last, own_cot[...], cots[0])
        grad_branch = cot.astype(full).reshape(count // SPAN, SPAN, width) * gate[0]
        grad_branch = grad_branch.reshape(count, width).astype(low)
        all_hidden[here, :] = hidden
        all_branch[here, :] = grad_branch
        grad_gated = dot_t(grad_branch, down[...])
        gate_up = dot(hidden, up[...]) + bias[...]
        gate_part, up_part = gate_up[:, :units], gate_up[:, units:]
        sigmoid = jax.nn.sigmoid(gate_part)
        silu = gate_part * sigmoid
        all_gated[here, :] = (silu * up_part).astype(low)
        slope = sigmoid * (1.0 + gate_part * (1.0 - sigmoid))
        grad_gate = (grad_gated * up_part * slope).astype(low)
        grad_up = (grad_gated * silu).astype(low)
        grads = jnp.concatenate([grad_gate, grad_up], axis=1)
        all_grads[here, :] = grads
        bias_out[...] += jnp.sum(grads.astype(full), axis=0, keepdims=True)

        for number in range(PLANE - 1):
            @pl.when(step == number + 1)
            def _(number=number):
                copies.start(number)

        hidden_term = dot_t(grads, up[...]).astype(low)

        @pl.when(step < last)
        def _():
            terms[step] = hidden_term

        @pl.when(step == last)
        def _():
            hidden_terms[...] = hidden_term

    @pl.when(step == PLANE)
    def _():
        @pl.loop(0, PLANE)
        def _(k):
            rows = pl.ds(pl.multiple_of(k * count, count), count)
            ffn_terms[k] = dot(all_gated[rows, :], down[...]).astype(low)

        cut = width // 3

        @pl.loop(0, 3)
        def _(k):
            part = pl.ds(pl.multiple_of(k * cut, 128), cut)
            up_parts[part, :] = outer_grad(all_hidden[:, part], all_grads[...]).astype(low)

        cut_columns(down_parts, outer_grad(all_gated[...], all_branch[...]))
        copies.finish()


def tail_kernel(*refs):
    (patch, cot, middle, branch, grad_middle, grad_two, one_blocks, one_own) = refs[:8]
    ffn_blocks, ffn_own, spans, bias, patch_grad, block_out, sums = refs[8:]

    def total(own, blocks):
        return own[0].astype(full) + sum(blocks[k].astype(full) for k in range(PLANE - 1))

    def mean(values):
        return jnp.mean(values, axis=1, keepdims=True)

    values, mid, grad_mid = patch[...].astype(full), middle[...], grad_middle[...]
    scale_one = lax.rsqrt(mean(values * values) + epsilon)
    normed_one = values * scale_one
    grad_one = total(one_own, one_blocks)
    scaled = grad_one * (1.0 + spans[0, 1:2])
    backward = scale_one * (scaled - normed_one * mean(scaled * normed_one))
    patch_grad[...] = (grad_mid + backward).astype(low)
    normed_two = mid * lax.rsqrt(mean(mid * mid) + epsilon)
    branch_ffn = total(ffn_own, ffn_blocks) + bias[...]
    block_out[...] = (mid + spans[0, 5:6] * branch_ffn).astype(low)
    grads = [
        grad_one,
        grad_one * normed_one,
        grad_mid * branch[...],
        grad_two[...],
        grad_two[...] * normed_two,
        cot[...].astype(full) * branch_ffn,
    ]
    for k, values in enumerate(grads):
        sums[0, k : k + 1] = jnp.sum(values, axis=0, keepdims=True)


def tail_call(rows, groups, spans, bias):
    count, _, width = spans.shape
    row = pl.BlockSpec((SPAN, width), lambda p: (p, 0))
    group = pl.BlockSpec((PLANE - 1, SPAN, width), lambda p: (0, p, 0))
    own = pl.BlockSpec((1, SPAN, width), lambda p: (PLANE - 1, p, 0))
    span = pl.BlockSpec((1,) + spans.shape[1:], lambda p: (p, 0, 0))
    whole = pl.BlockSpec((1, width), lambda p: (0, 0))
    result = jax.ShapeDtypeStruct(rows[0].shape, low)
    return pl.pallas_call(
        tail_kernel,
        grid=(count,),
        out_shape=[result, result, jax.ShapeDtypeStruct(spans.shape, full)],
        in_specs=[row] * 6 + [group, own, group, own, span, whole],
        out_specs=[row, row, span],
    )(*rows, *groups, spans, bias)


def split_kernel(groups, *refs):
    target, first = refs[-1], 0
    for source in refs[:-1]:
        count, rows, cols = source.shape
        part = cols // groups
        for p in range(count):
            pieces = []
            for t in range(groups):
                block, at = divmod(t * count + p, groups)
                pieces.append(source[block, :, at * part : (at + 1) * part])
            target[p, first : first + rows] = jnp.concatenate(pieces, axis=1)
        first += rows


def merge_kernel(groups, source, target):
    count, _, cols = source.shape
    part = cols // groups
    for z in range(count):
        pieces = []
        for at in range(groups):
            t, p = divmod(z * groups + at, count)
            pieces.append(source[p, :, t * part : (t + 1) * part])
        target[z] = jnp.concatenate(pieces, axis=1)


def whole_call(kernel, *values):
    count, _, cols = values[0].shape
    rows = sum(v.shape[1] for v in values)
    return pl.pallas_call(
        kernel, out_shape=jax.ShapeDtypeStruct((count, rows, cols), values[0].dtype)
    )(*values)


def block_call(
    kernel, inputs, blocked, out_blocks, out_whole, scratch, steps, flops, identity, moved, landed, plan
):
    def block_spec(shape, mark=1):
        tail = (0,) * (len(shape) - 1)
        if mark == 2:
            return pl.BlockSpec((1,) + shape[1:], lambda p: ((p + 2) % 3,) + tail)
        return pl.BlockSpec((1,) + shape[1:], lambda p: (jnp.minimum(p, shape[0] - 1),) + tail)

    def whole_spec(shape):
        return pl.BlockSpec(shape, lambda p: (0,) * len(shape))

    anywhere = pl.BlockSpec(memory_space=pl.ANY)
    counts = [len(inputs), len(moved), len(out_blocks) + len(out_whole), len(landed)]
    cuts = np.cumsum(counts).tolist()

    def body(*refs):
        ins, sources = refs[: cuts[0]], refs[cuts[0] : cuts[1]]
        outs, targets = refs[cuts[1] : cuts[2]], refs[cuts[2] : cuts[3]]
        rest, send, recv = refs[cuts[3] : -2], refs[-2], refs[-1]
        kernel(Copies(plan, sources, targets, send, recv), rest, *ins, *outs, *rest)

    return pl.pallas_call(
        body,
        grid=(steps,),
        out_shape=[jax.ShapeDtypeStruct(*o) for o in out_blocks + out_whole + landed],
        in_specs=[
            block_spec(v.shape, b) if b else whole_spec(v.shape) for v, b in zip(inputs, blocked)
        ]
        + [anywhere] * len(moved),
        out_specs=[block_spec(o[0]) for o in out_blocks]
        + [whole_spec(o[0]) for o in out_whole]
        + [anywhere] * len(landed),
        scratch_shapes=[pltpu.VMEM(*o) for o in scratch]
        + [pltpu.SemaphoreType.DMA((len(plan),)), pltpu.SemaphoreType.DMA((len(plan),))],
        compiler_params=pltpu.CompilerParams(collective_id=identity, has_side_effects=True),
        cost_estimate=pl.CostEstimate(
            flops=flops,
            bytes_accessed=sum(v.size * v.dtype.itemsize for v in inputs),
            transcendentals=flops // 1024,
        ),
    )(*inputs, *moved)


def make_plane(z_size):
    def per_device(
        patches,
        conditions,
        segment_ids,
        grid_coords,
        mod_weight,
        mod_bias,
        qkv_weight,
        qkv_bias,
        qk_gains,
        proj_weight,
        proj_bias,
        up_weight,
        up_bias,
        down_weight,
        down_bias,
        out_cotangent,
    ):
        row_count, width = patches.shape
        slots = conditions.shape[0]
        spans = row_count // SPAN
        head_size = width // HEADS
        heads = HEADS // PLANE
        part_cols = width // PLANE
        score_scale = head_size ** (-0.5)
        dp_index = lax.axis_index("dp")
        z_index = lax.axis_index("fsdp")
        chip = dp_index >> 1
        core = dp_index & 1
        upper = core == 1
        mod_rows, mod_cols = mod_weight.shape
        rows_all = PLANE * row_count
        shard = qkv_weight.shape[0]

        def halves(values):
            return values.reshape(2, row_count // 2, width)

        def core_order(mine, other):
            return jnp.where(upper, other, mine), jnp.where(upper, mine, other)

        cond_full = conditions.astype(full)
        silu_low = jax.nn.silu(cond_full).astype(low)
        vector = jnp.concatenate(
            [qkv_bias, proj_bias, up_bias, down_bias, qk_gains[0], qk_gains[1]]
        )[None]
        meta = jnp.concatenate([segment_ids[None], grid_coords], axis=0)
        cols_qkv = qkv_weight.shape[1]
        cols_proj = proj_weight.shape[1]
        plan = gather_moves(Z_HOPS + [SELF], 0, 0, lambda me, peer: (me.dp, me.z))
        plan += [(SELF, k, None, k, by_z, None) for k in (1, 3)]
        plan += gather_moves(Z_HOPS + [SELF], 4, 4, by_z)
        plan += gather_moves(PLANE_HOPS + [SELF], 5, 5, by_chip)
        plan += [(hop, 0, by_dp, 0, by_dp, (0, 1, 2, 3)) for hop in DP_HOPS if hop != SELF]
        plan += relayed(2, 2, hop_place, len(plan))
        silu_all, qkv_z, patch_blocks, proj_z, vectors, meta_all = exchange(
            1,
            [
                silu_low,
                qkv_weight,
                halves(patches),
                proj_weight,
                vector,
                meta,
            ],
            [
                ((2 * PLANE, z_size, slots, width), low),
                ((z_size, shard, cols_qkv), low),
                ((PLANE - 1, 2, row_count // 2, width), low),
                ((z_size, shard, cols_proj), low),
                ((z_size,) + vector.shape, low),
                ((PLANE,) + meta.shape, jnp.int32),
            ],
            plan,
            [(1, 1), (3, 3)],
        )

        up_cut = shard // 48 * 32
        up_cols = up_weight.shape[1]
        up_part = lambda me, peer: (pl.ds(0, up_cut),)
        up_rest = lambda me, peer: (pl.ds(up_cut, shard - up_cut),)

        silu_all = silu_all.reshape(-1, width)
        silu_cols = lax.dynamic_slice_in_dim(silu_all, dp_index * mod_rows, mod_rows, axis=1)
        mod_part = dot(silu_cols, mod_weight).reshape(2 * PLANE, z_size * slots, mod_cols)
        qkv_pieces = whole_call(functools.partial(split_kernel, 3), qkv_z)
        plan = [
            (hop, 0, to_chip, 0, by_dp, None) for hop in PLANE_HOPS
        ]
        plan += [
            (hop, 1, lambda me, peer: (peer.dp,), 1, lambda me, peer: (me.dp,), None)
            for hop in DP_HOPS
        ]
        plan.append((CORE_HOP, 2, None, 2, None, None))
        plan.append((SELF, 0, to_chip, 0, by_dp, None))
        plan += [(hop, 3, up_part, 3, by_z, None) for hop in Z_HOPS + [SELF]]
        for number, (dy, dx, dc, dz) in enumerate(PLANE_HOPS):
            from_hop = lambda me, peer, dy=dy, dx=dx: (me.hop(dy, dx, 0, 0).dp,)
            plan.append((CORE_HOP, 0, from_hop, 0, from_hop, (number,)))
        plan.append((CORE_HOP, 0, by_chip, 0, by_dp, None))
        qkv_slice, mod_parts, proj_other, up_z_part = exchange(
            2,
            [qkv_pieces, mod_part, proj_z, up_weight],
            [
                ((2 * PLANE, shard, 3 * part_cols), low),
                (mod_part.shape, full),
                (proj_z.shape, low),
                ((z_size, up_cut, up_cols), low),
            ],
            plan,
        )
        qkv_slice = qkv_slice.reshape(-1, 3 * part_cols)
        mod_sum = (jnp.sum(mod_parts, axis=0) + mod_bias.astype(full)).reshape(
            z_size, slots, mod_cols
        )
        plan = [
            (hop, 0, to_z, 0, lambda me, peer: (me.chip, me.z), None) for hop in Z_HOPS + [SELF]
        ]
        plan += [(hop, 0, by_chip, 0, by_chip, (0, 1, 2, 3)) for hop in PLANE_HOPS]
        plan += [(hop, 1, up_rest, 1, by_z, None) for hop in Z_HOPS + [SELF]]
        plan += relayed(2, 2, hop_place, len(plan))
        group_mod, up_z_rest, cot_blocks = exchange(
            3,
            [mod_sum, up_weight, halves(out_cotangent)],
            [
                ((PLANE, z_size, slots, mod_cols), full),
                ((z_size, shard - up_cut, up_cols), low),
                ((PLANE - 1, 2, row_count // 2, width), low),
            ],
            plan,
        )
        group_mod = group_mod.transpose(0, 2, 1, 3).reshape(PLANE, slots, z_size * mod_cols)
        modulation = lax.dynamic_index_in_dim(group_mod, chip, 0, keepdims=False)

        units = up_weight.shape[1] // 2
        up_pieces = whole_call(functools.partial(split_kernel, 2), up_z_part, up_z_rest)
        segments = meta_all[:, 0].reshape(-1)

        def in_steps(values):
            values = xor_order(values, chip, PLANE)
            return jnp.stack([values[k] for k in (3, 1, 2, 0)])

        meta_steps = in_steps(meta_all)
        meta_rows = meta_steps.transpose(0, 2, 1)
        seg_col = meta_steps[:, 0][:, None, :]
        cos_rows, sin_rows = rotary_rows(head_size)

        gain_cols = qk_gains.shape[1]
        sizes = [qkv_bias.shape[0], proj_bias.shape[0], up_bias.shape[0], down_bias.shape[0]]
        vectors = vectors[:, 0].astype(full)
        bounds = [0]
        for size in sizes + [gain_cols, gain_cols]:
            bounds.append(bounds[-1] + size)
        pieces = [vectors[:, bounds[k] : bounds[k + 1]] for k in range(6)]
        qkv_vector, proj_vector, up_vector, down_vector, gain_q, gain_k = [
            p.reshape(-1) for p in pieces
        ]

        def own_columns(flat, groups):
            parts = flat.reshape(groups, PLANE, -1)
            return lax.dynamic_slice_in_dim(parts, chip, 1, axis=1).reshape(-1)

        assert spans == slots
        many = (meta_all[:, 0, row_count - 1] != 0)[:, None, None]
        group_spans = jnp.where(many, group_mod, group_mod[:, :1])
        own_many = segment_ids[row_count - 1] != 0
        own_spans = jnp.where(own_many, modulation, modulation[:1])

        def spread(values):
            count = values.shape[0]
            return jnp.broadcast_to(values[:, None, :], (count, SPAN, width)).reshape(
                count * SPAN, width
            )

        def per_row(k):
            return spread(own_spans[:, k * width : (k + 1) * width])

        def per_row_all(k):
            return spread(
                group_spans[:, :, k * width : (k + 1) * width].reshape(PLANE * spans, width)
            )

        def core_swap(source, out, count):
            return [
                (
                    CORE_HOP,
                    source,
                    lambda me, peer, k=k: (k, peer.core),
                    out,
                    lambda me, peer, k=k: (k,),
                    None,
                )
                for k in range(count)
            ]

        def half_of(parts):
            return ((parts.shape[0],) + parts.shape[2:], low)

        def sum_cores(parts, other):
            mine = lax.dynamic_index_in_dim(parts, core, 1, keepdims=False)
            return (mine.astype(full) + other.astype(full)).astype(low)

        def own_of(values, index):
            return lax.dynamic_index_in_dim(values, index, 0, keepdims=False)

        def z_sum_of(blocks, sent):
            return block_sum(blocks, own_of(sent, z_index))

        def plane_gather(identity, values, *more):
            (out,) = exchange(
                identity,
                [values],
                [((PLANE,) + values.shape, low)],
                gather_moves(PLANE_HOPS, 0, 0, by_chip),
            )
            return put(out, values, chip).reshape(rows_all, width)

        scatter_plan = slotted(PLANE_HOPS, 0, to_chip, 0)
        others = (PLANE - 1, row_count, width)

        def plane_scatter(values):
            return values.astype(low).reshape(PLANE, row_count, width)

        def block_sum(blocks, own):
            return own.astype(full) + jnp.sum(blocks.astype(full), axis=0)

        def plane_sum_of(blocks, sent):
            return block_sum(blocks, lax.dynamic_index_in_dim(sent, chip, 0, keepdims=False))

        def group_span(k):
            return in_steps(group_spans[:, :, None, k * width : (k + 1) * width])

        gain_pad = jnp.zeros((2, LANES), full)
        gains = lax.dynamic_update_slice(gain_pad, jnp.stack([gain_q, gain_k]), (0, 0))
        steps = PLANE_HOPS[2:] + PLANE_HOPS[:2]
        others = (PLANE - 1, row_count, width)

        def in_step(source, out):
            return [
                (hop, source, lambda me, peer, k=k: (k,), out, lambda me, peer, k=k: (k,), None)
                for k, hop in enumerate(steps)
            ]

        plan = [(hop, 0, to_chip, 0, by_chip, None) for hop in PLANE_HOPS + [SELF]]
        plan += gather_moves(Z_HOPS + [SELF], 1, 1, by_z)
        plan += in_step(2, 2)
        (
            hidden_one,
            qkv_rows,
            attended_low,
            attn_terms,
            proj_slice,
            up_same,
            down_z,
            branch_blocks,
        ) = block_call(
            functools.partial(attention_forward_kernel, head_size, heads),
            [
                patches,
                patch_blocks.reshape(others),
                group_span(0),
                group_span(1),
                qkv_slice,
                own_columns(qkv_vector, 3)[None],
                gains,
                cos_rows,
                sin_rows,
                meta_rows,
                seg_col,
                proj_z,
                proj_other,
            ],
            [0, 2, 1, 1, 0, 0, 0, 0, 0, 1, 1, 0, 0],
            [
                ((PLANE, row_count, width), low),
                ((PLANE, row_count, 3 * part_cols), full),
                ((PLANE, row_count, part_cols), low),
            ],
            [((row_count, width), low), ((part_cols, width), low)],
            [(others, low)],
            PLANE,
            rows_all * width * 8 * part_cols,
            11,
            [up_pieces, down_weight],
            [
                (up_pieces.shape, low),
                ((z_size,) + down_weight.shape, low),
                (others, low),
            ],
            plan,
        )
        branch_attn = block_sum(branch_blocks, attn_terms) + proj_vector

        patch_full = patches.astype(full)
        scale_one = rms_scale(patch_full)
        normed_one = patch_full * scale_one
        middle = patch_full + per_row(2) * branch_attn
        scale_two = rms_scale(middle)
        normed_two = middle * scale_two
        hidden_two = (normed_two * (1.0 + per_row(4)) + per_row(3)).astype(low)

        hidden_blocks, down_other, up_other = exchange(
            5,
            [halves(hidden_two), down_z, up_same],
            [((PLANE - 1, 2, row_count // 2, width), low), (down_z.shape, low), (up_same.shape, low)],
            [(CORE_HOP, k, None, k, None, None) for k in (1, 2)] + relayed(0, 0, hop_place, 2),
        )
        gate_spans = in_steps(group_spans[:, :, 5 * width :])
        own_terms, up_bias_cols, ffn_terms, up_parts, down_parts, hidden_two_blocks = block_call(
            ffn_kernel,
            [
                hidden_two,
                hidden_blocks.reshape(others),
                out_cotangent,
                cot_blocks.reshape(others),
                gate_spans[:, :, None],
                up_same,
                up_other,
                down_z,
                down_other,
                own_columns(up_vector, 2)[None],
            ],
            [0, 2, 0, 2, 1, 0, 0, 0, 0, 0],
            [],
            [
                ((row_count, width), low),
                ((1, 2 * units), full),
                ((PLANE, row_count, width), low),
                ((width, 2 * units), low),
                ((z_size, 2) + down_weight.shape, low),
            ],
            [
                ((units, width), low),
                ((width, 2 * units), low),
                (others, low),
                ((rows_all, width), low),
                ((rows_all, width), low),
                ((rows_all, units), low),
                ((rows_all, 2 * units), low),
            ],
            PLANE + 1,
            rows_all * width * 18 * units,
            6,
            [],
            [(others, low)],
            in_step(0, 0),
        )
        up_parts = up_parts.reshape(PLANE, 2, shard, 2 * units)
        grad_hidden_two = block_sum(hidden_two_blocks, own_terms)

        grad_out = out_cotangent.astype(full)
        own_gbf = (grad_out * per_row(5)).astype(low).astype(full)
        down_bias_grad = jnp.sum(own_gbf, axis=0)
        grad_middle = grad_out + norm_backward(
            grad_hidden_two * (1.0 + per_row(4)), normed_two, scale_two
        )
        grad_branch_attn = (grad_middle * per_row(2)).astype(low)
        proj_bias_grad = jnp.sum(grad_branch_attn.astype(full), axis=0)
        grad_branch_blocks, down_swapped, up_swapped = exchange(
            7,
            [halves(grad_branch_attn), down_parts, up_parts],
            [
                ((PLANE - 1, 2, row_count // 2, width), low),
                half_of(down_parts),
                half_of(up_parts),
            ],
            relayed(0, 0, hop_place, 0)
            + core_swap(1, 1, z_size)
            + core_swap(2, 2, PLANE),
        )
        down_mine = sum_cores(down_parts, down_swapped)
        up_mine = sum_cores(up_parts, up_swapped)
        plan = in_step(0, 0)
        plan += [(hop, 1, to_chip, 1, by_chip, None) for hop in PLANE_HOPS + [SELF]]
        plan += slotted(Z_HOPS, 2, to_z, 2)
        (
            hidden_one_terms,
            qkv_bias_cols,
            gain_grads,
            qkv_parts,
            proj_parts,
            ffn_blocks,
            up_moved,
            down_blocks,
        ) = block_call(
            functools.partial(attention_backward_kernel, head_size, heads),
            [
                grad_branch_attn,
                grad_branch_blocks.reshape(others),
                qkv_rows,
                qkv_slice,
                gains,
                cos_rows,
                sin_rows,
                meta_rows,
                seg_col,
                proj_slice,
                hidden_one,
                attended_low,
            ],
            [0, 2, 1, 0, 0, 0, 0, 1, 1, 0, 1, 1],
            [((PLANE, row_count, width), low)],
            [
                ((1, 3 * part_cols), full),
                ((2, LANES), full),
                ((PLANE, 2, shard, 3 * part_cols), low),
                ((z_size, 2) + proj_weight.shape, low),
            ],
            [((width, 3 * part_cols), full), ((part_cols, width), full)],
            PLANE,
            rows_all * width * 18 * part_cols,
            12,
            [ffn_terms, up_mine, down_mine],
            [
                (others, low),
                (up_mine.shape, low),
                ((z_size - 1,) + down_mine.shape[1:], low),
            ],
            plan,
        )
        gain_q_grad, gain_k_grad = gain_grads[0, :head_size], gain_grads[1, :head_size]
        up_wide = whole_call(functools.partial(merge_kernel, 2), up_moved)
        to_z_part = lambda me, peer: (peer.z, pl.ds(0, up_cut))
        to_z_rest = lambda me, peer: (peer.z, pl.ds(up_cut, shard - up_cut))
        hidden_one_blocks, qkv_other, proj_other, up_blocks = exchange(
            8,
            [hidden_one_terms, qkv_parts, proj_parts, up_wide],
            [
                (others, low),
                half_of(qkv_parts),
                half_of(proj_parts),
                ((z_size - 1, up_cut, up_cols), low),
            ],
            in_step(0, 0)
            + core_swap(1, 1, PLANE)
            + core_swap(2, 2, z_size)
            + slotted(Z_HOPS, 3, to_z_part, 3),
        )
        down_grad = z_sum_of(down_blocks, down_mine)
        qkv_mine = sum_cores(qkv_parts, qkv_other)
        proj_mine = sum_cores(proj_parts, proj_other)
        patch_grad, block_out, grad_spans = tail_call(
            [patches, out_cotangent, middle, branch_attn, grad_middle, grad_hidden_two],
            [hidden_one_blocks, hidden_one_terms, ffn_blocks, ffn_terms],
            own_spans.reshape(spans, -1, width),
            down_vector[None],
        )
        grad_spans = grad_spans.reshape(spans, -1)

        one_image = jnp.concatenate(
            [jnp.sum(grad_spans, axis=0, keepdims=True), jnp.zeros_like(grad_spans[1:])], axis=0
        )
        grad_modulation = jnp.where(own_many, grad_spans, one_image).astype(low)
        grad_mod = grad_modulation.reshape(slots, z_size, mod_cols).transpose(1, 0, 2)

        def place(flat, groups):
            spot = (jnp.arange(PLANE) == chip).astype(full)
            return (flat.reshape(groups, 1, -1) * spot[None, :, None]).reshape(-1)

        rows = [
            place(qkv_bias_cols, 3),
            proj_bias_grad,
            place(up_bias_cols, 2),
            down_bias_grad,
            gain_q_grad,
            gain_k_grad,
        ]
        vector_grad = jnp.concatenate([r.reshape(z_size, 1, -1) for r in rows], axis=2)
        plan = [
            (hop, 1, to_z, 1, lambda me, peer: (me.dp, me.z), None) for hop in Z_HOPS + [SELF]
        ]
        plan += [(hop, 2, to_z, 2, by_z, None) for hop in Z_HOPS + [SELF]]
        plan += [(hop, 0, to_chip, 0, by_chip, None) for hop in PLANE_HOPS + [SELF]]
        plan += [(hop, 1, by_dp, 1, by_dp, (0, 1, 2, 3)) for hop in DP_HOPS if hop != SELF]
        plan += slotted(Z_HOPS, 3, to_z, 3) + slotted(Z_HOPS, 4, to_z_rest, 4)
        qkv_moved, grad_mod, vector_parts, proj_blocks, up_rest_blocks = exchange(
            9,
            [qkv_mine, grad_mod, vector_grad, proj_mine, up_wide],
            [
                (qkv_mine.shape, low),
                ((2 * PLANE, z_size, slots, mod_cols), low),
                (vector_grad.shape, full),
                ((z_size - 1,) + proj_mine.shape[1:], low),
                ((z_size - 1, shard - up_cut, up_cols), low),
            ],
            plan,
        )
        proj_grad = z_sum_of(proj_blocks, proj_mine)
        up_own = own_of(up_wide, z_index)
        up_grad = jnp.concatenate(
            [
                block_sum(up_blocks, up_own[:up_cut]),
                block_sum(up_rest_blocks, up_own[up_cut:]),
            ],
            axis=0,
        )
        qkv_wide = whole_call(functools.partial(merge_kernel, 3), qkv_moved)
        grad_mod = grad_mod.reshape(-1, mod_cols)
        vector_sum = jnp.sum(vector_parts, axis=0)
        cond_part = dot_t(grad_mod, mod_weight).reshape(2 * PLANE, z_size, slots, mod_rows)
        plan = slotted(Z_HOPS, 0, to_z, 0)
        plan += [
            (
                hop,
                1,
                lambda me, peer: (peer.dp, peer.z),
                1,
                lambda me, peer: (me.dp, me.z),
                None,
            )
            for hop in ALL_HOPS
        ]
        plan += gather_moves(DP_HOPS, 2, 2, by_dp)
        qkv_blocks, cond_parts, vector_parts = exchange(
            10,
            [qkv_wide, cond_part, vector_sum],
            [
                ((z_size - 1,) + qkv_wide.shape[1:], low),
                (cond_part.shape, full),
                ((2 * PLANE,) + vector_sum.shape, full),
            ],
            plan,
        )
        qkv_grad = z_sum_of(qkv_blocks, qkv_wide)
        mod_bias_grad = jnp.sum(grad_mod.astype(full), axis=0)
        mod_grad = outer_grad(silu_cols, grad_mod)
        cond_part = jnp.sum(cond_parts, axis=1)
        cond_grad = (
            cond_part.transpose(1, 0, 2).reshape(slots, width) * silu_slope(cond_full)
        ).astype(low)
        vector_grad = jnp.sum(vector_parts, axis=0)[0]
        out = [vector_grad[bounds[k] : bounds[k + 1]] for k in range(6)]
        return (
            block_out,
            patch_grad,
            cond_grad,
            mod_grad,
            mod_bias_grad,
            qkv_grad,
            out[0],
            jnp.stack([out[4], out[5]]),
            proj_grad,
            out[1],
            up_grad,
            out[2],
            down_grad,
            out[3],
        )

    return per_device


def solution(mesh):
    if mesh.shape["dp"] == 2 * PLANE and mesh.shape["fsdp"] == 4:
        body = make_plane(mesh.shape["fsdp"])
    else:
        body = make_plain(mesh.shape["dp"], mesh.shape["fsdp"])
    rows = P(("dp", "fsdp"), None)
    matrix = P("dp", "fsdp")
    vector = P("fsdp")
    gains = P(None, "fsdp")
    return jax.shard_map(
        body,
        mesh=mesh,
        in_specs=(
            rows,
            rows,
            P(("dp", "fsdp")),
            P(None, ("dp", "fsdp")),
            matrix,
            vector,
            matrix,
            vector,
            gains,
            matrix,
            vector,
            matrix,
            vector,
            matrix,
            vector,
            rows,
        ),
        out_specs=(
            rows,
            rows,
            rows,
            matrix,
            vector,
            matrix,
            vector,
            gains,
            matrix,
            vector,
            matrix,
            vector,
            matrix,
            vector,
        ),
        check_vma=False,
    )
```

```python
import functools

import jax
import jax.numpy as jnp
import numpy as np
from jax import lax
from jax.experimental import pallas as pl
from jax.experimental.pallas import tpu as pltpu
from jax.sharding import PartitionSpec as P

HEADS = 16
SPAN = 64
SIDE = 16

epsilon = 1e-06
low = jnp.bfloat16
full = jnp.float32


def rms_scale(values):
    return lax.rsqrt(jnp.mean(values * values, axis=-1, keepdims=True) + epsilon)


def norm_backward(grad_normed, normed, factor):
    return factor * (grad_normed - normed * jnp.mean(grad_normed * normed, axis=-1, keepdims=True))


def rotary_tables(coord_rows, quarter):
    frequencies = 10000.0 ** (-jnp.arange(quarter, dtype=full) / quarter)
    row_angle = coord_rows[0].astype(full)[:, None, None] * frequencies
    col_angle = coord_rows[1].astype(full)[:, None, None] * frequencies
    return (jnp.cos(row_angle), jnp.sin(row_angle), jnp.cos(col_angle), jnp.sin(col_angle))


def rotate(values, tables, direction):
    half_size = values.shape[-1] // 2
    quarter = half_size // 2
    pieces_out = []
    for which_half in range(2):
        cosine = tables[2 * which_half]
        sine_tab = direction * tables[2 * which_half + 1]
        start_col = which_half * half_size
        first_part = values[..., start_col : start_col + quarter]
        second = values[..., start_col + quarter : start_col + half_size]
        pieces_out.append(first_part * cosine - second * sine_tab)
        pieces_out.append(second * cosine + first_part * sine_tab)
    return jnp.concatenate(pieces_out, axis=-1)


def dot(left, right):
    return jnp.dot(left, right, preferred_element_type=full)


def dot_t(left, right):
    return lax.dot_general(left, right, (((1,), (1,)), ((), ())), preferred_element_type=full)


def outer_grad(left, right):
    return lax.dot_general(left, right, (((0,), (0,)), ((), ())), preferred_element_type=full)


def silu_slope(values):
    sigmoid_gate = jax.nn.sigmoid(values)
    return sigmoid_gate * (1.0 + values * (1.0 - sigmoid_gate))


def swap(values, axis, size, bit):
    return lax.ppermute(values, axis, [(k, k ^ bit) for k in range(size)])


def bits_of(size):
    return [1 << b for b in range(size.bit_length() - 1)]


def gather_small(values, axis, size):
    index = lax.axis_index(axis)
    for bit in bits_of(size):
        other = swap(values, axis, size, bit)
        upper = (index & bit) != 0
        values = jnp.concatenate(
            [jnp.where(upper, other, values), jnp.where(upper, values, other)], axis=0
        )
    return values


def scatter_sum_small(values, axis, size):
    index = lax.axis_index(axis)
    for bit in reversed(bits_of(size)):
        half = values.shape[0] // 2
        upper = (index & bit) != 0
        first, second = values[:half], values[half:]
        values = jnp.where(upper, second, first) + swap(
            jnp.where(upper, first, second), axis, size, bit
        )
    return values


def sum_small(values, axis, size):
    for bit in bits_of(size):
        values = values + swap(values, axis, size, bit)
    return values


def xor_order(values, index, size):
    tail = values.shape[1:]
    for bit in bits_of(size):
        paired = values.reshape((size // (2 * bit), 2, bit) + tail)
        values = jnp.where((index & bit) != 0, jnp.flip(paired, axis=1), paired)
        values = values.reshape((size,) + tail)
    return values


def exchange_small(values, axis, size):
    index = lax.axis_index(axis)
    tail = values.shape[1:]
    values = xor_order(values, index, size)
    for bit in bits_of(size):
        paired = values.reshape((size // (2 * bit), 2, bit) + tail)
        moved = swap(paired[:, 1], axis, size, bit)
        values = jnp.stack([paired[:, 0], moved], axis=1).reshape((size,) + tail)
    return xor_order(values, index, size)


def gather_weight(weight, dp_size, fsdp_size):
    rows, cols = weight.shape
    whole = lax.all_gather(weight, ("dp", "fsdp"), axis=0, tiled=False)
    whole = whole.reshape(dp_size, fsdp_size, rows, cols).transpose(1, 0, 2, 3)
    return whole.reshape(fsdp_size, dp_size * rows, cols)


def scatter_grad(blocks, dp_size):
    rows, cols = blocks[0].shape
    parts = jnp.stack([b.reshape(dp_size, rows // dp_size, cols) for b in blocks], axis=1)
    parts = lax.psum_scatter(parts, "dp", scatter_dimension=0, tiled=False)
    return lax.psum_scatter(parts, "fsdp", scatter_dimension=0, tiled=False).astype(full)


def masked_scores(query_low, key_low, same_item, score_scale):
    scores = jnp.einsum("qhd,khd->hqk", query_low, key_low, preferred_element_type=full)
    return jnp.where(same_item, scores * score_scale, -1e30)


def make_plain(dp_size, fsdp_size):
    def per_device(
        patches,
        conditions,
        segment_ids,
        grid_coords,
        mod_weight,
        mod_bias,
        qkv_weight,
        qkv_bias,
        qk_gains,
        proj_weight,
        proj_bias,
        up_weight,
        up_bias,
        down_weight,
        down_bias,
        out_cotangent,
    ):
        row_count, model_width = patches.shape
        slots = conditions.shape[0]
        spans = row_count // SPAN
        head_size = model_width // HEADS
        score_scale = head_size ** (-0.5)
        head_shape = (row_count, HEADS, head_size)
        dp_index = lax.axis_index("dp")
        mod_rows, mod_cols = mod_weight.shape

        qkv_full = gather_weight(qkv_weight, dp_size, fsdp_size)
        proj_full = gather_weight(proj_weight, dp_size, fsdp_size)
        up_full = gather_weight(up_weight, dp_size, fsdp_size)
        down_full = gather_weight(down_weight, dp_size, fsdp_size)

        gain_cols = qk_gains.shape[1]
        sizes = [qkv_bias.shape[0], proj_bias.shape[0], up_bias.shape[0], down_bias.shape[0]]
        vector = jnp.concatenate(
            [qkv_bias, proj_bias, up_bias, down_bias, qk_gains[0], qk_gains[1]]
        )
        vectors = gather_small(vector[None], "fsdp", fsdp_size).astype(full)
        bounds = [0]
        for size in sizes + [gain_cols, gain_cols]:
            bounds.append(bounds[-1] + size)
        pieces = [vectors[:, bounds[k] : bounds[k + 1]] for k in range(6)]
        qkv_vector, proj_vector, up_vector, down_vector, gain_q, gain_k = [
            p.reshape(-1) for p in pieces
        ]

        cond_full = conditions.astype(full)
        silu_low = jax.nn.silu(cond_full).astype(low)
        silu_all = gather_small(
            gather_small(silu_low[None], "fsdp", fsdp_size)[None], "dp", dp_size
        ).reshape(dp_size * fsdp_size * slots, model_width)
        silu_cols = lax.dynamic_slice_in_dim(silu_all, dp_index * mod_rows, mod_rows, axis=1)
        mod_part = dot(silu_cols, mod_weight).reshape(dp_size, fsdp_size, slots, mod_cols)
        mod_sum = scatter_sum_small(mod_part, "dp", dp_size)[0] + mod_bias.astype(full)
        modulation = exchange_small(mod_sum, "fsdp", fsdp_size)
        modulation = modulation.transpose(1, 0, 2).reshape(slots, fsdp_size * mod_cols)
        span_ids = segment_ids.reshape(spans, SPAN)[:, 0]
        span_hot = (span_ids[:, None] == jnp.arange(slots, dtype=jnp.int32)[None, :]).astype(full)
        span_mod = jnp.sum(span_hot[:, :, None] * modulation[None], axis=1)

        def per_row(k):
            part = span_mod[:, k * model_width : (k + 1) * model_width]
            return jnp.broadcast_to(part[:, None, :], (spans, SPAN, model_width)).reshape(
                row_count, model_width
            )

        shift_attn, scale_attn, gate_attn, shift_ffn, scale_ffn, gate_ffn = map(per_row, range(6))

        def cols_of(blocks):
            return jnp.concatenate(blocks, axis=1)

        def forward_dot(rows_low, weight_full):
            return cols_of([dot(rows_low, weight_full[j]) for j in range(fsdp_size)])

        def split(values):
            width = values.shape[1] // fsdp_size
            return [values[:, j * width : (j + 1) * width] for j in range(fsdp_size)]

        def backward_dot(grad_low, weight_full):
            parts = split(grad_low)
            total = dot_t(parts[0], weight_full[0])
            for j in range(1, fsdp_size):
                total = total + dot_t(parts[j], weight_full[j])
            return total

        def weight_grad(rows_low, grad_low):
            return scatter_grad(
                [outer_grad(rows_low, part).astype(low) for part in split(grad_low)], dp_size
            )

        tables = rotary_tables(grid_coords, head_size // 4)
        patch_full = patches.astype(full)
        scale_one = rms_scale(patch_full)
        normed_one = patch_full * scale_one
        hidden_one = (normed_one * (1.0 + scale_attn) + shift_attn).astype(low)
        qkv_rows = forward_dot(hidden_one, qkv_full) + qkv_vector
        query_raw = qkv_rows[:, 0:model_width].reshape(head_shape)
        key_raw = qkv_rows[:, model_width : 2 * model_width].reshape(head_shape)
        value_low = qkv_rows[:, 2 * model_width :].reshape(head_shape).astype(low)
        query_scale = rms_scale(query_raw)
        query_unit = query_raw * query_scale
        key_scale = rms_scale(key_raw)
        key_unit = key_raw * key_scale
        query_low = rotate(query_unit * gain_q, tables, 1.0).astype(low)
        key_low = rotate(key_unit * gain_k, tables, 1.0).astype(low)
        same_item = (segment_ids[:, None] == segment_ids[None, :])[None]
        scores = masked_scores(query_low, key_low, same_item, score_scale)
        exponentials = jnp.exp(scores - jnp.max(scores, axis=-1, keepdims=True))
        probs = exponentials / jnp.sum(exponentials, axis=-1, keepdims=True)
        probs_low = probs.astype(low)
        attended_low = (
            jnp.einsum("hqk,khd->qhd", probs_low, value_low, preferred_element_type=full)
            .reshape(row_count, model_width)
            .astype(low)
        )
        branch_attn = forward_dot(attended_low, proj_full) + proj_vector
        middle = patch_full + gate_attn * branch_attn
        scale_two = rms_scale(middle)
        normed_two = middle * scale_two
        hidden_two = (normed_two * (1.0 + scale_ffn) + shift_ffn).astype(low)
        gate_up = forward_dot(hidden_two, up_full) + up_vector
        hidden_units = gate_up.shape[1] // 2
        gate_part = gate_up[:, :hidden_units]
        up_part = gate_up[:, hidden_units:]
        gated_low = (jax.nn.silu(gate_part) * up_part).astype(low)
        branch_ffn = forward_dot(gated_low, down_full) + down_vector
        block_out = (middle + gate_ffn * branch_ffn).astype(low)

        grad_out = out_cotangent.astype(full)
        grad_gate_ffn = grad_out * branch_ffn
        grad_branch_ffn = (grad_out * gate_ffn).astype(low)
        down_bias_grad = jnp.sum(grad_branch_ffn.astype(full), axis=0)
        grad_gated = backward_dot(grad_branch_ffn, down_full)
        down_grad = weight_grad(gated_low, grad_branch_ffn)
        grad_gate_up = jnp.concatenate(
            [grad_gated * up_part * silu_slope(gate_part), grad_gated * jax.nn.silu(gate_part)],
            axis=1,
        ).astype(low)
        up_bias_grad = jnp.sum(grad_gate_up.astype(full), axis=0)
        grad_hidden_two = backward_dot(grad_gate_up, up_full)
        up_grad = weight_grad(hidden_two, grad_gate_up)
        grad_middle = grad_out + norm_backward(
            grad_hidden_two * (1.0 + scale_ffn), normed_two, scale_two
        )
        grad_gate_attn = grad_middle * branch_attn
        grad_branch_attn = (grad_middle * gate_attn).astype(low)
        proj_bias_grad = jnp.sum(grad_branch_attn.astype(full), axis=0)
        grad_attended = backward_dot(grad_branch_attn, proj_full).astype(low).reshape(head_shape)
        proj_grad = weight_grad(attended_low, grad_branch_attn)
        grad_probs = jnp.einsum(
            "qhd,khd->hqk", grad_attended, value_low, preferred_element_type=full
        )
        row_dot = jnp.sum(probs * grad_probs, axis=-1, keepdims=True)
        grad_scores = (probs * (grad_probs - row_dot)).astype(low)
        grad_values = jnp.einsum(
            "hqk,qhd->khd", probs_low, grad_attended, preferred_element_type=full
        )
        grad_query_rot = score_scale * jnp.einsum(
            "hqk,khd->qhd", grad_scores, key_low, preferred_element_type=full
        )
        grad_key_rot = score_scale * jnp.einsum(
            "hqk,qhd->khd", grad_scores, query_low, preferred_element_type=full
        )
        back_query = rotate(grad_query_rot, tables, -1.0)
        back_key = rotate(grad_key_rot, tables, -1.0)
        gain_q_grad = jnp.sum(back_query * query_unit, axis=(0, 1))
        gain_k_grad = jnp.sum(back_key * key_unit, axis=(0, 1))
        grad_query_raw = norm_backward(back_query * gain_q, query_unit, query_scale)
        grad_key_raw = norm_backward(back_key * gain_k, key_unit, key_scale)
        grad_qkv = jnp.concatenate(
            [
                grad_query_raw.reshape(row_count, model_width),
                grad_key_raw.reshape(row_count, model_width),
                grad_values.reshape(row_count, model_width),
            ],
            axis=1,
        ).astype(low)
        qkv_grad = weight_grad(hidden_one, grad_qkv)
        qkv_bias_grad = jnp.sum(grad_qkv.astype(full), axis=0)
        grad_hidden_one = backward_dot(grad_qkv, qkv_full)
        patch_grad = (
            grad_middle + norm_backward(grad_hidden_one * (1.0 + scale_attn), normed_one, scale_one)
        ).astype(low)

        def span_sum(values):
            return jnp.sum(values.reshape(spans, SPAN, model_width), axis=1)

        grad_spans = jnp.concatenate(
            [
                span_sum(grad_hidden_one),
                span_sum(grad_hidden_one * normed_one),
                span_sum(grad_gate_attn),
                span_sum(grad_hidden_two),
                span_sum(grad_hidden_two * normed_two),
                span_sum(grad_gate_ffn),
            ],
            axis=1,
        )
        grad_modulation = jnp.sum(span_hot[:, :, None] * grad_spans[:, None, :], axis=0).astype(low)
        grad_mod = grad_modulation.reshape(slots, fsdp_size, mod_cols).transpose(1, 0, 2)
        grad_mod = exchange_small(grad_mod, "fsdp", fsdp_size)
        grad_mod = gather_small(grad_mod[None], "dp", dp_size).reshape(-1, mod_cols)
        mod_bias_grad = jnp.sum(grad_mod.astype(full), axis=0)
        mod_grad = outer_grad(silu_cols, grad_mod)
        cond_part = dot_t(grad_mod, mod_weight).reshape(dp_size, fsdp_size, slots, mod_rows)
        cond_part = scatter_sum_small(cond_part.transpose(1, 0, 2, 3), "fsdp", fsdp_size)[0]
        cond_part = exchange_small(cond_part, "dp", dp_size)
        cond_grad = (
            cond_part.transpose(1, 0, 2).reshape(slots, model_width) * silu_slope(cond_full)
        ).astype(low)

        rows = [qkv_bias_grad, proj_bias_grad, up_bias_grad, down_bias_grad, gain_q_grad, gain_k_grad]
        vector_grad = jnp.concatenate([r.reshape(fsdp_size, -1) for r in rows], axis=1)
        vector_grad = scatter_sum_small(vector_grad, "fsdp", fsdp_size)
        vector_grad = sum_small(vector_grad, "dp", dp_size)[0]
        out = [vector_grad[bounds[k] : bounds[k + 1]] for k in range(6)]
        return (
            block_out,
            patch_grad,
            cond_grad,
            mod_grad,
            mod_bias_grad,
            qkv_grad,
            out[0],
            jnp.stack([out[4], out[5]]),
            proj_grad,
            out[1],
            up_grad,
            out[2],
            down_grad,
            out[3],
        )

    return per_device


PLANE = 4


def cross(values, hop):
    return lax.ppermute(values, "dp", [(k, k ^ (2 * hop)) for k in range(2 * PLANE)])


def partner(values):
    return lax.ppermute(values, "dp", [(k, k ^ 1) for k in range(2 * PLANE)])


def along(values, hop, size):
    return lax.ppermute(values, "fsdp", [(k, k ^ hop) for k in range(size)])


def plane_blocks(values):
    return [values] + [cross(values, hop) for hop in range(1, PLANE)]


def plane_sum(blocks):
    total = blocks[0]
    for hop in range(1, PLANE):
        total = total + cross(blocks[hop].astype(low), hop).astype(full)
    return total


def z_blocks(values, index, size):
    blocks = jnp.stack([values] + [along(values, hop, size) for hop in range(1, size)])
    return xor_order(blocks, index, size)


def z_exchange(values, index, size):
    values = xor_order(values, index, size)
    moved = jnp.stack([values[0]] + [along(values[hop], hop, size) for hop in range(1, size)])
    return xor_order(moved, index, size)


def z_sum_own(values, index, size):
    values = xor_order(values, index, size)
    total = values[0].astype(full)
    for hop in range(1, size):
        total = total + along(values[hop], hop, size).astype(full)
    return total


class Place:
    def __init__(self, y, x, core, z):
        self.y, self.x, self.core, self.z = y, x, core, z
        self.chip = 2 * y + x
        self.dp = 2 * self.chip + core

    def hop(self, dy, dx, dc, dz):
        low_z, high_z = self.z % 2, self.z // 2
        low_z = 1 - low_z if dz & 1 else low_z
        high_z = 1 - high_z if dz & 2 else high_z
        return Place(
            1 - self.y if dy else self.y,
            1 - self.x if dx else self.x,
            1 - self.core if dc else self.core,
            2 * high_z + low_z,
        )


SELF = (0, 0, 0, 0)
PLANE_HOPS = [(0, 1, 0, 0), (1, 0, 0, 0), (1, 1, 0, 0)]
Z_HOPS = [(0, 0, 0, 1), (0, 0, 0, 2), (0, 0, 0, 3)]
CORE_HOP = (0, 0, 1, 0)
DP_HOPS = [(dy, dx, dc, 0) for dy in (0, 1) for dx in (0, 1) for dc in (0, 1)]
ALL_HOPS = [(dy, dx, dc, dz) for dz in range(4) for dy, dx, dc, _ in DP_HOPS]
GROUP_HOPS = [(dy, dx, 0, dz) for dz in range(4) for dy in (0, 1) for dx in (0, 1)]


class Copies:
    def __init__(self, plan, ins, outs, send, recv):
        self.plan, self.ins, self.outs, self.send, self.recv = plan, ins, outs, send, recv

    def here(self):
        dp_index = lax.axis_index("dp")
        return Place(dp_index // 4, (dp_index // 2) % 2, dp_index % 2, lax.axis_index("fsdp"))

    def greet(self):
        hops = []
        for move in self.plan:
            if move[0] != SELF and move[0] not in hops:
                hops.append(move[0])
        barrier = pltpu.get_barrier_semaphore()
        for hop in hops:
            peer = self.here().hop(*hop)
            pl.semaphore_signal(
                barrier,
                1,
                device_id={"dp": peer.dp, "fsdp": peer.z},
                device_id_type=pl.DeviceIdType.MESH,
            )
        pl.semaphore_wait(barrier, len(hops))

    def copy(self, number):
        hop, source, source_at, out, out_at, after = self.plan[number]
        me = self.here()
        peer = me.hop(*hop)
        src = (self.ins if after is None else self.outs)[source]
        src = src if source_at is None else src.at[source_at(me, peer)]
        dst = self.outs[out]
        dst = dst if out_at is None else dst.at[out_at(me, peer)]
        if hop == SELF:
            return pltpu.make_async_copy(src, dst, self.send.at[number])
        return pltpu.make_async_remote_copy(
            src_ref=src,
            dst_ref=dst,
            send_sem=self.send.at[number],
            recv_sem=self.recv.at[number],
            device_id={"dp": peer.dp, "fsdp": peer.z},
            device_id_type=pl.DeviceIdType.MESH,
        )

    def start(self, number):
        self.copy(number).start()

    def wait_arrival(self, number):
        if self.plan[number][0] == SELF:
            self.copy(number).wait()
        else:
            self.copy(number).wait_recv()

    def finish(self, arrived=()):
        for number, move in enumerate(self.plan):
            if number not in arrived:
                self.wait_arrival(number)
            if move[0] != SELF:
                self.copy(number).wait_send()


def exchange(identity, inputs, out_shapes, plan, chains=()):
    near, across = (0, 0, 0, 1), (0, 0, 0, 3)
    moves = list(plan)
    for source, out in chains:
        first = len(moves)
        moves += [
            (near, source, None, out, by_z, None),
            (across, source, None, out, by_z, None),
            (across, out, lambda me, peer: (me.hop(*near).z,), out, lambda me, peer: (me.hop(*near).z,), (first,)),
            (near, out, lambda me, peer: (me.hop(*across).z,), out, lambda me, peer: (me.hop(*across).z,), (first + 1,)),
            (near, out, lambda me, peer: (me.hop(0, 0, 0, 2).z,), out, lambda me, peer: (me.hop(0, 0, 0, 2).z,), (first + 2,)),
        ]

    def kernel(*refs):
        ins, outs = refs[: len(inputs)], refs[len(inputs) : len(inputs) + len(out_shapes)]
        copies = Copies(moves, ins, outs, *refs[-2:])
        copies.greet()
        z_index = lax.axis_index("fsdp")
        middle = (z_index + 1) // 2 == 1
        firsts = [len(plan) + 5 * k for k in range(len(chains))]
        for first in firsts:
            copies.start(first)
        if chains:

            @pl.when(middle)
            def _():
                for first in firsts:
                    copies.start(first + 1)

        done = set()

        def follow(wanted):
            for number in wanted:
                for earlier in plan[number][5]:
                    if earlier not in done:
                        copies.wait_arrival(earlier)
                        done.add(earlier)
                copies.start(number)

        later = [number for number, move in enumerate(plan) if move[5] is not None]
        for number, move in enumerate(plan):
            if move[5] is None:
                copies.start(number)
        follow(later[: len(later) // 2])
        if chains:

            @pl.when(middle)
            def _():
                for step in range(3):
                    for first in firsts:
                        copies.wait_arrival(first + step)
                        copies.start(first + step + 2)

        follow(later[len(later) // 2 :])
        for number, move in enumerate(plan):
            if number not in done:
                copies.wait_arrival(number)
            if move[0] != SELF:
                copies.copy(number).wait_send()
        for first in firsts:
            copies.copy(first).wait_send()
        if chains:

            @pl.when(middle)
            def _():
                for first in firsts:
                    for step in range(1, 5):
                        copies.copy(first + step).wait_send()

            @pl.when(jnp.logical_not(middle))
            def _():
                for first in firsts:
                    for step in (0, 3, 4):
                        copies.wait_arrival(first + step)

    anywhere = pl.BlockSpec(memory_space=pl.ANY)
    return pl.pallas_call(
        kernel,
        out_shape=[jax.ShapeDtypeStruct(shape, dtype) for shape, dtype in out_shapes],
        in_specs=[anywhere] * len(inputs),
        out_specs=[anywhere] * len(out_shapes),
        scratch_shapes=[
            pltpu.SemaphoreType.DMA((len(moves),)),
            pltpu.SemaphoreType.DMA((len(moves),)),
        ],
        compiler_params=pltpu.CompilerParams(collective_id=identity, has_side_effects=True),
    )(*inputs)


def gather_moves(hops, source, out, out_at):
    return [(hop, source, None, out, out_at, None) for hop in hops]


def by_chip(me, peer):
    return (me.chip,)


def by_dp(me, peer):
    return (me.dp,)


def by_z(me, peer):
    return (me.z,)


def by_core(me, peer):
    return (me.core,)


def tie(first, second):
    return lax.optimization_barrier((first, second))


def put(values, own, *at):
    start = tuple(at) + (0,) * (values.ndim - len(at))
    return lax.dynamic_update_slice(values, own.reshape((1,) * len(at) + own.shape), start)


HOP_X, HOP_Y = PLANE_HOPS[0], PLANE_HOPS[1]


def relayed(source, out, place, first):
    def at(hop, half):
        return lambda me, peer: (place(me, hop), half)

    def onto(hop, half):
        return lambda me, peer: (place(peer, hop), half)

    def part(half):
        return lambda me, peer: (half,)

    diagonal = PLANE_HOPS[2]
    return [
        (HOP_X, source, part(0), out, onto(HOP_X, 0), None),
        (HOP_Y, source, part(1), out, onto(HOP_Y, 1), None),
        (HOP_X, source, part(1), out, onto(HOP_X, 1), None),
        (HOP_Y, source, part(0), out, onto(HOP_Y, 0), None),
        (HOP_Y, out, at(HOP_X, 0), out, onto(diagonal, 0), (first,)),
        (HOP_X, out, at(HOP_Y, 1), out, onto(diagonal, 1), (first + 1,)),
    ]


def chip_place(me, hop):
    return me.hop(*hop).chip


def hop_place(me, hop):
    return PLANE_HOPS.index(hop)


def slotted(hops, source, source_at, out):
    return [
        (hop, source, source_at, out, lambda me, peer, n=n: (n,), None)
        for n, hop in enumerate(hops)
    ]


def to_chip(me, peer):
    return (peer.chip,)


def to_z(me, peer):
    return (peer.z,)


LANES = 128


def head_of(values, number, head_size):
    part = values[:, number * head_size : (number + 1) * head_size]
    pad = jnp.zeros((values.shape[0], LANES - head_size), values.dtype)
    return jnp.concatenate([part, pad], axis=1)


def pair_of(values, head_size):
    quarter = head_size // 4
    lane = lax.broadcasted_iota(jnp.int32, values.shape, 1)
    second = (lane // quarter) % 2 == 1
    return jnp.where(
        second, pltpu.roll(values, quarter, 1), pltpu.roll(values, LANES - quarter, 1)
    )


def unit_of(raw, head_size):
    factor = lax.rsqrt(jnp.sum(raw * raw, axis=1, keepdims=True) * (1.0 / head_size) + epsilon)
    return raw * factor, factor


def head_probs(query, key, same, score_scale):
    scores = jnp.where(same, dot_t(query, key) * score_scale, -1e30)
    exponentials = jnp.exp(scores - jnp.max(scores, axis=1, keepdims=True))
    return exponentials * (1.0 / jnp.sum(exponentials, axis=1, keepdims=True))


def rotary_rows(head_size):
    quarter = head_size // 4
    frequencies = np.float32(10000.0) ** (-np.arange(quarter, dtype=np.float32) / quarter)
    angles = np.arange(SIDE, dtype=np.float32)[:, None] * frequencies.astype(np.float32)
    cosine = np.zeros((2, SIDE, LANES), np.float32)
    sine = np.zeros((2, SIDE, LANES), np.float32)
    for k in range(2):
        first = 2 * quarter * k
        cosine[k, :, first : first + 2 * quarter] = np.tile(np.cos(angles), (1, 2))
        sine[k, :, first : first + quarter] = -np.sin(angles)
        sine[k, :, first + quarter : first + 2 * quarter] = np.sin(angles)
    return jnp.asarray(cosine.reshape(-1, LANES)), jnp.asarray(sine.reshape(-1, LANES))


def rotary_of(meta, cosine_rows, sine_rows):
    place = lax.broadcasted_iota(jnp.int32, (meta.shape[0], 2 * SIDE), 1)
    hot = (meta[:, 1:2] == place) | (meta[:, 2:3] + SIDE == place)
    hot = hot.astype(full)
    take = functools.partial(jnp.dot, preferred_element_type=full, precision=lax.Precision.HIGHEST)
    return take(hot, cosine_rows), take(hot, sine_rows)


def attention_block(head_size, heads, refs):
    (rows, gains, cosine, sine, seg_row, seg_col) = refs
    same = seg_row == seg_col
    gain_q, gain_k = gains[0:1], gains[1:2]
    for h in range(heads):
        query_unit, query_factor = unit_of(head_of(rows, h, head_size), head_size)
        key_unit, key_factor = unit_of(head_of(rows, heads + h, head_size), head_size)
        query = query_unit * gain_q
        key = key_unit * gain_k
        query = (query * cosine + pair_of(query, head_size) * sine).astype(low)
        key = (key * cosine + pair_of(key, head_size) * sine).astype(low)
        value = head_of(rows, 2 * heads + h, head_size).astype(low)
        probs = head_probs(query, key, same, head_size ** (-0.5))
        yield query_unit, query_factor, key_unit, key_factor, query, key, value, probs


def fill_rows(target, mine, other):
    rows = mine.shape[1]
    core = lax.axis_index("dp") % 2
    for source, place in ((mine, core), (other, 1 - core)):
        target[pl.ds(pl.multiple_of(place * rows, 16), rows), :] = jnp.concatenate(
            [source[j] for j in range(source.shape[0])], axis=1
        )


def attention_forward_kernel(head_size, heads, copies, rest, *refs):
    (own_patch, patches, shift, scale, weight, bias, gains, cos_rows, sin_rows) = refs[:9]
    meta, seg_col, proj_mine, proj_other = refs[9:13]
    hidden_out, rows_out, attended_out, own_terms, proj, terms = refs[13:]
    copies.ins = list(copies.ins) + [terms]
    step, last = pl.program_id(0), pl.num_programs(0) - 1
    first = len(copies.plan) - (PLANE - 1)

    @pl.when(step == 0)
    def _():
        copies.greet()
        for number in range(first):
            copies.start(number)
        fill_rows(proj, proj_mine, proj_other)

    cosine, sine = rotary_of(meta[0], cos_rows[...], sin_rows[...])
    values = jnp.where(step == last, own_patch[...], patches[0]).astype(full)
    count, width = values.shape
    normed = values * lax.rsqrt(jnp.mean(values * values, axis=1, keepdims=True) + epsilon)
    hidden = normed.reshape(count // SPAN, SPAN, width) * (1.0 + scale[0]) + shift[0]
    hidden = hidden.reshape(count, width).astype(low)
    hidden_out[0] = hidden
    rows = dot(hidden, weight[...]) + bias[...]
    rows_out[0] = rows
    pieces = []
    refs = (rows, gains[...], cosine, sine, meta[0, :, 0:1], seg_col[0])
    for *_, value, probs in attention_block(head_size, heads, refs):
        pieces.append(dot(probs.astype(low), value)[:, :head_size])
    attended = jnp.concatenate(pieces, axis=1).astype(low)
    attended_out[0] = attended

    for number in range(PLANE - 1):
        @pl.when(step == number + 1)
        def _(number=number):
            copies.start(first + number)

    term = dot(attended, proj[...]).astype(low)

    @pl.when(step < last)
    def _():
        terms[step] = term

    @pl.when(step == last)
    def _():
        own_terms[...] = term
        copies.finish()


def cut_columns(parts, total):
    cols = parts.shape[3]
    for j in range(parts.shape[0]):
        parts[j] = total[:, j * cols : (j + 1) * cols].astype(low).reshape(parts.shape[1:])


def attention_backward_kernel(head_size, heads, copies, rest, *refs):
    (own_grad, grads, rows, weight, gains, cos_rows, sin_rows, meta, seg_col, proj) = refs[:10]
    hidden, attended = refs[10:12]
    terms_out, bias_out, gains_out, qkv_parts, proj_parts = refs[12:17]
    qkv_total, proj_total = refs[17:]

    @pl.when(pl.program_id(0) == 0)
    def _():
        bias_out[...] = jnp.zeros_like(bias_out)
        gains_out[...] = jnp.zeros_like(gains_out)
        qkv_total[...] = jnp.zeros_like(qkv_total)
        proj_total[...] = jnp.zeros_like(proj_total)
        copies.greet()
        for number in range(len(copies.plan)):
            copies.start(number)

    score_scale = head_size ** (-0.5)
    gain_values = gains[...]
    cos_tab, sin_tab = rotary_of(meta[0], cos_rows[...], sin_rows[...])
    own_step = pl.program_id(0) == pl.num_programs(0) - 1
    grad = jnp.where(own_step, own_grad[...], grads[0])
    grad_attended = dot_t(grad, proj[...])
    values = rows[0]
    grad_queries, grad_keys, grad_values = [], [], []
    gain_sums = [jnp.zeros((1, LANES), full), jnp.zeros((1, LANES), full)]

    def raw_grad(rotated, unit, factor, which):
        back = rotated * cos_tab - pair_of(rotated, head_size) * sin_tab
        gain_sums[which] = gain_sums[which] + jnp.sum(back * unit, axis=0, keepdims=True)
        turned = back * gain_values[which : which + 1]
        mean = jnp.sum(turned * unit, axis=1, keepdims=True) * (1.0 / head_size)
        return ((turned - unit * mean) * factor)[:, :head_size]

    refs = (values, gain_values, cos_tab, sin_tab, meta[0, :, 0:1], seg_col[0])
    for h, parts in enumerate(attention_block(head_size, heads, refs)):
        query_unit, query_factor, key_unit, key_factor, query, key, value, probs = parts
        grad_head = head_of(grad_attended, h, head_size).astype(low)
        grad_probs = dot_t(grad_head, value)
        row_dot = jnp.sum(probs * grad_probs, axis=1, keepdims=True)
        grad_scores = (probs * (grad_probs - row_dot)).astype(low)
        grad_values.append(outer_grad(probs.astype(low), grad_head)[:, :head_size])
        grad_queries.append(
            raw_grad(dot(grad_scores, key) * score_scale, query_unit, query_factor, 0)
        )
        grad_keys.append(
            raw_grad(outer_grad(grad_scores, query) * score_scale, key_unit, key_factor, 1)
        )
    result = jnp.concatenate(grad_queries + grad_keys + grad_values, axis=1).astype(low)
    bias_out[...] += jnp.sum(result.astype(full), axis=0, keepdims=True)
    gains_out[0:1, :] += gain_sums[0]
    gains_out[1:2, :] += gain_sums[1]
    terms_out[0] = dot_t(result, weight[...]).astype(low)
    qkv_total[...] += outer_grad(hidden[0], result)
    proj_total[...] += outer_grad(attended[0], grad)

    @pl.when(pl.program_id(0) == pl.num_programs(0) - 1)
    def _():
        qkv_parts[...] = qkv_total[...].astype(low).reshape(qkv_parts.shape)
        cut_columns(proj_parts, proj_total[...])
        copies.finish()


def ffn_kernel(copies, rest, *refs):
    (own_hidden, hiddens, own_cot, cots, gate, up_mine, up_other) = refs[:7]
    (down_mine, down_other, bias) = refs[7:10]
    hidden_terms, bias_out, ffn_terms, up_parts, down_parts = refs[10:15]
    down, up, terms, all_hidden, all_branch, all_gated, all_grads = refs[15:]
    copies.ins = [terms]
    step = pl.program_id(0)
    count, width = own_hidden.shape
    units = down.shape[0]
    last = PLANE - 1

    @pl.when(step == 0)
    def _():
        copies.greet()
        bias_out[...] = jnp.zeros_like(bias_out)
        fill_rows(down, down_mine, down_other)
        rows = up_mine.shape[1]
        core = lax.axis_index("dp") % 2
        for source, place in ((up_mine, core), (up_other, 1 - core)):
            for p in range(source.shape[0]):
                at = pl.multiple_of((2 * p + place) * rows, 16)
                up[pl.ds(at, rows), :] = source[p]

    @pl.when(step < PLANE)
    def _():
        here = pl.ds(pl.multiple_of(step * count, count), count)
        hidden = jnp.where(step == last, own_hidden[...], hiddens[0])
        cot = jnp.where(step == last, own_cot[...], cots[0])
        grad_branch = cot.astype(full).reshape(count // SPAN, SPAN, width) * gate[0]
        grad_branch = grad_branch.reshape(count, width).astype(low)
        all_hidden[here, :] = hidden
        all_branch[here, :] = grad_branch
        grad_gated = dot_t(grad_branch, down[...])
        gate_up = dot(hidden, up[...]) + bias[...]
        gate_part, up_part = gate_up[:, :units], gate_up[:, units:]
        sigmoid = jax.nn.sigmoid(gate_part)
        silu = gate_part * sigmoid
        all_gated[here, :] = (silu * up_part).astype(low)
        slope = sigmoid * (1.0 + gate_part * (1.0 - sigmoid))
        grad_gate = (grad_gated * up_part * slope).astype(low)
        grad_up = (grad_gated * silu).astype(low)
        grads = jnp.concatenate([grad_gate, grad_up], axis=1)
        all_grads[here, :] = grads
        bias_out[...] += jnp.sum(grads.astype(full), axis=0, keepdims=True)

        for number in range(PLANE - 1):
            @pl.when(step == number + 1)
            def _(number=number):
                copies.start(number)

        hidden_term = dot_t(grads, up[...]).astype(low)

        @pl.when(step < last)
        def _():
            terms[step] = hidden_term

        @pl.when(step == last)
        def _():
            hidden_terms[...] = hidden_term

    @pl.when(step == PLANE)
    def _():
        @pl.loop(0, PLANE)
        def _(k):
            rows = pl.ds(pl.multiple_of(k * count, count), count)
            ffn_terms[k] = dot(all_gated[rows, :], down[...]).astype(low)

        cut = width // 3

        @pl.loop(0, 3)
        def _(k):
            part = pl.ds(pl.multiple_of(k * cut, 128), cut)
            up_parts[part, :] = outer_grad(all_hidden[:, part], all_grads[...]).astype(low)

        cut_columns(down_parts, outer_grad(all_gated[...], all_branch[...]))
        copies.finish()


def tail_kernel(*refs):
    (patch, cot, middle, branch, grad_middle, grad_two, one_blocks, one_own) = refs[:8]
    ffn_blocks, ffn_own, spans, bias, patch_grad, block_out, sums = refs[8:]

    def total(own, blocks):
        return own[0].astype(full) + sum(blocks[k].astype(full) for k in range(PLANE - 1))

    def mean(values):
        return jnp.mean(values, axis=1, keepdims=True)

    values, mid, grad_mid = patch[...].astype(full), middle[...], grad_middle[...]
    scale_one = lax.rsqrt(mean(values * values) + epsilon)
    normed_one = values * scale_one
    grad_one = total(one_own, one_blocks)
    scaled = grad_one * (1.0 + spans[0, 1:2])
    backward = scale_one * (scaled - normed_one * mean(scaled * normed_one))
    patch_grad[...] = (grad_mid + backward).astype(low)
    normed_two = mid * lax.rsqrt(mean(mid * mid) + epsilon)
    branch_ffn = total(ffn_own, ffn_blocks) + bias[...]
    block_out[...] = (mid + spans[0, 5:6] * branch_ffn).astype(low)
    grads = [
        grad_one,
        grad_one * normed_one,
        grad_mid * branch[...],
        grad_two[...],
        grad_two[...] * normed_two,
        cot[...].astype(full) * branch_ffn,
    ]
    for k, values in enumerate(grads):
        sums[0, k : k + 1] = jnp.sum(values, axis=0, keepdims=True)


def tail_call(rows, groups, spans, bias):
    count, _, width = spans.shape
    row = pl.BlockSpec((SPAN, width), lambda p: (p, 0))
    group = pl.BlockSpec((PLANE - 1, SPAN, width), lambda p: (0, p, 0))
    own = pl.BlockSpec((1, SPAN, width), lambda p: (PLANE - 1, p, 0))
    span = pl.BlockSpec((1,) + spans.shape[1:], lambda p: (p, 0, 0))
    whole = pl.BlockSpec((1, width), lambda p: (0, 0))
    result = jax.ShapeDtypeStruct(rows[0].shape, low)
    return pl.pallas_call(
        tail_kernel,
        grid=(count,),
        out_shape=[result, result, jax.ShapeDtypeStruct(spans.shape, full)],
        in_specs=[row] * 6 + [group, own, group, own, span, whole],
        out_specs=[row, row, span],
    )(*rows, *groups, spans, bias)


def split_kernel(groups, *refs):
    target, first = refs[-1], 0
    for source in refs[:-1]:
        count, rows, cols = source.shape
        part = cols // groups
        for p in range(count):
            pieces = []
            for t in range(groups):
                block, at = divmod(t * count + p, groups)
                pieces.append(source[block, :, at * part : (at + 1) * part])
            target[p, first : first + rows] = jnp.concatenate(pieces, axis=1)
        first += rows


def merge_kernel(groups, source, target):
    count, _, cols = source.shape
    part = cols // groups
    for z in range(count):
        pieces = []
        for at in range(groups):
            t, p = divmod(z * groups + at, count)
            pieces.append(source[p, :, t * part : (t + 1) * part])
        target[z] = jnp.concatenate(pieces, axis=1)


def whole_call(kernel, *values):
    count, _, cols = values[0].shape
    rows = sum(v.shape[1] for v in values)
    return pl.pallas_call(
        kernel, out_shape=jax.ShapeDtypeStruct((count, rows, cols), values[0].dtype)
    )(*values)


def block_call(
    kernel, inputs, blocked, out_blocks, out_whole, scratch, steps, flops, identity, moved, landed, plan
):
    def block_spec(shape, mark=1):
        tail = (0,) * (len(shape) - 1)
        if mark == 2:
            return pl.BlockSpec((1,) + shape[1:], lambda p: ((p + 2) % 3,) + tail)
        return pl.BlockSpec((1,) + shape[1:], lambda p: (jnp.minimum(p, shape[0] - 1),) + tail)

    def whole_spec(shape):
        return pl.BlockSpec(shape, lambda p: (0,) * len(shape))

    anywhere = pl.BlockSpec(memory_space=pl.ANY)
    counts = [len(inputs), len(moved), len(out_blocks) + len(out_whole), len(landed)]
    cuts = np.cumsum(counts).tolist()

    def body(*refs):
        ins, sources = refs[: cuts[0]], refs[cuts[0] : cuts[1]]
        outs, targets = refs[cuts[1] : cuts[2]], refs[cuts[2] : cuts[3]]
        rest, send, recv = refs[cuts[3] : -2], refs[-2], refs[-1]
        kernel(Copies(plan, sources, targets, send, recv), rest, *ins, *outs, *rest)

    return pl.pallas_call(
        body,
        grid=(steps,),
        out_shape=[jax.ShapeDtypeStruct(*o) for o in out_blocks + out_whole + landed],
        in_specs=[
            block_spec(v.shape, b) if b else whole_spec(v.shape) for v, b in zip(inputs, blocked)
        ]
        + [anywhere] * len(moved),
        out_specs=[block_spec(o[0]) for o in out_blocks]
        + [whole_spec(o[0]) for o in out_whole]
        + [anywhere] * len(landed),
        scratch_shapes=[pltpu.VMEM(*o) for o in scratch]
        + [pltpu.SemaphoreType.DMA((len(plan),)), pltpu.SemaphoreType.DMA((len(plan),))],
        compiler_params=pltpu.CompilerParams(collective_id=identity, has_side_effects=True),
        cost_estimate=pl.CostEstimate(
            flops=flops,
            bytes_accessed=sum(v.size * v.dtype.itemsize for v in inputs),
            transcendentals=flops // 1024,
        ),
    )(*inputs, *moved)


def make_plane(z_size):
    def per_device(
        patches,
        conditions,
        segment_ids,
        grid_coords,
        mod_weight,
        mod_bias,
        qkv_weight,
        qkv_bias,
        qk_gains,
        proj_weight,
        proj_bias,
        up_weight,
        up_bias,
        down_weight,
        down_bias,
        out_cotangent,
    ):
        row_count, width = patches.shape
        slots = conditions.shape[0]
        spans = row_count // SPAN
        head_size = width // HEADS
        heads = HEADS // PLANE
        part_cols = width // PLANE
        score_scale = head_size ** (-0.5)
        dp_index = lax.axis_index("dp")
        z_index = lax.axis_index("fsdp")
        chip = dp_index >> 1
        core = dp_index & 1
        upper = core == 1
        mod_rows, mod_cols = mod_weight.shape
        rows_all = PLANE * row_count
        shard = qkv_weight.shape[0]

        def halves(values):
            return values.reshape(2, row_count // 2, width)

        def core_order(mine, other):
            return jnp.where(upper, other, mine), jnp.where(upper, mine, other)

        cond_full = conditions.astype(full)
        silu_low = jax.nn.silu(cond_full).astype(low)
        vector = jnp.concatenate(
            [qkv_bias, proj_bias, up_bias, down_bias, qk_gains[0], qk_gains[1]]
        )[None]
        meta = jnp.concatenate([segment_ids[None], grid_coords], axis=0)
        cols_qkv = qkv_weight.shape[1]
        cols_proj = proj_weight.shape[1]
        plan = gather_moves(Z_HOPS + [SELF], 0, 0, lambda me, peer: (me.dp, me.z))
        plan += [(SELF, k, None, k, by_z, None) for k in (1, 3)]
        plan += gather_moves(Z_HOPS + [SELF], 4, 4, by_z)
        plan += gather_moves(PLANE_HOPS + [SELF], 5, 5, by_chip)
        plan += [(hop, 0, by_dp, 0, by_dp, (0, 1, 2, 3)) for hop in DP_HOPS if hop != SELF]
        plan += relayed(2, 2, hop_place, len(plan))
        silu_all, qkv_z, patch_blocks, proj_z, vectors, meta_all = exchange(
            1,
            [
                silu_low,
                qkv_weight,
                halves(patches),
                proj_weight,
                vector,
                meta,
            ],
            [
                ((2 * PLANE, z_size, slots, width), low),
                ((z_size, shard, cols_qkv), low),
                ((PLANE - 1, 2, row_count // 2, width), low),
                ((z_size, shard, cols_proj), low),
                ((z_size,) + vector.shape, low),
                ((PLANE,) + meta.shape, jnp.int32),
            ],
            plan,
            [(1, 1), (3, 3)],
        )

        up_cut = shard // 48 * 32
        up_cols = up_weight.shape[1]
        up_part = lambda me, peer: (pl.ds(0, up_cut),)
        up_rest = lambda me, peer: (pl.ds(up_cut, shard - up_cut),)

        silu_all = silu_all.reshape(-1, width)
        silu_cols = lax.dynamic_slice_in_dim(silu_all, dp_index * mod_rows, mod_rows, axis=1)
        mod_part = dot(silu_cols, mod_weight).astype(low)
        mod_part = mod_part.reshape(2 * PLANE, z_size * slots, mod_cols)
        qkv_pieces = whole_call(functools.partial(split_kernel, 3), qkv_z)
        plan = [
            (hop, 0, to_chip, 0, by_dp, None) for hop in PLANE_HOPS
        ]
        plan += [
            (hop, 1, lambda me, peer: (peer.dp,), 1, lambda me, peer: (me.dp,), None)
            for hop in DP_HOPS
        ]
        plan.append((CORE_HOP, 2, None, 2, None, None))
        plan.append((SELF, 0, to_chip, 0, by_dp, None))
        plan += [(hop, 3, up_part, 3, by_z, None) for hop in Z_HOPS + [SELF]]
        for number, (dy, dx, dc, dz) in enumerate(PLANE_HOPS):
            from_hop = lambda me, peer, dy=dy, dx=dx: (me.hop(dy, dx, 0, 0).dp,)
            plan.append((CORE_HOP, 0, from_hop, 0, from_hop, (number,)))
        plan.append((CORE_HOP, 0, by_chip, 0, by_dp, None))
        qkv_slice, mod_parts, proj_other, up_z_part = exchange(
            2,
            [qkv_pieces, mod_part, proj_z, up_weight],
            [
                ((2 * PLANE, shard, 3 * part_cols), low),
                (mod_part.shape, low),
                (proj_z.shape, low),
                ((z_size, up_cut, up_cols), low),
            ],
            plan,
        )
        qkv_slice = qkv_slice.reshape(-1, 3 * part_cols)
        mod_sum = (jnp.sum(mod_parts.astype(full), axis=0) + mod_bias.astype(full)).reshape(
            z_size, slots, mod_cols
        )
        plan = [
            (hop, 0, to_z, 0, lambda me, peer: (me.chip, me.z), None) for hop in Z_HOPS + [SELF]
        ]
        plan += [(hop, 0, by_chip, 0, by_chip, (0, 1, 2, 3)) for hop in PLANE_HOPS]
        plan += [(hop, 1, up_rest, 1, by_z, None) for hop in Z_HOPS + [SELF]]
        plan += relayed(2, 2, hop_place, len(plan))
        group_mod, up_z_rest, cot_blocks = exchange(
            3,
            [mod_sum, up_weight, halves(out_cotangent)],
            [
                ((PLANE, z_size, slots, mod_cols), full),
                ((z_size, shard - up_cut, up_cols), low),
                ((PLANE - 1, 2, row_count // 2, width), low),
            ],
            plan,
        )
        group_mod = group_mod.transpose(0, 2, 1, 3).reshape(PLANE, slots, z_size * mod_cols)
        modulation = lax.dynamic_index_in_dim(group_mod, chip, 0, keepdims=False)

        units = up_weight.shape[1] // 2
        up_pieces = whole_call(functools.partial(split_kernel, 2), up_z_part, up_z_rest)
        segments = meta_all[:, 0].reshape(-1)

        def in_steps(values):
            values = xor_order(values, chip, PLANE)
            return jnp.stack([values[k] for k in (3, 1, 2, 0)])

        meta_steps = in_steps(meta_all)
        meta_rows = meta_steps.transpose(0, 2, 1)
        seg_col = meta_steps[:, 0][:, None, :]
        cos_rows, sin_rows = rotary_rows(head_size)

        gain_cols = qk_gains.shape[1]
        sizes = [qkv_bias.shape[0], proj_bias.shape[0], up_bias.shape[0], down_bias.shape[0]]
        vectors = vectors[:, 0].astype(full)
        bounds = [0]
        for size in sizes + [gain_cols, gain_cols]:
            bounds.append(bounds[-1] + size)
        pieces = [vectors[:, bounds[k] : bounds[k + 1]] for k in range(6)]
        qkv_vector, proj_vector, up_vector, down_vector, gain_q, gain_k = [
            p.reshape(-1) for p in pieces
        ]

        def own_columns(flat, groups):
            parts = flat.reshape(groups, PLANE, -1)
            return lax.dynamic_slice_in_dim(parts, chip, 1, axis=1).reshape(-1)

        assert spans == slots
        many = (meta_all[:, 0, row_count - 1] != 0)[:, None, None]
        group_spans = jnp.where(many, group_mod, group_mod[:, :1])
        own_many = segment_ids[row_count - 1] != 0
        own_spans = jnp.where(own_many, modulation, modulation[:1])

        def spread(values):
            count = values.shape[0]
            return jnp.broadcast_to(values[:, None, :], (count, SPAN, width)).reshape(
                count * SPAN, width
            )

        def per_row(k):
            return spread(own_spans[:, k * width : (k + 1) * width])

        def per_row_all(k):
            return spread(
                group_spans[:, :, k * width : (k + 1) * width].reshape(PLANE * spans, width)
            )

        def core_swap(source, out, count):
            return [
                (
                    CORE_HOP,
                    source,
                    lambda me, peer, k=k: (k, peer.core),
                    out,
                    lambda me, peer, k=k: (k,),
                    None,
                )
                for k in range(count)
            ]

        def half_of(parts):
            return ((parts.shape[0],) + parts.shape[2:], low)

        def sum_cores(parts, other):
            mine = lax.dynamic_index_in_dim(parts, core, 1, keepdims=False)
            return (mine.astype(full) + other.astype(full)).astype(low)

        def own_of(values, index):
            return lax.dynamic_index_in_dim(values, index, 0, keepdims=False)

        def z_sum_of(blocks, sent):
            return block_sum(blocks, own_of(sent, z_index))

        def plane_gather(identity, values, *more):
            (out,) = exchange(
                identity,
                [values],
                [((PLANE,) + values.shape, low)],
                gather_moves(PLANE_HOPS, 0, 0, by_chip),
            )
            return put(out, values, chip).reshape(rows_all, width)

        scatter_plan = slotted(PLANE_HOPS, 0, to_chip, 0)
        others = (PLANE - 1, row_count, width)

        def plane_scatter(values):
            return values.astype(low).reshape(PLANE, row_count, width)

        def block_sum(blocks, own):
            return own.astype(full) + jnp.sum(blocks.astype(full), axis=0)

        def plane_sum_of(blocks, sent):
            return block_sum(blocks, lax.dynamic_index_in_dim(sent, chip, 0, keepdims=False))

        def group_span(k):
            return in_steps(group_spans[:, :, None, k * width : (k + 1) * width])

        gain_pad = jnp.zeros((2, LANES), full)
        gains = lax.dynamic_update_slice(gain_pad, jnp.stack([gain_q, gain_k]), (0, 0))
        steps = PLANE_HOPS[2:] + PLANE_HOPS[:2]
        others = (PLANE - 1, row_count, width)

        def in_step(source, out):
            return [
                (hop, source, lambda me, peer, k=k: (k,), out, lambda me, peer, k=k: (k,), None)
                for k, hop in enumerate(steps)
            ]

        plan = [(hop, 0, to_chip, 0, by_chip, None) for hop in PLANE_HOPS + [SELF]]
        plan += gather_moves(Z_HOPS + [SELF], 1, 1, by_z)
        plan += in_step(2, 2)
        (
            hidden_one,
            qkv_rows,
            attended_low,
            attn_terms,
            proj_slice,
            up_same,
            down_z,
            branch_blocks,
        ) = block_call(
            functools.partial(attention_forward_kernel, head_size, heads),
            [
                patches,
                patch_blocks.reshape(others),
                group_span(0),
                group_span(1),
                qkv_slice,
                own_columns(qkv_vector, 3)[None],
                gains,
                cos_rows,
                sin_rows,
                meta_rows,
                seg_col,
                proj_z,
                proj_other,
            ],
            [0, 2, 1, 1, 0, 0, 0, 0, 0, 1, 1, 0, 0],
            [
                ((PLANE, row_count, width), low),
                ((PLANE, row_count, 3 * part_cols), full),
                ((PLANE, row_count, part_cols), low),
            ],
            [((row_count, width), low), ((part_cols, width), low)],
            [(others, low)],
            PLANE,
            rows_all * width * 8 * part_cols,
            11,
            [up_pieces, down_weight],
            [
                (up_pieces.shape, low),
                ((z_size,) + down_weight.shape, low),
                (others, low),
            ],
            plan,
        )
        branch_attn = block_sum(branch_blocks, attn_terms) + proj_vector

        patch_full = patches.astype(full)
        scale_one = rms_scale(patch_full)
        normed_one = patch_full * scale_one
        middle = patch_full + per_row(2) * branch_attn
        scale_two = rms_scale(middle)
        normed_two = middle * scale_two
        hidden_two = (normed_two * (1.0 + per_row(4)) + per_row(3)).astype(low)

        hidden_blocks, down_other, up_other = exchange(
            5,
            [halves(hidden_two), down_z, up_same],
            [((PLANE - 1, 2, row_count // 2, width), low), (down_z.shape, low), (up_same.shape, low)],
            [(CORE_HOP, k, None, k, None, None) for k in (1, 2)] + relayed(0, 0, hop_place, 2),
        )
        gate_spans = in_steps(group_spans[:, :, 5 * width :])
        own_terms, up_bias_cols, ffn_terms, up_parts, down_parts, hidden_two_blocks = block_call(
            ffn_kernel,
            [
                hidden_two,
                hidden_blocks.reshape(others),
                out_cotangent,
                cot_blocks.reshape(others),
                gate_spans[:, :, None],
                up_same,
                up_other,
                down_z,
                down_other,
                own_columns(up_vector, 2)[None],
            ],
            [0, 2, 0, 2, 1, 0, 0, 0, 0, 0],
            [],
            [
                ((row_count, width), low),
                ((1, 2 * units), full),
                ((PLANE, row_count, width), low),
                ((width, 2 * units), low),
                ((z_size, 2) + down_weight.shape, low),
            ],
            [
                ((units, width), low),
                ((width, 2 * units), low),
                (others, low),
                ((rows_all, width), low),
                ((rows_all, width), low),
                ((rows_all, units), low),
                ((rows_all, 2 * units), low),
            ],
            PLANE + 1,
            rows_all * width * 18 * units,
            6,
            [],
            [(others, low)],
            in_step(0, 0),
        )
        up_parts = up_parts.reshape(PLANE, 2, shard, 2 * units)
        grad_hidden_two = block_sum(hidden_two_blocks, own_terms)

        grad_out = out_cotangent.astype(full)
        own_gbf = (grad_out * per_row(5)).astype(low).astype(full)
        down_bias_grad = jnp.sum(own_gbf, axis=0)
        grad_middle = grad_out + norm_backward(
            grad_hidden_two * (1.0 + per_row(4)), normed_two, scale_two
        )
        grad_branch_attn = (grad_middle * per_row(2)).astype(low)
        proj_bias_grad = jnp.sum(grad_branch_attn.astype(full), axis=0)
        grad_branch_blocks, down_swapped, up_swapped = exchange(
            7,
            [halves(grad_branch_attn), down_parts, up_parts],
            [
                ((PLANE - 1, 2, row_count // 2, width), low),
                half_of(down_parts),
                half_of(up_parts),
            ],
            relayed(0, 0, hop_place, 0)
            + core_swap(1, 1, z_size)
            + core_swap(2, 2, PLANE),
        )
        down_mine = sum_cores(down_parts, down_swapped)
        up_mine = sum_cores(up_parts, up_swapped)
        plan = in_step(0, 0)
        plan += [(hop, 1, to_chip, 1, by_chip, None) for hop in PLANE_HOPS + [SELF]]
        plan += slotted(Z_HOPS, 2, to_z, 2)
        (
            hidden_one_terms,
            qkv_bias_cols,
            gain_grads,
            qkv_parts,
            proj_parts,
            ffn_blocks,
            up_moved,
            down_blocks,
        ) = block_call(
            functools.partial(attention_backward_kernel, head_size, heads),
            [
                grad_branch_attn,
                grad_branch_blocks.reshape(others),
                qkv_rows,
                qkv_slice,
                gains,
                cos_rows,
                sin_rows,
                meta_rows,
                seg_col,
                proj_slice,
                hidden_one,
                attended_low,
            ],
            [0, 2, 1, 0, 0, 0, 0, 1, 1, 0, 1, 1],
            [((PLANE, row_count, width), low)],
            [
                ((1, 3 * part_cols), full),
                ((2, LANES), full),
                ((PLANE, 2, shard, 3 * part_cols), low),
                ((z_size, 2) + proj_weight.shape, low),
            ],
            [((width, 3 * part_cols), full), ((part_cols, width), full)],
            PLANE,
            rows_all * width * 18 * part_cols,
            12,
            [ffn_terms, up_mine, down_mine],
            [
                (others, low),
                (up_mine.shape, low),
                ((z_size - 1,) + down_mine.shape[1:], low),
            ],
            plan,
        )
        gain_q_grad, gain_k_grad = gain_grads[0, :head_size], gain_grads[1, :head_size]
        up_wide = whole_call(functools.partial(merge_kernel, 2), up_moved)
        to_z_part = lambda me, peer: (peer.z, pl.ds(0, up_cut))
        to_z_rest = lambda me, peer: (peer.z, pl.ds(up_cut, shard - up_cut))
        hidden_one_blocks, qkv_other, proj_other, up_blocks = exchange(
            8,
            [hidden_one_terms, qkv_parts, proj_parts, up_wide],
            [
                (others, low),
                half_of(qkv_parts),
                half_of(proj_parts),
                ((z_size - 1, up_cut, up_cols), low),
            ],
            in_step(0, 0)
            + core_swap(1, 1, PLANE)
            + core_swap(2, 2, z_size)
            + slotted(Z_HOPS, 3, to_z_part, 3),
        )
        down_grad = z_sum_of(down_blocks, down_mine)
        qkv_mine = sum_cores(qkv_parts, qkv_other)
        proj_mine = sum_cores(proj_parts, proj_other)
        patch_grad, block_out, grad_spans = tail_call(
            [patches, out_cotangent, middle, branch_attn, grad_middle, grad_hidden_two],
            [hidden_one_blocks, hidden_one_terms, ffn_blocks, ffn_terms],
            own_spans.reshape(spans, -1, width),
            down_vector[None],
        )
        grad_spans = grad_spans.reshape(spans, -1)

        one_image = jnp.concatenate(
            [jnp.sum(grad_spans, axis=0, keepdims=True), jnp.zeros_like(grad_spans[1:])], axis=0
        )
        grad_modulation = jnp.where(own_many, grad_spans, one_image).astype(low)
        grad_mod = grad_modulation.reshape(slots, z_size, mod_cols).transpose(1, 0, 2)

        def place(flat, groups):
            spot = (jnp.arange(PLANE) == chip).astype(full)
            return (flat.reshape(groups, 1, -1) * spot[None, :, None]).reshape(-1)

        rows = [
            place(qkv_bias_cols, 3),
            proj_bias_grad,
            place(up_bias_cols, 2),
            down_bias_grad,
            gain_q_grad,
            gain_k_grad,
        ]
        vector_grad = jnp.concatenate([r.reshape(z_size, 1, -1) for r in rows], axis=2)
        plan = [
            (hop, 1, to_z, 1, lambda me, peer: (me.dp, me.z), None) for hop in Z_HOPS + [SELF]
        ]
        plan += [(hop, 2, to_z, 2, by_z, None) for hop in Z_HOPS + [SELF]]
        plan += [(hop, 0, to_chip, 0, by_chip, None) for hop in PLANE_HOPS + [SELF]]
        plan += [(hop, 1, by_dp, 1, by_dp, (0, 1, 2, 3)) for hop in DP_HOPS if hop != SELF]
        plan += slotted(Z_HOPS, 3, to_z, 3) + slotted(Z_HOPS, 4, to_z_rest, 4)
        qkv_moved, grad_mod, vector_parts, proj_blocks, up_rest_blocks = exchange(
            9,
            [qkv_mine, grad_mod, vector_grad, proj_mine, up_wide],
            [
                (qkv_mine.shape, low),
                ((2 * PLANE, z_size, slots, mod_cols), low),
                (vector_grad.shape, full),
                ((z_size - 1,) + proj_mine.shape[1:], low),
                ((z_size - 1, shard - up_cut, up_cols), low),
            ],
            plan,
        )
        proj_grad = z_sum_of(proj_blocks, proj_mine)
        up_own = own_of(up_wide, z_index)
        up_grad = jnp.concatenate(
            [
                block_sum(up_blocks, up_own[:up_cut]),
                block_sum(up_rest_blocks, up_own[up_cut:]),
            ],
            axis=0,
        )
        qkv_wide = whole_call(functools.partial(merge_kernel, 3), qkv_moved)
        grad_mod = grad_mod.reshape(-1, mod_cols)
        vector_sum = jnp.sum(vector_parts, axis=0)
        cond_part = dot_t(grad_mod, mod_weight).reshape(2 * PLANE, z_size, slots, mod_rows)
        plan = slotted(Z_HOPS, 0, to_z, 0)
        plan += [
            (
                hop,
                1,
                lambda me, peer: (peer.dp, peer.z),
                1,
                lambda me, peer: (me.dp, me.z),
                None,
            )
            for hop in ALL_HOPS
        ]
        plan += gather_moves(DP_HOPS, 2, 2, by_dp)
        qkv_blocks, cond_parts, vector_parts = exchange(
            10,
            [qkv_wide, cond_part, vector_sum],
            [
                ((z_size - 1,) + qkv_wide.shape[1:], low),
                (cond_part.shape, full),
                ((2 * PLANE,) + vector_sum.shape, full),
            ],
            plan,
        )
        qkv_grad = z_sum_of(qkv_blocks, qkv_wide)
        mod_bias_grad = jnp.sum(grad_mod.astype(full), axis=0)
        mod_grad = outer_grad(silu_cols, grad_mod)
        cond_part = jnp.sum(cond_parts, axis=1)
        cond_grad = (
            cond_part.transpose(1, 0, 2).reshape(slots, width) * silu_slope(cond_full)
        ).astype(low)
        vector_grad = jnp.sum(vector_parts, axis=0)[0]
        out = [vector_grad[bounds[k] : bounds[k + 1]] for k in range(6)]
        return (
            block_out,
            patch_grad,
            cond_grad,
            mod_grad,
            mod_bias_grad,
            qkv_grad,
            out[0],
            jnp.stack([out[4], out[5]]),
            proj_grad,
            out[1],
            up_grad,
            out[2],
            down_grad,
            out[3],
        )

    return per_device


def solution(mesh):
    if mesh.shape["dp"] == 2 * PLANE and mesh.shape["fsdp"] == 4:
        body = make_plane(mesh.shape["fsdp"])
    else:
        body = make_plain(mesh.shape["dp"], mesh.shape["fsdp"])
    rows = P(("dp", "fsdp"), None)
    matrix = P("dp", "fsdp")
    vector = P("fsdp")
    gains = P(None, "fsdp")
    return jax.shard_map(
        body,
        mesh=mesh,
        in_specs=(
            rows,
            rows,
            P(("dp", "fsdp")),
            P(None, ("dp", "fsdp")),
            matrix,
            vector,
            matrix,
            vector,
            gains,
            matrix,
            vector,
            matrix,
            vector,
            matrix,
            vector,
            rows,
        ),
        out_specs=(
            rows,
            rows,
            rows,
            matrix,
            vector,
            matrix,
            vector,
            gains,
            matrix,
            vector,
            matrix,
            vector,
            matrix,
            vector,
        ),
        check_vma=False,
    )
```
